512 devices in a mesh: dom: 64 (over z, y), tp: 8 (over x, core).
Axes of the slice: x: 4, y: 4, z: 16, core: 2. Of those that a mesh axis runs over, the one named last changes fastest.
Arguments:
- queries: bfloat16 [2, 1024, 8192], P(None, 'dom', 'tp'), may hold values from -400 to 400
- new_kv: bfloat16 [2, 1024, 2048], P(None, 'dom', 'tp'), may hold values from -5 to 5
- gen_cache: bfloat16 [1024, 128, 2048], P('dom', None, 'tp'), may hold values from -5 to 5
- prompt_kv: bfloat16 [4096, 2048], P(None, 'tp'), may hold values from -5 to 5
- lengths: int32 [1024], replicated, may hold values from 1 to 126
- ancestors: int32 [1024], replicated, may hold values from 0 to 1023, as said below
- tokens: int32 [2, 1024], P(None, 'dom'), may hold values from 0 to 128255
- twist_vector: float32 [8192], P('tp'), may hold values from -31 to 31
- twist_bias: float32 [128256], replicated, may hold values from -5 to 5
- prior_weights: float32 [1024], P('dom'), may hold values from -252 to 4
Outputs:
- twist: float32 [2, 1024], P(None, 'dom')
- normalized: float32 [1024], P('dom')
- resampled_cache: bfloat16 [1024, 128, 2048], P('dom', None, 'tp')
- new_lengths: int32 [1024], P('dom')
The draws below stay inside these ranges and needn't reach their ends.
Inputs may be any that keep to these rules, and one draw needn't show every extreme that they name: Particle p's ancestor lies on the index of dom that holds p or at most 2 indices from it; the particles of one index of dom name at most 2 distinct ancestors on any other index, and exactly 2 for some pair of indices.
All inputs are finite; a program needn't handle non-finite values.
Results may differ from the reference program's by a relative error of at most 0.0018.
Values may be sent and summed in bfloat16 or wider, within the bound.
A program may use at most 64 MiB of HBM per device.

```python
import math
import jax
import jax.numpy as jnp
import numpy as np
from jax import lax

HEADS = 64
KV_HEADS = 8
HEAD_DIM = 128
VOCAB = 128256
PROMPT = 4096
GEN = 128
PART_DEV = 16
SPAN = 2
PARTICLES = 1024


def drawn_pair(key):
    base_key = jax.random.fold_in(key, 7)
    key_query, key_prompt = jax.random.split(base_key)
    prompt = jnp.clip(jax.random.normal(key_prompt, (PROMPT, KV_HEADS, 2, HEAD_DIM), jnp.float32), -5.0, 5.0)
    query_draw = jnp.clip(jax.random.normal(key_query, (2, PARTICLES, HEADS, HEAD_DIM), jnp.float32), -5.0, 5.0)
    return (query_draw.reshape(2, PARTICLES, HEADS * HEAD_DIM), prompt.reshape(PROMPT, KV_HEADS * 2 * HEAD_DIM))


def draw_queries(key, part):
    return drawn_pair(key)[0].astype(jnp.bfloat16)


def draw_prompt_kv(key, part):
    return drawn_pair(key)[1].astype(jnp.bfloat16)


def draw_ancestors(key, part):
    base_key = jax.random.fold_in(key, 11)
    key_offset, key_stay, key_heavy, key_pick, key_local = jax.random.split(base_key, 5)
    dom_count = PARTICLES // PART_DEV
    positions = jnp.arange(PARTICLES, dtype=jnp.int32)
    home_dev = positions // PART_DEV
    offsets = jax.random.randint(key_offset, (PARTICLES,), -SPAN, SPAN + 1)
    stay_home = jax.random.randint(key_stay, (PARTICLES,), 0, 3) == 0
    offsets = jnp.where(stay_home, 0, offsets)
    last_first = (dom_count - 1) * PART_DEV
    offsets = offsets.at[0].set(SPAN).at[1].set(SPAN).at[last_first].set(-SPAN).at[last_first + 1].set(-SPAN)
    source_dev = jnp.clip(home_dev + offsets, 0, dom_count - 1)
    heavy_scores = jax.random.randint(key_heavy, (dom_count, PART_DEV), 0, 1 << 20) * PART_DEV + jnp.arange(PART_DEV, dtype=jnp.int32)[None, :]
    heavy_slots = jnp.argsort(heavy_scores, axis=1)[:, :2].astype(jnp.int32)
    heavy_pick = jax.random.randint(key_pick, (PARTICLES,), 0, 2)
    heavy_pick = heavy_pick.at[0].set(0).at[1].set(1).at[last_first].set(0).at[last_first + 1].set(1)
    local_draw = jax.random.randint(key_local, (PARTICLES,), 0, PART_DEV)
    remote_local = heavy_slots[source_dev, heavy_pick]
    local_index = jnp.where(source_dev == home_dev, local_draw, remote_local)
    return (source_dev * PART_DEV + local_index).astype(jnp.int32)


def draw_twist_vector(key, part):
    head_ids = (jnp.arange(HEADS * HEAD_DIM) // HEAD_DIM).astype(jnp.float32)
    base_draw = jnp.clip(jax.random.normal(jax.random.fold_in(key, 17), (HEADS * HEAD_DIM,), jnp.float32), -4.0, 4.0)
    head_ramp = 1.0 + 2.0 * head_ids / (HEADS - 1)
    return base_draw * head_ramp


def draw_prior_weights(key, part):
    positions = jnp.arange(PARTICLES).astype(jnp.float32)
    noise = jax.random.uniform(jax.random.fold_in(key, 23), (PARTICLES,), jnp.float32, -1.0, 1.0)
    return jnp.log(1.0 + 2.0 * positions / (PARTICLES - 1)) + noise


def set_ends(array, key, least, top_value):
    extent = array.shape
    place = [jax.random.randint(jax.random.fold_in(key, axis), (), 0, extent[axis]) for axis in range(len(extent))]
    array = array.at[tuple(place)].set(least)
    longest = extent.index(max(extent))
    place[longest] = (place[longest] + 1) % extent[longest]
    return array.at[tuple(place)].set(top_value)


def levels(rng, extent, cuts, low, high):
    loudness, own = 1.0, jax.random.fold_in(rng, 6)
    for position, blocks in cuts:
        steps = jnp.exp(jax.random.uniform(jax.random.fold_in(own, position), (blocks,), jnp.float32, low / len(cuts), high / len(cuts)))
        loudness = loudness * jnp.repeat(steps, extent[position] // blocks).reshape([-1 if axis == position else 1 for axis in range(len(extent))])
    return loudness


def wide_ids(own_key, extent, amount, skew):
    loads = [min(1 << octave, amount + 1 - (1 << octave)) * (1 << 20) // math.isqrt((1 << octave) ** skew) + 1 for octave in range((amount + 1).bit_length()) if 1 << octave <= amount]
    deviation = 1 + sum(loads) // (1 << 30)
    grid = np.cumsum(np.array([max(1, weight // deviation) for weight in loads]))
    pick = jax.random.randint(jax.random.fold_in(own_key, 1), extent, 0, int(grid[len(loads) - 1]))
    start = jnp.left_shift(1, jnp.searchsorted(jnp.asarray(grid, jnp.int32), pick, side="right").astype(jnp.int32))
    standing = start - 1 + jax.random.randint(jax.random.fold_in(own_key, 4), extent, 0, 1 << 30) % jnp.minimum(start, amount + 1 - start)
    return jax.random.permutation(jax.random.fold_in(own_key, 2), amount)[standing].astype(jnp.int32)


def scatter_about(key, extent, deviation, limit, cuts=(), held_as=jnp.bfloat16):
    drawn = deviation * jax.random.normal(key, extent, jnp.float32)
    if cuts:
        drawn = drawn * levels(key, extent, cuts, -0.22, 0.18)
    return jnp.clip(drawn, -limit, limit).astype(held_as)


def setup_inputs(seed: int = 0) -> dict:
    key_list = jax.random.split(jax.random.key(seed), 11)
    return {
        "queries": draw_queries(jax.random.fold_in(key_list[10], 71), 0),
        "new_kv": scatter_about(key_list[1], (2, PARTICLES, KV_HEADS * 2 * HEAD_DIM), 1.0, 5.0, ((1, 64), (2, 8))),
        "gen_cache": scatter_about(key_list[2], (PARTICLES, GEN, KV_HEADS * 2 * HEAD_DIM), 1.0, 5.0, ((0, 64), (2, 8))),
        "prompt_kv": draw_prompt_kv(jax.random.fold_in(key_list[10], 71), 0),
        "lengths": set_ends(jax.random.randint(key_list[4], (PARTICLES,), 1, GEN - 1), jax.random.fold_in(key_list[4], 1), 1, (GEN - 1) - 1).astype(jnp.int32),
        "ancestors": draw_ancestors(jax.random.fold_in(key_list[10], 71), 0),
        "tokens": set_ends(wide_ids(key_list[6], (2, PARTICLES), VOCAB, 2), jax.random.fold_in(key_list[6], 3), 0, VOCAB - 1).astype(jnp.int32),
        "twist_vector": draw_twist_vector(jax.random.fold_in(key_list[10], 71), 0),
        "twist_bias": scatter_about(key_list[8], (VOCAB,), 1.0, 5.0, (), jnp.float32),
        "prior_weights": draw_prior_weights(jax.random.fold_in(key_list[10], 71), 0),
    }


NEG_FILL = -1e+30

def grow_cache(gen_cache, new_kv, own_lengths):
    slot_ids = lax.broadcasted_iota(jnp.int32, (1, gen_cache.shape[1], 1), 1)
    start_row = own_lengths[:, None, None]
    first_row = new_kv[0][:, None, :]
    second = new_kv[1][:, None, :]
    empty_rows = jnp.zeros_like(gen_cache)
    later_rows = jnp.where(slot_ids == start_row + 1, second, empty_rows)
    return jnp.where(slot_ids < start_row, gen_cache, jnp.where(slot_ids == start_row, first_row, later_rows))

def attend_block(block_queries, prompt_kv, grown, own_lengths):
    step_count, per_block, width = block_queries.shape
    kv_count = prompt_kv.shape[1] // (2 * HEAD_DIM)
    group_size = width // (kv_count * HEAD_DIM)
    query_heads = block_queries.reshape(step_count, per_block, kv_count, group_size, HEAD_DIM).astype(jnp.float32)
    prompt = prompt_kv.reshape(prompt_kv.shape[0], kv_count, 2, HEAD_DIM).astype(jnp.float32)
    cached = grown.reshape(per_block, grown.shape[1], kv_count, 2, HEAD_DIM).astype(jnp.float32)
    score_scale = 1.0 / math.sqrt(HEAD_DIM)
    prompt_scores = jnp.einsum('tpcgd,scd->tpcgs', query_heads, prompt[:, :, 0]) * score_scale
    cache_scores = jnp.einsum('tpcgd,pscd->tpcgs', query_heads, cached[:, :, :, 0]) * score_scale
    slot_ids = lax.broadcasted_iota(jnp.int32, (step_count, 1, 1, 1, grown.shape[1]), 4)
    step_ids = lax.broadcasted_iota(jnp.int32, (step_count, 1, 1, 1, 1), 0)
    visible = slot_ids <= own_lengths[None, :, None, None, None] + step_ids
    cache_scores = jnp.where(visible, cache_scores, NEG_FILL)
    row_max = jnp.maximum(lax.optimization_barrier(jnp.max(prompt_scores, axis=-1, keepdims=True)), lax.optimization_barrier(jnp.max(cache_scores, axis=-1, keepdims=True)))
    prompt_exp = jnp.exp(prompt_scores - row_max)
    cache_exp = jnp.where(visible, jnp.exp(cache_scores - row_max), 0.0)
    row_sum = lax.optimization_barrier(jnp.sum(prompt_exp, axis=-1)) + lax.optimization_barrier(jnp.sum(cache_exp, axis=-1))
    prompt_probs = prompt_exp.astype(jnp.bfloat16).astype(jnp.float32)
    cache_probs = cache_exp.astype(jnp.bfloat16).astype(jnp.float32)
    mixed = jnp.einsum('tpcgs,scd->tpcgd', prompt_probs, prompt[:, :, 1]) + jnp.einsum('tpcgs,pscd->tpcgd', cache_probs, cached[:, :, :, 1])
    return mixed / row_sum[..., None]

def reference(queries, new_kv, gen_cache, prompt_kv, lengths, ancestors, tokens, twist_vector, twist_bias, prior_weights):
    grown = grow_cache(gen_cache, new_kv, lengths)
    block_count = PARTICLES // 8
    query_blocks = jnp.transpose(queries.reshape(2, block_count, 8, queries.shape[2]), (1, 0, 2, 3))
    grown_blocks = grown.reshape(block_count, 8, GEN, grown.shape[2])
    length_blocks = lengths.reshape(block_count, 8)

    def block_twist(block_item):
        block_queries, block_grown, block_lengths = block_item
        mixed = attend_block(block_queries, prompt_kv, block_grown, block_lengths)
        head_weights = twist_vector.reshape(mixed.shape[2:])
        return lax.optimization_barrier(jnp.sum(mixed * head_weights, axis=(2, 3, 4)))
    partial_twist = lax.map(block_twist, (query_blocks, grown_blocks, length_blocks))
    twist = jnp.transpose(partial_twist, (1, 0, 2)).reshape(2, PARTICLES) + twist_bias[tokens]
    log_weight = prior_weights + twist[1] - twist[0]
    largest = jnp.max(log_weight)
    normalized = log_weight - (largest + jnp.log(jnp.sum(jnp.exp(log_weight - largest))))
    resampled_cache = grown[ancestors]
    new_lengths = lengths[ancestors] + 2
    return (twist, normalized, resampled_cache, new_lengths)
```

```python
import functools
import math

import jax
import jax.numpy as jnp
from jax import lax
from jax.experimental import pallas as pl
from jax.experimental.pallas import tpu as pltpu
from jax.sharding import PartitionSpec as P

HEAD_DIM = 128
Y_DIM = 4
NEG_FILL = -1e30
MESH = pl.DeviceIdType.MESH
LOG2E = 1.4426950408889634
OFFSETS = (2, 1, -2, -1)


def kernel(
    sizes,
    anc,
    lens,
    toks,
    prior,
    q_hbm,
    new_hbm,
    gen_hbm,
    prompt_hbm,
    tv_ref,
    bias_hbm,
    twist_out,
    norm_out,
    cache_out,
    len_out,
    qv,
    newv,
    cache,
    keyv,
    valv,
    biasv,
    scores,
    picked,
    relay,
    landed,
    outv,
    bias_rows,
    plane_rows,
    z_rows,
    in_sems,
    out_sem,
    hop_send,
    hop_recv,
    plane_send,
    plane_recv,
    z_send,
    z_recv,
):
    n_dom, n_tp, per_dev, gen, prompt_len, group = sizes
    n_z = n_dom // Y_DIM
    n_plane = n_tp * Y_DIM
    dom = lax.axis_index("dom")
    tp = lax.axis_index("tp")
    my_y = lax.rem(dom, Y_DIM)
    my_z = dom // Y_DIM
    base = dom * per_dev

    def device(d, t):
        return {"dom": d, "tp": t}

    after = lax.rem(dom + 1, n_dom)
    before = lax.rem(dom + n_dom - 1, n_dom)

    def plane_peer(k):
        slot = lax.rem(tp * Y_DIM + my_y + k, n_plane)
        return slot, device(my_z * Y_DIM + lax.rem(slot, Y_DIM), slot // Y_DIM)

    def z_peer(k):
        slot = lax.rem(my_z + k, n_z)
        return slot, device(slot * Y_DIM + my_y, tp)

    def load(src, dst, i):
        return pltpu.make_async_copy(src, dst, in_sems.at[i])

    loads = [
        load(gen_hbm, cache, 0),
        load(new_hbm, newv, 1),
        load(q_hbm, qv, 2),
        load(prompt_hbm.at[:, 0:HEAD_DIM], keyv, 3),
        load(prompt_hbm.at[:, HEAD_DIM : 2 * HEAD_DIM], valv, 4),
        load(bias_hbm, biasv, 5),
    ]
    for item in loads:
        item.start()

    barrier = pltpu.get_barrier_semaphore()
    for d in (after, before):
        pl.semaphore_signal(barrier, inc=1, device_id=device(d, tp), device_id_type=MESH)

    def greet_plane(k, carry):
        pl.semaphore_signal(barrier, inc=1, device_id=plane_peer(k)[1], device_id_type=MESH)
        return carry

    def greet_z(k, carry):
        pl.semaphore_signal(barrier, inc=1, device_id=z_peer(k)[1], device_id_type=MESH)
        return carry

    lax.fori_loop(1, n_plane, greet_plane, 0)
    lax.fori_loop(1, n_z, greet_z, 0)

    for p in range(per_dev):
        len_out[p] = lens[anc[base + p]] + 2

    loads[0].wait()
    loads[1].wait()
    rows = lax.broadcasted_iota(jnp.int32, (gen, 2 * HEAD_DIM), 0)

    def grow(p, carry):
        start = lens[base + p]
        first = newv[0, pl.ds(p, 1), :].astype(jnp.float32)
        second = newv[1, pl.ds(p, 1), :].astype(jnp.float32)
        kept = cache[p].astype(jnp.float32)
        later = jnp.where(rows == start + 1, second, 0.0)
        grown = jnp.where(rows < start, kept, jnp.where(rows == start, first, later))
        cache[p] = grown.astype(jnp.bfloat16)
        return carry

    for p in range(per_dev):
        grow(p, 0)

    for slot, offset in enumerate(OFFSETS):
        target = lax.rem(dom + offset + n_dom, n_dom) * per_dev
        low, high = per_dev - 1, 0
        for i in range(per_dev):
            spot = anc[target + i] - base
            mine = jnp.logical_and(spot >= 0, spot < per_dev)
            low = jnp.minimum(low, jnp.where(mine, spot, per_dev - 1))
            high = jnp.maximum(high, jnp.where(mine, spot, 0))
        picked[slot, 0] = cache[low]
        picked[slot, 1] = cache[high]

    pl.semaphore_wait(barrier, 2 + n_plane - 1 + n_z - 1)

    def hop(src, dst, i, d):
        return pltpu.make_async_remote_copy(
            src_ref=src,
            dst_ref=dst,
            send_sem=hop_send.at[i],
            recv_sem=hop_recv.at[i],
            device_id=device(d, tp),
            device_id_type=MESH,
        )

    hops = [
        hop(picked.at[0], relay.at[0], 0, after),
        hop(picked.at[2], relay.at[1], 1, before),
        hop(picked.at[1], landed.at[1], 2, after),
        hop(picked.at[3], landed.at[3], 3, before),
        hop(relay.at[0], landed.at[0], 4, after),
        hop(relay.at[1], landed.at[2], 5, before),
    ]
    for item in hops[:4]:
        item.start()

    n_rows = 2 * group * per_dev
    loads[2].wait()
    tiles = [qv[t, :, h * HEAD_DIM : (h + 1) * HEAD_DIM] for t in range(2) for h in range(group)]
    stacked = jnp.concatenate(tiles, axis=0)
    to_row = lax.broadcasted_iota(jnp.int32, (n_rows, n_rows), 0)
    from_row = lax.broadcasted_iota(jnp.int32, (n_rows, n_rows), 1)
    wanted = lax.rem(to_row, 2 * group) * per_dev + to_row // (2 * group)
    order = jnp.where(from_row == wanted, 1.0, 0.0).astype(jnp.bfloat16)
    query = jnp.dot(order, stacked, preferred_element_type=jnp.float32).astype(jnp.bfloat16)

    nt = (((1,), (1,)), ((), ()))
    part = 2 * group
    own = []
    cols = lax.broadcasted_iota(jnp.int32, (part, gen), 1)
    step = lax.broadcasted_iota(jnp.int32, (part, gen), 0) // group
    for p in range(per_dev):
        raw = lax.dot_general(
            query[p * part : (p + 1) * part], cache[p, :, 0:HEAD_DIM], nt,
            preferred_element_type=jnp.float32,
        )
        own.append(jnp.where(cols <= lens[base + p] + step, raw, NEG_FILL))
    own = jnp.concatenate(own, axis=0)
    top = own
    loads[3].wait()
    chunk = 512
    for c in range(prompt_len // chunk):
        raw = lax.dot_general(
            query, keyv[c * chunk : (c + 1) * chunk, :], nt, preferred_element_type=jnp.float32
        )
        scores[:, c * chunk : (c + 1) * chunk] = raw
        for i in range(chunk // 128):
            top = jnp.maximum(top, raw[:, i * 128 : (i + 1) * 128])
    row_max = jnp.max(top, axis=1, keepdims=True)
    scale = LOG2E / math.sqrt(HEAD_DIM)
    exps = jnp.exp2((own - row_max) * scale)
    total = exps
    probs = exps.astype(jnp.bfloat16)
    mixed = []
    for p in range(per_dev):
        mixed.append(
            jnp.dot(
                probs[p * part : (p + 1) * part], cache[p, :, HEAD_DIM : 2 * HEAD_DIM],
                preferred_element_type=jnp.float32,
            )
        )
    mixed = jnp.concatenate(mixed, axis=0)
    loads[4].wait()
    for c in range(prompt_len // chunk):
        exps = jnp.exp2((scores[:, c * chunk : (c + 1) * chunk] - row_max) * scale)
        for i in range(chunk // 128):
            total = total + exps[:, i * 128 : (i + 1) * 128]
        mixed = mixed + jnp.dot(
            exps.astype(jnp.bfloat16), valv[c * chunk : (c + 1) * chunk, :],
            preferred_element_type=jnp.float32,
        )
    row_sum = jnp.sum(total, axis=1, keepdims=True)
    mixed = mixed / row_sum
    weighted = mixed.reshape(2 * per_dev, group, HEAD_DIM) * tv_ref[...][None]
    pair_rows = jnp.sum(weighted, axis=1)

    loads[5].wait()
    lanes = lax.broadcasted_iota(jnp.int32, (1, 128), 1)
    for p in range(per_dev):
        for t in range(2):
            token = toks[t, p]
            row = biasv[pl.ds(token // 128, 1), :]
            bias_rows[p * 2 + t : p * 2 + t + 1, :] = jnp.where(lanes == lax.rem(token, 128), row, 0.0)
    first_tp = jnp.where(tp == 0, 1.0, 0.0)
    pair_rows = pair_rows + bias_rows[...] * first_tp
    pair_col = jnp.sum(pair_rows, axis=1, keepdims=True)
    pair_ids = lax.broadcasted_iota(jnp.int32, (2 * per_dev, 128), 0)
    lane_ids = lax.broadcasted_iota(jnp.int32, (2 * per_dev, 128), 1)
    at_lane = lane_ids == lax.rem(pair_ids, 2) * per_dev + pair_ids // 2
    message = jnp.sum(jnp.where(at_lane, pair_col, 0.0), axis=0, keepdims=True)
    for p in range(per_dev):
        message = jnp.where(lanes == 2 * per_dev + p, prior[p] * first_tp, message)

    me = tp * Y_DIM + my_y
    plane_rows[me] = message

    def plane_copy(src, dst, peer):
        return pltpu.make_async_remote_copy(
            src_ref=plane_rows.at[src],
            dst_ref=plane_rows.at[dst],
            send_sem=plane_send.at[peer[0]],
            recv_sem=plane_recv.at[dst],
            device_id=peer[1],
            device_id_type=MESH,
        )

    def plane_start(k, carry):
        plane_copy(me, me, plane_peer(k)).start()
        return carry

    lax.fori_loop(1, n_plane, plane_start, 0)

    hops[0].wait_recv()
    hops[4].start()
    hops[1].wait_recv()
    hops[5].start()

    def plane_wait(k, carry):
        peer = plane_peer(k)
        plane_copy(me, peer[0], peer).wait()
        return carry

    lax.fori_loop(1, n_plane, plane_wait, 0)

    def summed(y):
        acc = plane_rows[y]
        for t in range(1, n_tp):
            acc = acc + plane_rows[t * Y_DIM + y]
        return acc

    def weights(acc):
        later = pltpu.roll(acc, 128 - per_dev, 1)
        given = pltpu.roll(acc, 128 - 2 * per_dev, 1)
        return jnp.where(lanes < per_dev, given + later - acc, NEG_FILL), later

    own_sum = summed(my_y)
    own_weight, own_later = weights(own_sum)
    twist_out[0:1, :] = own_sum[:, 0:per_dev]
    twist_out[1:2, :] = own_later[:, 0:per_dev]
    all_weights = jnp.concatenate([weights(summed(y))[0] for y in range(Y_DIM)], axis=0)
    z_max = jnp.max(jnp.max(all_weights, axis=1, keepdims=True), axis=0, keepdims=True)
    z_exp = jnp.exp(all_weights - z_max)
    z_sum = jnp.sum(jnp.sum(z_exp, axis=1, keepdims=True), axis=0, keepdims=True)
    z_rows[my_z, 0:1, :] = jnp.broadcast_to(z_max, (1, 128))
    z_rows[my_z, 1:2, :] = jnp.broadcast_to(z_sum, (1, 128))

    def z_copy(dst, peer):
        return pltpu.make_async_remote_copy(
            src_ref=z_rows.at[my_z],
            dst_ref=z_rows.at[dst],
            send_sem=z_send.at[peer[0]],
            recv_sem=z_recv.at[dst],
            device_id=peer[1],
            device_id_type=MESH,
        )

    def z_start(k, carry):
        z_copy(my_z, z_peer(k)).start()
        return carry

    lax.fori_loop(1, n_z, z_start, 0)

    for item in hops[2:]:
        item.wait_recv()
    firsts = []
    for offset in OFFSETS:
        low = per_dev - 1
        for i in range(per_dev):
            spot = anc[base + i] - (base - offset * per_dev)
            theirs = jnp.logical_and(spot >= 0, spot < per_dev)
            low = jnp.minimum(low, jnp.where(theirs, spot, per_dev - 1))
        firsts.append(low)
    for p in range(per_dev):
        spot = anc[base + p] - base
        home = jnp.logical_and(spot >= 0, spot < per_dev)
        home_spot = jnp.clip(spot, 0, per_dev - 1)
        place = 0
        for slot, offset in enumerate(OFFSETS):
            there = spot + offset * per_dev
            theirs = jnp.logical_and(there >= 0, there < per_dev)
            second = jnp.where(there == firsts[slot], 0, 1)
            place = jnp.where(theirs, 2 * slot + second, place)
        moved = landed[place // 2, lax.rem(place, 2)]
        outv[p] = jnp.where(home, cache[home_spot], moved)
    written = pltpu.make_async_copy(outv, cache_out, out_sem)
    written.start()

    def z_wait(k, carry):
        peer = z_peer(k)
        z_copy(peer[0], peer).wait()
        return carry

    lax.fori_loop(1, n_z, z_wait, 0)
    maxes = z_rows[:, 0, :]
    sums = z_rows[:, 1, :]
    largest = jnp.max(maxes, axis=0, keepdims=True)
    exp_total = jnp.sum(sums * jnp.exp(maxes - largest), axis=0, keepdims=True)
    normalized = own_weight - (largest + jnp.log(exp_total))
    norm_out[...] = normalized[:, 0:per_dev]

    for item in hops:
        item.wait_send()
    written.wait()


def local(
    n_dom,
    n_tp,
    queries,
    new_kv,
    gen_cache,
    prompt_kv,
    lengths,
    ancestors,
    tokens,
    twist_vector,
    twist_bias,
    prior_weights,
):
    per_dev, gen, width = gen_cache.shape
    prompt_len = prompt_kv.shape[0]
    group = queries.shape[2] // HEAD_DIM
    n_rows = 2 * group * per_dev
    n_z = n_dom // Y_DIM
    n_plane = n_tp * Y_DIM
    any_space = pl.BlockSpec(memory_space=pl.ANY)
    smem = pl.BlockSpec(memory_space=pltpu.SMEM)
    vmem = pl.BlockSpec(memory_space=pltpu.VMEM)
    f32, bf16 = jnp.float32, jnp.bfloat16
    twist, normalized, resampled, new_lengths = pl.pallas_call(
        functools.partial(kernel, (n_dom, n_tp, per_dev, gen, prompt_len, group)),
        out_shape=(
            jax.ShapeDtypeStruct((2, per_dev), f32),
            jax.ShapeDtypeStruct((1, per_dev), f32),
            jax.ShapeDtypeStruct(gen_cache.shape, bf16),
            jax.ShapeDtypeStruct((per_dev,), jnp.int32),
        ),
        in_specs=[smem] * 4 + [any_space] * 4 + [vmem, any_space],
        out_specs=(vmem, vmem, any_space, smem),
        scratch_shapes=[
            pltpu.VMEM(queries.shape, bf16),
            pltpu.VMEM(new_kv.shape, bf16),
            pltpu.VMEM(gen_cache.shape, bf16),
            pltpu.VMEM((prompt_len, HEAD_DIM), bf16),
            pltpu.VMEM((prompt_len, HEAD_DIM), bf16),
            pltpu.VMEM((twist_bias.shape[0] // 128, 128), f32),
            pltpu.VMEM((n_rows, prompt_len), f32),
            pltpu.VMEM((4, 2, gen, width), bf16),
            pltpu.VMEM((2, 2, gen, width), bf16),
            pltpu.VMEM((4, 2, gen, width), bf16),
            pltpu.VMEM(gen_cache.shape, bf16),
            pltpu.VMEM((2 * per_dev, 128), f32),
            pltpu.VMEM((n_plane, 1, 128), f32),
            pltpu.VMEM((n_z, 2, 128), f32),
            pltpu.SemaphoreType.DMA((6,)),
            pltpu.SemaphoreType.DMA,
            pltpu.SemaphoreType.DMA((6,)),
            pltpu.SemaphoreType.DMA((6,)),
            pltpu.SemaphoreType.DMA((n_plane,)),
            pltpu.SemaphoreType.DMA((n_plane,)),
            pltpu.SemaphoreType.DMA((n_z,)),
            pltpu.SemaphoreType.DMA((n_z,)),
        ],
        compiler_params=pltpu.CompilerParams(collective_id=0, has_side_effects=True),
        name="smc_step",
    )(
        ancestors,
        lengths,
        tokens,
        prior_weights,
        queries,
        new_kv,
        gen_cache,
        prompt_kv,
        twist_vector.reshape(group, HEAD_DIM),
        twist_bias.reshape(-1, 128),
    )
    return twist, normalized.reshape(per_dev), resampled, new_lengths


def solution(mesh):
    in_specs = (
        P(None, "dom", "tp"),
        P(None, "dom", "tp"),
        P("dom", None, "tp"),
        P(None, "tp"),
        P(),
        P(),
        P(None, "dom"),
        P("tp"),
        P(),
        P("dom"),
    )
    out_specs = (P(None, "dom"), P("dom"), P("dom", None, "tp"), P("dom"))
    return jax.shard_map(
        functools.partial(local, mesh.shape["dom"], mesh.shape["tp"]),
        mesh=mesh,
        in_specs=in_specs,
        out_specs=out_specs,
        check_vma=False,
    )
```

```python
import functools
import math

import jax
import jax.numpy as jnp
from jax import lax
from jax.experimental import pallas as pl
from jax.experimental.pallas import tpu as pltpu
from jax.sharding import PartitionSpec as P

HEAD_DIM = 128
Y_DIM = 4
NEG_FILL = -1e30
MESH = pl.DeviceIdType.MESH
LOG2E = 1.4426950408889634
PARTS = 4
OFFSETS = (2, 1, -2, -1)


def kernel(
    sizes,
    anc_hbm,
    lens_hbm,
    toks_hbm,
    prior_hbm,
    q_hbm,
    new_hbm,
    gen_hbm,
    prompt_hbm,
    tv_hbm,
    bias_hbm,
    twist_out,
    norm_out,
    cache_out,
    len_out,
    anc,
    lens,
    toks,
    prior,
    qv,
    newv,
    cache,
    keyv,
    valv,
    tvv,
    biasv,
    scores,
    picked,
    relay,
    landed,
    bias_rows,
    plane_rows,
    z_rows,
    small_sems,
    in_sems,
    key_sems,
    val_sems,
    hop_send,
    hop_recv,
    plane_send,
    plane_recv,
    z_send,
    z_recv,
    below_sem,
    above_sem,
):
    n_dom, n_tp, per_dev, gen, prompt_len, group = sizes
    n_z = n_dom // Y_DIM
    n_plane = n_tp * Y_DIM
    dom = lax.axis_index("dom")
    tp = lax.axis_index("tp")
    my_y = lax.rem(dom, Y_DIM)
    my_z = dom // Y_DIM
    base = dom * per_dev
    bias_len = bias_hbm.shape[0]
    bias_part = biasv.shape[0]
    bias_last = bias_len - (n_tp - 1) * bias_part
    key_part = prompt_len // PARTS

    def device(d, t):
        return {"dom": d, "tp": t}

    def signal(sem, target):
        pl.semaphore_signal(sem, inc=1, device_id=target, device_id_type=MESH)

    def z_device(z):
        return device(z * Y_DIM + my_y, tp)

    def plane_peer(k):
        slot = lax.rem(tp * Y_DIM + my_y + k, n_plane)
        return slot, device(my_z * Y_DIM + lax.rem(slot, Y_DIM), slot // Y_DIM)

    copy = pltpu.make_async_copy
    load_q = copy(q_hbm, qv, in_sems.at[0])
    load_gen = copy(gen_hbm, cache, in_sems.at[1])
    load_new = copy(new_hbm, newv, in_sems.at[2])
    load_tv = copy(tv_hbm, tvv, in_sems.at[3])
    load_keys = [
        copy(
            prompt_hbm.at[c * key_part : (c + 1) * key_part, 0:HEAD_DIM],
            keyv.at[c * key_part : (c + 1) * key_part],
            key_sems.at[c],
        )
        for c in range(PARTS)
    ]
    load_vals = [
        copy(
            prompt_hbm.at[c * key_part : (c + 1) * key_part, HEAD_DIM : 2 * HEAD_DIM],
            valv.at[c * key_part : (c + 1) * key_part],
            val_sems.at[c],
        )
        for c in range(PARTS)
    ]
    load_anc = copy(anc_hbm, anc, small_sems.at[0])
    load_lens = copy(lens_hbm, lens, small_sems.at[1])
    load_toks = copy(toks_hbm, toks, small_sems.at[2])
    load_prior = copy(prior_hbm, prior, small_sems.at[3])
    bias_most = copy(
        bias_hbm.at[pl.ds(pl.multiple_of(tp * bias_part, 8), bias_part)], biasv, small_sems.at[4]
    )
    bias_rest = copy(
        bias_hbm.at[bias_len - bias_last : bias_len], biasv.at[0:bias_last], small_sems.at[4]
    )
    load_q.start()
    for item in load_keys:
        item.start()
    load_toks.start()
    load_lens.start()

    @pl.when(tp < n_tp - 1)
    def _():
        bias_most.start()

    @pl.when(tp == n_tp - 1)
    def _():
        bias_rest.start()

    load_gen.start()
    load_new.start()
    for item in load_vals:
        item.start()
    load_tv.start()
    load_prior.start()
    load_anc.start()

    barrier = pltpu.get_barrier_semaphore()

    def greet_plane(k, carry):
        signal(barrier, plane_peer(k)[1])
        return carry

    lax.fori_loop(1, n_plane, greet_plane, 0)

    @pl.when(dom < n_dom - 1)
    def _():
        signal(barrier, device(dom + 1, tp))

    @pl.when(dom > 0)
    def _():
        signal(barrier, device(dom - 1, tp))

    @pl.when(my_z < n_z - 1)
    def _():
        signal(barrier, z_device(my_z + 1))

    @pl.when(my_z > 0)
    def _():
        signal(barrier, z_device(my_z - 1))

    n_rows = 2 * group * per_dev
    to_row = lax.broadcasted_iota(jnp.int32, (n_rows, n_rows), 0)
    from_row = lax.broadcasted_iota(jnp.int32, (n_rows, n_rows), 1)
    wanted = lax.rem(to_row, 2 * group) * per_dev + to_row // (2 * group)
    order = jnp.where(from_row == wanted, 1.0, 0.0).astype(jnp.bfloat16)
    load_q.wait()
    tiles = [qv[t, :, h * HEAD_DIM : (h + 1) * HEAD_DIM] for t in range(2) for h in range(group)]
    stacked = jnp.concatenate(tiles, axis=0)
    query = jnp.dot(order, stacked, preferred_element_type=jnp.float32).astype(jnp.bfloat16)

    load_toks.wait()

    @pl.when(tp < n_tp - 1)
    def _():
        bias_most.wait()

    @pl.when(tp == n_tp - 1)
    def _():
        bias_rest.wait()

    lanes = lax.broadcasted_iota(jnp.int32, (1, 128), 1)
    for p in range(per_dev):
        for t in range(2):
            token = toks[t, p]
            spot = token // 128 - tp * bias_part
            held = jnp.logical_and(spot >= 0, spot < bias_part)
            lane = jnp.where(held, lax.rem(token, 128), -1)
            row = biasv[pl.ds(jnp.clip(spot, 0, bias_part - 1), 1), :]
            bias_rows[p * 2 + t : p * 2 + t + 1, :] = jnp.where(lanes == lane, row, 0.0)

    nt = (((1,), (1,)), ((), ()))
    part = 2 * group
    chunk = 512
    top = None
    for c in range(prompt_len // chunk):
        if c * chunk % key_part == 0:
            load_keys[c * chunk // key_part].wait()
        raw = lax.dot_general(
            query, keyv[c * chunk : (c + 1) * chunk, :], nt, preferred_element_type=jnp.float32
        )
        scores[:, c * chunk : (c + 1) * chunk] = raw
        for i in range(chunk // 128):
            piece = raw[:, i * 128 : (i + 1) * 128]
            top = piece if top is None else jnp.maximum(top, piece)

    load_lens.wait()
    load_new.wait()
    load_gen.wait()
    rows = lax.broadcasted_iota(jnp.int32, (gen, 2 * HEAD_DIM), 0)
    for p in range(per_dev):
        start = lens[base + p]
        first = newv[0, pl.ds(p, 1), :].astype(jnp.float32)
        second = newv[1, pl.ds(p, 1), :].astype(jnp.float32)
        kept = cache[p].astype(jnp.float32)
        later = jnp.where(rows == start + 1, second, 0.0)
        grown = jnp.where(rows < start, kept, jnp.where(rows == start, first, later))
        cache[p] = grown.astype(jnp.bfloat16)

    own = []
    cols = lax.broadcasted_iota(jnp.int32, (part, gen), 1)
    step = lax.broadcasted_iota(jnp.int32, (part, gen), 0) // group
    for p in range(per_dev):
        raw = lax.dot_general(
            query[p * part : (p + 1) * part], cache[p, :, 0:HEAD_DIM], nt,
            preferred_element_type=jnp.float32,
        )
        own.append(jnp.where(cols <= lens[base + p] + step, raw, NEG_FILL))
    own = jnp.concatenate(own, axis=0)
    row_max = jnp.max(jnp.maximum(top, own), axis=1, keepdims=True)
    scale = LOG2E / math.sqrt(HEAD_DIM)
    exps = jnp.exp2((own - row_max) * scale)
    total = exps
    probs = exps.astype(jnp.bfloat16)
    mixed = []
    for p in range(per_dev):
        mixed.append(
            jnp.dot(
                probs[p * part : (p + 1) * part], cache[p, :, HEAD_DIM : 2 * HEAD_DIM],
                preferred_element_type=jnp.float32,
            )
        )
    mixed = jnp.concatenate(mixed, axis=0)
    for c in range(prompt_len // chunk):
        if c * chunk % key_part == 0:
            load_vals[c * chunk // key_part].wait()
        exps = jnp.exp2((scores[:, c * chunk : (c + 1) * chunk] - row_max) * scale)
        for i in range(chunk // 128):
            total = total + exps[:, i * 128 : (i + 1) * 128]
        mixed = mixed + jnp.dot(
            exps.astype(jnp.bfloat16), valv[c * chunk : (c + 1) * chunk, :],
            preferred_element_type=jnp.float32,
        )
    row_sum = jnp.sum(total, axis=1, keepdims=True)
    mixed = mixed / row_sum
    load_tv.wait()
    weighted = mixed.reshape(2 * per_dev, group, HEAD_DIM) * tvv[...][None]
    pair_rows = jnp.sum(weighted, axis=1) + bias_rows[...]
    pair_col = jnp.sum(pair_rows, axis=1, keepdims=True)
    pair_ids = lax.broadcasted_iota(jnp.int32, (2 * per_dev, 128), 0)
    lane_ids = lax.broadcasted_iota(jnp.int32, (2 * per_dev, 128), 1)
    at_lane = lane_ids == lax.rem(pair_ids, 2) * per_dev + pair_ids // 2
    message = jnp.sum(jnp.where(at_lane, pair_col, 0.0), axis=0, keepdims=True)
    first_tp = jnp.where(tp == 0, 1.0, 0.0)
    load_prior.wait()
    for p in range(per_dev):
        message = jnp.where(lanes == 2 * per_dev + p, prior[p] * first_tp, message)
    me = tp * Y_DIM + my_y
    plane_rows[me] = message

    around = lambda count, top: (count > 0).astype(jnp.int32) + (count < top - 1).astype(jnp.int32)
    pl.semaphore_wait(barrier, n_plane - 1 + around(dom, n_dom) + around(my_z, n_z))

    def plane_copy(src, dst, peer):
        return pltpu.make_async_remote_copy(
            src_ref=plane_rows.at[src],
            dst_ref=plane_rows.at[dst],
            send_sem=plane_send.at[peer[0]],
            recv_sem=plane_recv.at[dst],
            device_id=peer[1],
            device_id_type=MESH,
        )

    def plane_start(k, carry):
        plane_copy(me, me, plane_peer(k)).start()
        return carry

    lax.fori_loop(1, n_plane, plane_start, 0)

    load_anc.wait()
    for slot, offset in enumerate(OFFSETS):
        target = jnp.clip(dom + offset, 0, n_dom - 1) * per_dev
        low, high = per_dev - 1, 0
        for i in range(per_dev):
            spot = anc[target + i] - base
            mine = jnp.logical_and(spot >= 0, spot < per_dev)
            low = jnp.minimum(low, jnp.where(mine, spot, per_dev - 1))
            high = jnp.maximum(high, jnp.where(mine, spot, 0))
        picked[slot, 0] = cache[low]
        picked[slot, 1] = cache[high]

    @pl.when(my_z > 0)
    def _():
        pl.semaphore_wait(below_sem, 1)

    @pl.when(my_z < n_z - 1)
    def _():
        signal(below_sem, z_device(my_z + 1))

    def greet_below(z, carry):
        signal(above_sem, z_device(z))
        return carry

    lax.fori_loop(0, my_z, greet_below, 0)

    def hop(src, dst, i, shift):
        return pltpu.make_async_remote_copy(
            src_ref=src,
            dst_ref=dst,
            send_sem=hop_send.at[i],
            recv_sem=hop_recv.at[i],
            device_id=device(jnp.clip(dom + shift, 0, n_dom - 1), tp),
            device_id_type=MESH,
        )

    far = n_dom - 1
    inner = jnp.logical_and(dom > 0, dom < far)
    hops = [
        (hop(picked.at[0], relay.at[0], 0, 1), dom < far - 1, inner),
        (hop(picked.at[2], relay.at[1], 1, -1), dom > 1, inner),
        (hop(picked.at[1], landed.at[1], 2, 1), dom < far, dom > 0),
        (hop(picked.at[3], landed.at[3], 3, -1), dom > 0, dom < far),
        (hop(relay.at[0], landed.at[0], 4, 1), inner, dom > 1),
        (hop(relay.at[1], landed.at[2], 5, -1), inner, dom < far - 1),
    ]

    def start_hop(i):
        pl.when(hops[i][1])(hops[i][0].start)

    def receive_hop(i):
        pl.when(hops[i][2])(hops[i][0].wait_recv)

    for i in range(4):
        start_hop(i)

    def plane_wait(k, carry):
        peer = plane_peer(k)
        plane_copy(me, peer[0], peer).wait()
        return carry

    lax.fori_loop(1, n_plane, plane_wait, 0)

    def summed(y):
        acc = plane_rows[y]
        for t in range(1, n_tp):
            acc = acc + plane_rows[t * Y_DIM + y]
        return acc

    def weights(acc):
        later = pltpu.roll(acc, 128 - per_dev, 1)
        given = pltpu.roll(acc, 128 - 2 * per_dev, 1)
        return jnp.where(lanes < per_dev, given + later - acc, NEG_FILL), later

    all_weights = jnp.concatenate([weights(summed(y))[0] for y in range(Y_DIM)], axis=0)
    z_max = jnp.max(jnp.max(all_weights, axis=1, keepdims=True), axis=0, keepdims=True)
    z_exp = jnp.exp(all_weights - z_max)
    z_sum = jnp.sum(jnp.sum(z_exp, axis=1, keepdims=True), axis=0, keepdims=True)
    z_rows[my_z, 0:1, :] = jnp.broadcast_to(z_max, (1, 128))
    z_rows[my_z, 1:2, :] = jnp.broadcast_to(z_sum, (1, 128))

    def z_copy(dst, z):
        return pltpu.make_async_remote_copy(
            src_ref=z_rows.at[my_z],
            dst_ref=z_rows.at[dst],
            send_sem=z_send.at[z],
            recv_sem=z_recv.at[dst],
            device_id=z_device(z),
            device_id_type=MESH,
        )

    def z_start(z, carry):
        z_copy(my_z, z).start()
        return carry

    lax.fori_loop(0, my_z, z_start, 0)

    receive_hop(0)
    start_hop(4)
    receive_hop(1)
    start_hop(5)

    @pl.when(my_z < n_z - 1)
    def _():
        pl.semaphore_wait(above_sem, n_z - 1 - my_z)

    lax.fori_loop(my_z + 1, n_z, z_start, 0)

    own_sum = summed(my_y)
    own_weight, own_later = weights(own_sum)
    twist_out[0:1, :] = own_sum[:, 0:per_dev]
    twist_out[1:2, :] = own_later[:, 0:per_dev]

    for i in range(2, 6):
        receive_hop(i)
    firsts = []
    for offset in OFFSETS:
        low = per_dev - 1
        for i in range(per_dev):
            spot = anc[base + i] - (base - offset * per_dev)
            theirs = jnp.logical_and(spot >= 0, spot < per_dev)
            low = jnp.minimum(low, jnp.where(theirs, spot, per_dev - 1))
        firsts.append(low)
    new_lens = jnp.zeros((1, 128), jnp.int32)
    for p in range(per_dev):
        new_lens = jnp.where(lanes == p, lens[anc[base + p]] + 2, new_lens)
        spot = anc[base + p] - base
        home = jnp.logical_and(spot >= 0, spot < per_dev)
        home_spot = jnp.clip(spot, 0, per_dev - 1)
        place = 0
        for slot, offset in enumerate(OFFSETS):
            there = spot + offset * per_dev
            theirs = jnp.logical_and(there >= 0, there < per_dev)
            second = jnp.where(there == firsts[slot], 0, 1)
            place = jnp.where(theirs, 2 * slot + second, place)
        moved = landed[place // 2, lax.rem(place, 2)]
        cache_out[p] = jnp.where(home, cache[home_spot], moved)
    len_out[...] = new_lens[:, 0:per_dev]

    def z_wait(k, carry):
        z = lax.rem(my_z + k, n_z)
        z_copy(z, z).wait()
        return carry

    lax.fori_loop(1, n_z, z_wait, 0)
    maxes = z_rows[:, 0, :]
    sums = z_rows[:, 1, :]
    largest = jnp.max(maxes, axis=0, keepdims=True)
    exp_total = jnp.sum(sums * jnp.exp(maxes - largest), axis=0, keepdims=True)
    normalized = own_weight - (largest + jnp.log(exp_total))
    norm_out[...] = normalized[:, 0:per_dev]

    for item, sends, _ in hops:
        pl.when(sends)(item.wait_send)


def finish(*refs):
    count = (len(refs) - 1) // 2
    copies = [
        pltpu.make_async_copy(refs[i], refs[count + i], refs[-1].at[i]) for i in range(count)
    ]
    for item in copies:
        item.start()
    for item in copies:
        item.wait()


def local(
    n_dom,
    n_tp,
    queries,
    new_kv,
    gen_cache,
    prompt_kv,
    lengths,
    ancestors,
    tokens,
    twist_vector,
    twist_bias,
    prior_weights,
):
    per_dev, gen, width = gen_cache.shape
    prompt_len = prompt_kv.shape[0]
    group = queries.shape[2] // HEAD_DIM
    n_rows = 2 * group * per_dev
    n_z = n_dom // Y_DIM
    n_plane = n_tp * Y_DIM
    bias_table = twist_bias.reshape(-1, 128)
    bias_part = -(-bias_table.shape[0] // (8 * n_tp)) * 8
    any_space = pl.BlockSpec(memory_space=pl.ANY)
    vmem = pl.BlockSpec(memory_space=pltpu.VMEM)
    f32, bf16, i32 = jnp.float32, jnp.bfloat16, jnp.int32
    dma = pltpu.SemaphoreType.DMA
    shapes = (((2, per_dev), f32), ((1, per_dev), f32), (gen_cache.shape, bf16), ((1, per_dev), i32))
    results = pl.pallas_call(
        functools.partial(kernel, (n_dom, n_tp, per_dev, gen, prompt_len, group)),
        out_shape=tuple(pltpu.VMEM(*shape) for shape in shapes),
        in_specs=[any_space] * 10,
        out_specs=(vmem,) * 4,
        scratch_shapes=[
            pltpu.SMEM(ancestors.shape, i32),
            pltpu.SMEM(lengths.shape, i32),
            pltpu.SMEM(tokens.shape, i32),
            pltpu.SMEM(prior_weights.shape, f32),
            pltpu.VMEM(queries.shape, bf16),
            pltpu.VMEM(new_kv.shape, bf16),
            pltpu.VMEM(gen_cache.shape, bf16),
            pltpu.VMEM((prompt_len, HEAD_DIM), bf16),
            pltpu.VMEM((prompt_len, HEAD_DIM), bf16),
            pltpu.VMEM((group, HEAD_DIM), f32),
            pltpu.VMEM((bias_part, 128), f32),
            pltpu.VMEM((n_rows, prompt_len), f32),
            pltpu.VMEM((4, 2, gen, width), bf16),
            pltpu.VMEM((2, 2, gen, width), bf16),
            pltpu.VMEM((4, 2, gen, width), bf16),
            pltpu.VMEM((2 * per_dev, 128), f32),
            pltpu.VMEM((n_plane, 1, 128), f32),
            pltpu.VMEM((n_z, 2, 128), f32),
            dma((5,)),
            dma((4,)),
            dma((PARTS,)),
            dma((PARTS,)),
            dma((6,)),
            dma((6,)),
            dma((n_plane,)),
            dma((n_plane,)),
            dma((n_z,)),
            dma((n_z,)),
            pltpu.SemaphoreType.REGULAR,
            pltpu.SemaphoreType.REGULAR,
        ],
        compiler_params=pltpu.CompilerParams(collective_id=0, has_side_effects=True),
        name="smc_step",
    )(
        ancestors,
        lengths,
        tokens,
        prior_weights,
        queries,
        new_kv,
        gen_cache,
        prompt_kv,
        twist_vector.reshape(group, HEAD_DIM),
        bias_table,
    )
    held = [pltpu.with_memory_space_constraint(x, pltpu.VMEM) for x in results]
    twist, normalized, resampled, new_lengths = pl.pallas_call(
        finish,
        out_shape=tuple(jax.ShapeDtypeStruct(*shape) for shape in shapes),
        in_specs=[any_space] * 4,
        out_specs=(any_space,) * 4,
        scratch_shapes=[dma((4,))],
        compiler_params=pltpu.CompilerParams(vmem_limit_bytes=4 << 20),
        name="finish",
    )(*held)
    return twist, normalized.reshape(per_dev), resampled, new_lengths.reshape(per_dev)


def solution(mesh):
    in_specs = (
        P(None, "dom", "tp"),
        P(None, "dom", "tp"),
        P("dom", None, "tp"),
        P(None, "tp"),
        P(),
        P(),
        P(None, "dom"),
        P("tp"),
        P(),
        P("dom"),
    )
    out_specs = (P(None, "dom"), P("dom"), P("dom", None, "tp"), P("dom"))
    return jax.shard_map(
        functools.partial(local, mesh.shape["dom"], mesh.shape["tp"]),
        mesh=mesh,
        in_specs=in_specs,
        out_specs=out_specs,
        check_vma=False,
    )
```

```python
import functools
import math

import jax
import jax.numpy as jnp
from jax import lax
from jax.experimental import pallas as pl
from jax.experimental.pallas import tpu as pltpu
from jax.sharding import PartitionSpec as P

HEAD_DIM = 128
Y_DIM = 4
NEG_FILL = -1e30
MESH = pl.DeviceIdType.MESH
LOG2E = 1.4426950408889634
PARTS = 4
OFFSETS = (2, 1, -2, -1)


def kernel(
    sizes,
    anc_hbm,
    lens_hbm,
    toks_hbm,
    prior_hbm,
    q_hbm,
    new_hbm,
    gen_hbm,
    prompt_hbm,
    tv_hbm,
    bias_hbm,
    twist_out,
    norm_out,
    cache_out,
    len_out,
    anc,
    lens,
    toks,
    prior,
    qv,
    newv,
    cache,
    keyv,
    valv,
    tvv,
    biasv,
    scores,
    picked,
    relay,
    landed,
    bias_rows,
    plane_rows,
    z_rows,
    small_sems,
    in_sems,
    key_sems,
    val_sems,
    hop_send,
    hop_recv,
    plane_send,
    plane_recv,
    z_send,
    z_recv,
    next_sem,
    above_sem,
):
    n_dom, n_tp, per_dev, gen, prompt_len, group = sizes
    f32, bf16 = jnp.float32, jnp.bfloat16
    n_z = n_dom // Y_DIM
    n_plane = n_tp * Y_DIM
    dom = lax.axis_index("dom")
    tp = lax.axis_index("tp")
    my_y = lax.rem(dom, Y_DIM)
    my_z = dom // Y_DIM
    base = dom * per_dev
    bias_len = bias_hbm.shape[0]
    bias_part = biasv.shape[0]
    bias_last = bias_len - (n_tp - 1) * bias_part
    key_part = prompt_len // PARTS

    def device(d, t):
        return {"dom": d, "tp": t}

    def signal(sem, target):
        pl.semaphore_signal(sem, inc=1, device_id=target, device_id_type=MESH)

    def z_device(z):
        return device(z * Y_DIM + my_y, tp)

    me = tp * Y_DIM + my_y

    def plane_slot(k):
        return lax.rem(me + k, n_plane)

    def plane_device(slot):
        return device(my_z * Y_DIM + lax.rem(slot, Y_DIM), slot // Y_DIM)

    copy = pltpu.make_async_copy
    load_q = copy(q_hbm, qv, in_sems.at[0])
    load_gen = copy(gen_hbm, cache, in_sems.at[1])
    load_new = copy(new_hbm, newv, in_sems.at[2])
    load_tv = copy(tv_hbm, tvv, in_sems.at[3])
    load_keys = [
        copy(
            prompt_hbm.at[c * key_part : (c + 1) * key_part, 0:HEAD_DIM],
            keyv.at[c * key_part : (c + 1) * key_part],
            key_sems.at[c],
        )
        for c in range(PARTS)
    ]
    load_vals = [
        copy(
            prompt_hbm.at[c * key_part : (c + 1) * key_part, HEAD_DIM : 2 * HEAD_DIM],
            valv.at[c * key_part : (c + 1) * key_part],
            val_sems.at[c],
        )
        for c in range(PARTS)
    ]
    load_anc = copy(anc_hbm, anc, small_sems.at[0])
    load_lens = copy(lens_hbm, lens, small_sems.at[1])
    load_toks = copy(toks_hbm, toks, small_sems.at[2])
    load_prior = copy(prior_hbm, prior, small_sems.at[3])
    bias_most = copy(
        bias_hbm.at[pl.ds(pl.multiple_of(tp * bias_part, 8), bias_part)], biasv, small_sems.at[4]
    )
    bias_rest = copy(
        bias_hbm.at[bias_len - bias_last : bias_len], biasv.at[0:bias_last], small_sems.at[4]
    )
    load_q.start()
    for item in load_keys:
        item.start()
    load_toks.start()
    load_lens.start()

    @pl.when(tp < n_tp - 1)
    def _():
        bias_most.start()

    @pl.when(tp == n_tp - 1)
    def _():
        bias_rest.start()

    load_gen.start()
    load_new.start()
    for item in load_vals:
        item.start()
    load_tv.start()
    load_prior.start()
    load_anc.start()

    barrier = pltpu.get_barrier_semaphore()

    def greet_plane(k, carry):
        signal(barrier, plane_device(plane_slot(k)))
        return carry

    def greet_above(z, carry):
        signal(barrier, z_device(z))
        return carry

    lax.fori_loop(1, n_plane, greet_plane, 0)
    lax.fori_loop(my_z + 1, n_z, greet_above, 0)

    @pl.when(dom < n_dom - 1)
    def _():
        signal(barrier, device(dom + 1, tp))

    n_rows = 2 * group * per_dev
    to_row = lax.broadcasted_iota(jnp.int32, (n_rows, n_rows), 0)
    from_row = lax.broadcasted_iota(jnp.int32, (n_rows, n_rows), 1)
    wanted = lax.rem(to_row, 2 * group) * per_dev + to_row // (2 * group)
    order = jnp.where(from_row == wanted, 1.0, 0.0).astype(jnp.bfloat16)
    load_q.wait()
    tiles = [qv[t, :, h * HEAD_DIM : (h + 1) * HEAD_DIM] for t in range(2) for h in range(group)]
    stacked = jnp.concatenate(tiles, axis=0)
    query = jnp.dot(order, stacked, preferred_element_type=jnp.float32).astype(jnp.bfloat16)

    load_toks.wait()

    @pl.when(tp < n_tp - 1)
    def _():
        bias_most.wait()

    @pl.when(tp == n_tp - 1)
    def _():
        bias_rest.wait()

    lanes = lax.broadcasted_iota(jnp.int32, (1, 128), 1)
    for p in range(per_dev):
        for t in range(2):
            token = toks[t, p]
            spot = token // 128 - tp * bias_part
            held = jnp.logical_and(spot >= 0, spot < bias_part)
            lane = jnp.where(held, lax.rem(token, 128), -1)
            row = biasv[pl.ds(jnp.clip(spot, 0, bias_part - 1), 1), :]
            bias_rows[p * 2 + t : p * 2 + t + 1, :] = jnp.where(lanes == lane, row, 0.0)

    nt = (((1,), (1,)), ((), ()))
    part = 2 * group
    chunk = 512
    top = None
    for c in range(prompt_len // chunk):
        if c * chunk % key_part == 0:
            load_keys[c * chunk // key_part].wait()
        raw = lax.dot_general(
            query, keyv[c * chunk : (c + 1) * chunk, :], nt, preferred_element_type=jnp.float32
        )
        scores[:, c * chunk : (c + 1) * chunk] = raw
        for i in range(chunk // 128):
            piece = raw[:, i * 128 : (i + 1) * 128]
            top = piece if top is None else jnp.maximum(top, piece)

    load_lens.wait()
    load_new.wait()
    load_gen.wait()
    rows = lax.broadcasted_iota(jnp.int32, (gen, 2 * HEAD_DIM), 0).astype(f32).astype(bf16)
    for p in range(per_dev):
        start = lens[base + p].astype(f32)
        at_first = jnp.full((gen, 2 * HEAD_DIM), start, f32).astype(bf16)
        at_second = jnp.full((gen, 2 * HEAD_DIM), start + 1.0, f32).astype(bf16)
        first = jnp.broadcast_to(newv[0, pl.ds(p, 1), :], (gen, 2 * HEAD_DIM))
        second = jnp.broadcast_to(newv[1, pl.ds(p, 1), :], (gen, 2 * HEAD_DIM))
        later = jnp.where(rows == at_second, second, jnp.zeros_like(second))
        cache[p] = jnp.where(
            rows < at_first, cache[p], jnp.where(rows == at_first, first, later)
        )

    own = []
    cols = lax.broadcasted_iota(jnp.int32, (part, gen), 1)
    step = lax.broadcasted_iota(jnp.int32, (part, gen), 0) // group
    for p in range(per_dev):
        raw = lax.dot_general(
            query[p * part : (p + 1) * part], cache[p, :, 0:HEAD_DIM], nt,
            preferred_element_type=jnp.float32,
        )
        own.append(jnp.where(cols <= lens[base + p] + step, raw, NEG_FILL))
    own = jnp.concatenate(own, axis=0)
    row_max = jnp.max(jnp.maximum(top, own), axis=1, keepdims=True)
    scale = LOG2E / math.sqrt(HEAD_DIM)
    exps = jnp.exp2((own - row_max) * scale)
    total = exps
    probs = exps.astype(jnp.bfloat16)
    mixed = []
    for p in range(per_dev):
        mixed.append(
            jnp.dot(
                probs[p * part : (p + 1) * part], cache[p, :, HEAD_DIM : 2 * HEAD_DIM],
                preferred_element_type=jnp.float32,
            )
        )
    mixed = jnp.concatenate(mixed, axis=0)
    for c in range(prompt_len // chunk):
        if c * chunk % key_part == 0:
            load_vals[c * chunk // key_part].wait()
        exps = jnp.exp2((scores[:, c * chunk : (c + 1) * chunk] - row_max) * scale)
        for i in range(chunk // 128):
            total = total + exps[:, i * 128 : (i + 1) * 128]
        mixed = mixed + jnp.dot(
            exps.astype(jnp.bfloat16), valv[c * chunk : (c + 1) * chunk, :],
            preferred_element_type=jnp.float32,
        )
    row_sum = jnp.sum(total, axis=1, keepdims=True)
    mixed = mixed / row_sum
    load_tv.wait()
    weighted = mixed.reshape(2 * per_dev, group, HEAD_DIM) * tvv[...][None]
    pair_rows = jnp.sum(weighted, axis=1) + bias_rows[...]
    pair_col = jnp.sum(pair_rows, axis=1, keepdims=True)
    pair_ids = lax.broadcasted_iota(jnp.int32, (2 * per_dev, 128), 0)
    lane_ids = lax.broadcasted_iota(jnp.int32, (2 * per_dev, 128), 1)
    at_lane = lane_ids == lax.rem(pair_ids, 2) * per_dev + pair_ids // 2
    message = jnp.sum(jnp.where(at_lane, pair_col, 0.0), axis=0, keepdims=True)
    first_tp = jnp.where(tp == 0, 1.0, 0.0)
    load_prior.wait()
    for p in range(per_dev):
        message = jnp.where(lanes == 2 * per_dev + p, prior[p] * first_tp, message)
    plane_rows[me] = message

    pl.semaphore_wait(
        barrier, n_plane - 1 + my_z + jnp.where(dom > 0, 1, 0)
    )

    n_x = n_tp // 2
    my_x, core = tp // 2, lax.rem(tp, 2)
    farthest = lambda n: sorted(range(n), key=lambda d: -min(d, n - d))
    targets = []
    for target_core in range(2):
        for dx in farthest(n_x):
            for dy in farthest(Y_DIM):
                if dx or dy:
                    targets.append((dx, dy, target_core))
    targets.append((0, 0, 1 - core))

    def plane_send_to(j):
        dx, dy, target_core = targets[j]
        x = lax.rem(my_x + dx, n_x)
        y = lax.rem(my_y + dy, Y_DIM)
        return pltpu.make_async_remote_copy(
            src_ref=plane_rows.at[me],
            dst_ref=plane_rows.at[me],
            send_sem=plane_send.at[j],
            recv_sem=plane_recv.at[me],
            device_id=device(my_z * Y_DIM + y, x * 2 + target_core),
            device_id_type=MESH,
        )

    plane_sends = [plane_send_to(j) for j in range(len(targets))]
    for item in plane_sends:
        item.start()

    @pl.when(dom > 0)
    def _():
        signal(next_sem, device(dom - 1, tp))

    load_anc.wait()
    for slot, offset in enumerate(OFFSETS):
        target = jnp.clip(dom + offset, 0, n_dom - 1) * per_dev
        low, high = per_dev - 1, 0
        for i in range(per_dev):
            spot = anc[target + i] - base
            mine = jnp.logical_and(spot >= 0, spot < per_dev)
            low = jnp.minimum(low, jnp.where(mine, spot, per_dev - 1))
            high = jnp.maximum(high, jnp.where(mine, spot, 0))
        picked[slot, 0] = cache[low]
        picked[slot, 1] = cache[high]

    def plane_wait(k, carry):
        slot = plane_slot(k)
        pltpu.make_async_remote_copy(
            src_ref=plane_rows.at[slot],
            dst_ref=plane_rows.at[slot],
            send_sem=plane_send.at[0],
            recv_sem=plane_recv.at[slot],
            device_id=plane_device(slot),
            device_id_type=MESH,
        ).wait_recv()
        return carry

    lax.fori_loop(1, n_plane, plane_wait, 0)

    def summed(y):
        acc = plane_rows[y]
        for t in range(1, n_tp):
            acc = acc + plane_rows[t * Y_DIM + y]
        return acc

    def weights(acc):
        later = pltpu.roll(acc, 128 - per_dev, 1)
        given = pltpu.roll(acc, 128 - 2 * per_dev, 1)
        return jnp.where(lanes < per_dev, given + later - acc, NEG_FILL), later

    all_weights = jnp.concatenate([weights(summed(y))[0] for y in range(Y_DIM)], axis=0)
    z_max = jnp.max(jnp.max(all_weights, axis=1, keepdims=True), axis=0, keepdims=True)
    z_exp = jnp.exp(all_weights - z_max)
    z_sum = jnp.sum(jnp.sum(z_exp, axis=1, keepdims=True), axis=0, keepdims=True)
    z_rows[my_z, 0:1, :] = jnp.broadcast_to(z_max, (1, 128))
    z_rows[my_z, 1:2, :] = jnp.broadcast_to(z_sum, (1, 128))

    def z_copy(dst, z):
        return pltpu.make_async_remote_copy(
            src_ref=z_rows.at[my_z],
            dst_ref=z_rows.at[dst],
            send_sem=z_send.at[z],
            recv_sem=z_recv.at[dst],
            device_id=z_device(z),
            device_id_type=MESH,
        )

    def z_start(z, carry):
        z_copy(my_z, z).start()
        return carry

    lax.fori_loop(0, my_z, z_start, 0)

    def greet_below(z, carry):
        signal(above_sem, z_device(z))
        return carry

    lax.fori_loop(0, my_z, greet_below, 0)

    def hop(src, dst, i, shift):
        return pltpu.make_async_remote_copy(
            src_ref=src,
            dst_ref=dst,
            send_sem=hop_send.at[i],
            recv_sem=hop_recv.at[i],
            device_id=device(jnp.clip(dom + shift, 0, n_dom - 1), tp),
            device_id_type=MESH,
        )

    far = n_dom - 1
    inner = jnp.logical_and(dom > 0, dom < far)
    hops = [
        (hop(picked.at[0], relay.at[0], 0, 1), dom < far - 1, inner),
        (hop(picked.at[2], relay.at[1], 1, -1), dom > 1, inner),
        (hop(picked.at[1], landed.at[1], 2, 1), dom < far, dom > 0),
        (hop(picked.at[3], landed.at[3], 3, -1), dom > 0, dom < far),
        (hop(relay.at[0], landed.at[0], 4, 1), inner, dom > 1),
        (hop(relay.at[1], landed.at[2], 5, -1), inner, dom < far - 1),
    ]

    def start_hop(i):
        pl.when(hops[i][1])(hops[i][0].start)

    def receive_hop(i):
        pl.when(hops[i][2])(hops[i][0].wait_recv)

    @pl.when(dom < far)
    def _():
        pl.semaphore_wait(next_sem, 1)

    for i in range(4):
        start_hop(i)

    receive_hop(0)
    start_hop(4)
    receive_hop(1)
    start_hop(5)

    @pl.when(my_z < n_z - 1)
    def _():
        pl.semaphore_wait(above_sem, n_z - 1 - my_z)

    lax.fori_loop(my_z + 1, n_z, z_start, 0)

    own_sum = summed(my_y)
    own_weight, own_later = weights(own_sum)
    twist_out[0:1, :] = own_sum[:, 0:per_dev]
    twist_out[1:2, :] = own_later[:, 0:per_dev]

    for i in range(2, 6):
        receive_hop(i)
    firsts = []
    for offset in OFFSETS:
        low = per_dev - 1
        for i in range(per_dev):
            spot = anc[base + i] - (base - offset * per_dev)
            theirs = jnp.logical_and(spot >= 0, spot < per_dev)
            low = jnp.minimum(low, jnp.where(theirs, spot, per_dev - 1))
        firsts.append(low)
    new_lens = jnp.zeros((1, 128), jnp.int32)
    for p in range(per_dev):
        new_lens = jnp.where(lanes == p, lens[anc[base + p]] + 2, new_lens)
        spot = anc[base + p] - base
        home = jnp.logical_and(spot >= 0, spot < per_dev)
        home_spot = jnp.clip(spot, 0, per_dev - 1)
        place = 0
        for slot, offset in enumerate(OFFSETS):
            there = spot + offset * per_dev
            theirs = jnp.logical_and(there >= 0, there < per_dev)
            second = jnp.where(there == firsts[slot], 0, 1)
            place = jnp.where(theirs, 2 * slot + second, place)
        moved = landed[place // 2, lax.rem(place, 2)]
        cache_out[p] = jnp.where(home, cache[home_spot], moved)
    len_out[...] = new_lens[:, 0:per_dev]

    def z_wait(k, carry):
        z = lax.rem(my_z + k, n_z)
        z_copy(z, z).wait()
        return carry

    lax.fori_loop(1, n_z, z_wait, 0)
    maxes = z_rows[:, 0, :]
    sums = z_rows[:, 1, :]
    largest = jnp.max(maxes, axis=0, keepdims=True)
    exp_total = jnp.sum(sums * jnp.exp(maxes - largest), axis=0, keepdims=True)
    normalized = own_weight - (largest + jnp.log(exp_total))
    norm_out[...] = normalized[:, 0:per_dev]

    for item, sends, _ in hops:
        pl.when(sends)(item.wait_send)
    for item in plane_sends:
        item.wait_send()


def finish(*refs):
    count = (len(refs) - 1) // 2
    copies = [
        pltpu.make_async_copy(refs[i], refs[count + i], refs[-1].at[i]) for i in range(count)
    ]
    for item in copies:
        item.start()
    for item in copies:
        item.wait()


def local(
    n_dom,
    n_tp,
    queries,
    new_kv,
    gen_cache,
    prompt_kv,
    lengths,
    ancestors,
    tokens,
    twist_vector,
    twist_bias,
    prior_weights,
):
    per_dev, gen, width = gen_cache.shape
    prompt_len = prompt_kv.shape[0]
    group = queries.shape[2] // HEAD_DIM
    n_rows = 2 * group * per_dev
    n_z = n_dom // Y_DIM
    n_plane = n_tp * Y_DIM
    bias_table = twist_bias.reshape(-1, 128)
    bias_part = -(-bias_table.shape[0] // (8 * n_tp)) * 8
    any_space = pl.BlockSpec(memory_space=pl.ANY)
    vmem = pl.BlockSpec(memory_space=pltpu.VMEM)
    f32, bf16, i32 = jnp.float32, jnp.bfloat16, jnp.int32
    dma = pltpu.SemaphoreType.DMA
    shapes = (((2, per_dev), f32), ((1, per_dev), f32), (gen_cache.shape, bf16), ((1, per_dev), i32))
    results = pl.pallas_call(
        functools.partial(kernel, (n_dom, n_tp, per_dev, gen, prompt_len, group)),
        out_shape=tuple(pltpu.VMEM(*shape) for shape in shapes),
        in_specs=[any_space] * 10,
        out_specs=(vmem,) * 4,
        scratch_shapes=[
            pltpu.SMEM(ancestors.shape, i32),
            pltpu.SMEM(lengths.shape, i32),
            pltpu.SMEM(tokens.shape, i32),
            pltpu.SMEM(prior_weights.shape, f32),
            pltpu.VMEM(queries.shape, bf16),
            pltpu.VMEM(new_kv.shape, bf16),
            pltpu.VMEM(gen_cache.shape, bf16),
            pltpu.VMEM((prompt_len, HEAD_DIM), bf16),
            pltpu.VMEM((prompt_len, HEAD_DIM), bf16),
            pltpu.VMEM((group, HEAD_DIM), f32),
            pltpu.VMEM((bias_part, 128), f32),
            pltpu.VMEM((n_rows, prompt_len), f32),
            pltpu.VMEM((4, 2, gen, width), bf16),
            pltpu.VMEM((2, 2, gen, width), bf16),
            pltpu.VMEM((4, 2, gen, width), bf16),
            pltpu.VMEM((2 * per_dev, 128), f32),
            pltpu.VMEM((n_plane, 1, 128), f32),
            pltpu.VMEM((n_z, 2, 128), f32),
            dma((5,)),
            dma((4,)),
            dma((PARTS,)),
            dma((PARTS,)),
            dma((6,)),
            dma((6,)),
            dma((n_plane,)),
            dma((n_plane,)),
            dma((n_z,)),
            dma((n_z,)),
            pltpu.SemaphoreType.REGULAR,
            pltpu.SemaphoreType.REGULAR,
        ],
        compiler_params=pltpu.CompilerParams(collective_id=0, has_side_effects=True),
        name="smc_step",
    )(
        ancestors,
        lengths,
        tokens,
        prior_weights,
        queries,
        new_kv,
        gen_cache,
        prompt_kv,
        twist_vector.reshape(group, HEAD_DIM),
        bias_table,
    )
    held = [pltpu.with_memory_space_constraint(x, pltpu.VMEM) for x in results]
    twist, normalized, resampled, new_lengths = pl.pallas_call(
        finish,
        out_shape=tuple(jax.ShapeDtypeStruct(*shape) for shape in shapes),
        in_specs=[any_space] * 4,
        out_specs=(any_space,) * 4,
        scratch_shapes=[dma((4,))],
        compiler_params=pltpu.CompilerParams(vmem_limit_bytes=4 << 20),
        name="finish",
    )(*held)
    return twist, normalized.reshape(per_dev), resampled, new_lengths.reshape(per_dev)


def solution(mesh):
    in_specs = (
        P(None, "dom", "tp"),
        P(None, "dom", "tp"),
        P("dom", None, "tp"),
        P(None, "tp"),
        P(),
        P(),
        P(None, "dom"),
        P("tp"),
        P(),
        P("dom"),
    )
    out_specs = (P(None, "dom"), P("dom"), P("dom", None, "tp"), P("dom"))
    return jax.shard_map(
        functools.partial(local, mesh.shape["dom"], mesh.shape["tp"]),
        mesh=mesh,
        in_specs=in_specs,
        out_specs=out_specs,
        check_vma=False,
    )
```

```python
import functools
import math

import jax
import jax.numpy as jnp
from jax import lax
from jax.experimental import pallas as pl
from jax.experimental.pallas import tpu as pltpu
from jax.sharding import PartitionSpec as P

HEAD_DIM = 128
Y_DIM = 4
NEG_FILL = -1e30
MESH = pl.DeviceIdType.MESH
LOG2E = 1.4426950408889634
PARTS = 4
OFFSETS = (2, 1, -2, -1)


def kernel(
    sizes,
    anc_hbm,
    lens_hbm,
    toks_hbm,
    prior_hbm,
    q_hbm,
    new_hbm,
    gen_hbm,
    prompt_hbm,
    tv_hbm,
    bias_hbm,
    twist_out,
    norm_out,
    cache_out,
    len_out,
    anc,
    lens,
    toks,
    prior,
    qv,
    newv,
    cache,
    keyv,
    valv,
    tvv,
    biasv,
    scores,
    picked,
    relay,
    landed,
    bias_rows,
    plane_rows,
    z_rows,
    small_sems,
    in_sems,
    key_sems,
    val_sems,
    hop_send,
    hop_recv,
    plane_send,
    plane_recv,
    z_send,
    z_recv,
    next_sem,
    above_sem,
):
    n_dom, n_tp, per_dev, gen, prompt_len, group = sizes
    f32, bf16 = jnp.float32, jnp.bfloat16
    n_z = n_dom // Y_DIM
    n_plane = n_tp * Y_DIM
    dom = lax.axis_index("dom")
    tp = lax.axis_index("tp")
    my_y = lax.rem(dom, Y_DIM)
    my_z = dom // Y_DIM
    base = dom * per_dev
    bias_len = bias_hbm.shape[0]
    bias_part = biasv.shape[0]
    bias_last = bias_len - (n_tp - 1) * bias_part
    key_part = prompt_len // PARTS

    def device(d, t):
        return {"dom": d, "tp": t}

    def signal(sem, target):
        pl.semaphore_signal(sem, inc=1, device_id=target, device_id_type=MESH)

    def z_device(z):
        return device(z * Y_DIM + my_y, tp)

    me = tp * Y_DIM + my_y

    def plane_slot(k):
        return lax.rem(me + k, n_plane)

    def plane_device(slot):
        return device(my_z * Y_DIM + lax.rem(slot, Y_DIM), slot // Y_DIM)

    copy = pltpu.make_async_copy
    load_q = copy(q_hbm, qv, in_sems.at[0])
    load_gen = copy(gen_hbm, cache, in_sems.at[1])
    load_new = copy(new_hbm, newv, in_sems.at[2])
    load_tv = copy(tv_hbm, tvv, in_sems.at[3])
    load_keys = [
        copy(
            prompt_hbm.at[c * key_part : (c + 1) * key_part, 0:HEAD_DIM],
            keyv.at[c * key_part : (c + 1) * key_part],
            key_sems.at[c],
        )
        for c in range(PARTS)
    ]
    load_vals = [
        copy(
            prompt_hbm.at[c * key_part : (c + 1) * key_part, HEAD_DIM : 2 * HEAD_DIM],
            valv.at[c * key_part : (c + 1) * key_part],
            val_sems.at[c],
        )
        for c in range(PARTS)
    ]
    load_anc = copy(anc_hbm, anc, small_sems.at[0])
    load_lens = copy(lens_hbm, lens, small_sems.at[1])
    load_toks = copy(toks_hbm, toks, small_sems.at[2])
    load_prior = copy(prior_hbm, prior, small_sems.at[3])
    bias_most = copy(
        bias_hbm.at[pl.ds(pl.multiple_of(tp * bias_part, 8), bias_part)], biasv, small_sems.at[4]
    )
    bias_rest = copy(
        bias_hbm.at[bias_len - bias_last : bias_len], biasv.at[0:bias_last], small_sems.at[4]
    )
    load_toks.start()
    load_prior.start()
    load_lens.start()
    load_q.start()

    @pl.when(tp < n_tp - 1)
    def _():
        bias_most.start()

    @pl.when(tp == n_tp - 1)
    def _():
        bias_rest.start()

    for item in load_keys:
        item.start()
    load_new.start()
    load_gen.start()
    for item in load_vals:
        item.start()
    load_tv.start()
    load_anc.start()

    barrier = pltpu.get_barrier_semaphore()

    def greet_plane(k, carry):
        signal(barrier, plane_device(plane_slot(k)))
        return carry

    def greet_above(z, carry):
        signal(barrier, z_device(z))
        return carry

    lax.fori_loop(1, n_plane, greet_plane, 0)
    lax.fori_loop(my_z + 1, n_z, greet_above, 0)

    @pl.when(dom < n_dom - 1)
    def _():
        signal(barrier, device(dom + 1, tp))

    n_rows = 2 * group * per_dev
    to_row = lax.broadcasted_iota(jnp.int32, (n_rows, n_rows), 0)
    from_row = lax.broadcasted_iota(jnp.int32, (n_rows, n_rows), 1)
    wanted = lax.rem(to_row, 2 * group) * per_dev + to_row // (2 * group)
    order = jnp.where(from_row == wanted, 1.0, 0.0).astype(jnp.bfloat16)
    load_q.wait()
    tiles = [qv[t, :, h * HEAD_DIM : (h + 1) * HEAD_DIM] for t in range(2) for h in range(group)]
    stacked = jnp.concatenate(tiles, axis=0)
    query = jnp.dot(order, stacked, preferred_element_type=jnp.float32).astype(jnp.bfloat16)

    load_toks.wait()

    @pl.when(tp < n_tp - 1)
    def _():
        bias_most.wait()

    @pl.when(tp == n_tp - 1)
    def _():
        bias_rest.wait()

    lanes = lax.broadcasted_iota(jnp.int32, (1, 128), 1)
    bias_start = tp * (bias_part * 128)
    for p in range(per_dev):
        for t in range(2):
            local_token = toks[t, p] - bias_start
            spot = jnp.clip(lax.shift_right_arithmetic(local_token, 7), 0, bias_part - 1)
            row = biasv[pl.ds(spot, 1), :]
            bias_rows[p * 2 + t : p * 2 + t + 1, :] = jnp.where(
                lanes == local_token - spot * 128, row, 0.0
            )

    first_tp = jnp.where(tp == 0, 1.0, 0.0)
    load_prior.wait()
    weight_lane = 2 * 2 * per_dev + per_dev * my_y
    prior_row = jnp.zeros((1, 128), f32)
    for p in range(per_dev):
        prior_row = jnp.where(lanes == weight_lane + p, prior[p] * first_tp, prior_row)
    pair_ids = lax.broadcasted_iota(jnp.int32, (2 * per_dev, 128), 0)
    lane_ids = lax.broadcasted_iota(jnp.int32, (2 * per_dev, 128), 1)
    pair_step = lax.rem(pair_ids, 2)
    at_twist = lane_ids == pair_step * per_dev + pair_ids // 2
    at_weight = lane_ids == weight_lane + pair_ids // 2
    placed = jnp.where(
        at_twist, 1.0, jnp.where(at_weight, (2 * pair_step - 1).astype(f32), 0.0)
    )

    nt = (((1,), (1,)), ((), ()))
    part = 2 * group
    chunk = 512
    top = None
    for c in range(prompt_len // chunk):
        if c * chunk % key_part == 0:
            load_keys[c * chunk // key_part].wait()
        raw = lax.dot_general(
            query, keyv[c * chunk : (c + 1) * chunk, :], nt, preferred_element_type=jnp.float32
        )
        scores[:, c * chunk : (c + 1) * chunk] = raw
        for i in range(chunk // 128):
            piece = raw[:, i * 128 : (i + 1) * 128]
            top = piece if top is None else jnp.maximum(top, piece)

    load_lens.wait()
    load_new.wait()
    filler = jnp.zeros((128 - 2 * per_dev, HEAD_DIM), bf16)
    new_keys = jnp.concatenate([newv[0, :, 0:HEAD_DIM], newv[1, :, 0:HEAD_DIM], filler], axis=0)
    new_vals = jnp.concatenate(
        [newv[0, :, HEAD_DIM : 2 * HEAD_DIM], newv[1, :, HEAD_DIM : 2 * HEAD_DIM], filler], axis=0
    )
    new_row = lax.broadcasted_iota(jnp.int32, (n_rows, 128), 0)
    new_col = lax.broadcasted_iota(jnp.int32, (n_rows, 128), 1)
    shown = jnp.logical_and(
        lax.rem(new_col, per_dev) == new_row // (2 * group),
        new_col // per_dev <= lax.rem(new_row // group, 2),
    )
    fresh = lax.dot_general(query, new_keys, nt, preferred_element_type=f32)
    fresh = jnp.where(shown, fresh, NEG_FILL)
    load_gen.wait()
    own = []
    cols = lax.broadcasted_iota(jnp.int32, (part, gen), 1)
    for p in range(per_dev):
        raw = lax.dot_general(
            query[p * part : (p + 1) * part], cache[p, :, 0:HEAD_DIM], nt,
            preferred_element_type=jnp.float32,
        )
        own.append(jnp.where(cols < lens[base + p], raw, NEG_FILL))
    own = jnp.concatenate(own, axis=0)
    row_max = jnp.max(jnp.maximum(jnp.maximum(top, fresh), own), axis=1, keepdims=True)
    scale = LOG2E / math.sqrt(HEAD_DIM)
    exps = jnp.exp2((own - row_max) * scale)
    fresh_exps = jnp.exp2((fresh - row_max) * scale)
    total = exps + fresh_exps
    probs = exps.astype(jnp.bfloat16)
    mixed = []
    for p in range(per_dev):
        mixed.append(
            jnp.dot(
                probs[p * part : (p + 1) * part], cache[p, :, HEAD_DIM : 2 * HEAD_DIM],
                preferred_element_type=jnp.float32,
            )
        )
    mixed = jnp.concatenate(mixed, axis=0) + jnp.dot(
        fresh_exps.astype(bf16), new_vals, preferred_element_type=f32
    )
    for item in load_vals:
        item.wait()
    block = n_rows // 2
    totals, mixes = [], []
    for r in range(2):
        lines = slice(r * block, (r + 1) * block)
        part_total, part_mixed = total[lines], mixed[lines]
        for c in range(prompt_len // chunk):
            exps = jnp.exp2((scores[lines, c * chunk : (c + 1) * chunk] - row_max[lines]) * scale)
            for i in range(chunk // 128):
                part_total = part_total + exps[:, i * 128 : (i + 1) * 128]
            part_mixed = part_mixed + jnp.dot(
                exps.astype(bf16), valv[c * chunk : (c + 1) * chunk, :], preferred_element_type=f32
            )
        totals.append(part_total)
        mixes.append(part_mixed)
    total, mixed = jnp.concatenate(totals, axis=0), jnp.concatenate(mixes, axis=0)
    row_sum = jnp.sum(total, axis=1, keepdims=True)
    mixed = mixed / row_sum
    load_tv.wait()
    weighted = mixed.reshape(2 * per_dev, group, HEAD_DIM) * tvv[...][None]
    pair_rows = jnp.sum(weighted, axis=1) + bias_rows[...]
    pair_col = jnp.sum(pair_rows, axis=1, keepdims=True)
    message = jnp.sum(placed * pair_col, axis=0, keepdims=True) + prior_row
    plane_rows[me] = message

    pl.semaphore_wait(
        barrier, n_plane - 1 + my_z + jnp.where(dom > 0, 1, 0)
    )

    n_x = n_tp // 2
    my_x, core = tp // 2, lax.rem(tp, 2)
    farthest = lambda n: sorted(range(n), key=lambda d: -min(d, n - d))
    targets = []
    for target_core in range(2):
        for dx in farthest(n_x):
            for dy in farthest(Y_DIM):
                if dx or dy:
                    targets.append((dx, dy, target_core))
    targets.append((0, 0, 1 - core))

    def plane_send_to(j):
        dx, dy, target_core = targets[j]
        x = lax.rem(my_x + dx, n_x)
        y = lax.rem(my_y + dy, Y_DIM)
        return pltpu.make_async_remote_copy(
            src_ref=plane_rows.at[me],
            dst_ref=plane_rows.at[me],
            send_sem=plane_send.at[j],
            recv_sem=plane_recv.at[me],
            device_id=device(my_z * Y_DIM + y, x * 2 + target_core),
            device_id_type=MESH,
        )

    plane_sends = [plane_send_to(j) for j in range(len(targets))]
    for item in plane_sends:
        item.start()

    @pl.when(dom > 0)
    def _():
        signal(next_sem, device(dom - 1, tp))

    rows = lax.broadcasted_iota(jnp.int32, (gen, 2 * HEAD_DIM), 0).astype(f32).astype(bf16)
    for p in range(per_dev):
        start = lens[base + p].astype(f32)
        at_first = jnp.full((gen, 2 * HEAD_DIM), start, f32).astype(bf16)
        at_second = jnp.full((gen, 2 * HEAD_DIM), start + 1.0, f32).astype(bf16)
        first = jnp.broadcast_to(newv[0, pl.ds(p, 1), :], (gen, 2 * HEAD_DIM))
        second = jnp.broadcast_to(newv[1, pl.ds(p, 1), :], (gen, 2 * HEAD_DIM))
        later = jnp.where(rows == at_second, second, jnp.zeros_like(second))
        cache[p] = jnp.where(
            rows < at_first, cache[p], jnp.where(rows == at_first, first, later)
        )

    load_anc.wait()
    for slot, offset in enumerate(OFFSETS):
        target = jnp.clip(dom + offset, 0, n_dom - 1) * per_dev
        low, high = per_dev - 1, 0
        for i in range(per_dev):
            spot = anc[target + i] - base
            mine = jnp.logical_and(spot >= 0, spot < per_dev)
            low = jnp.minimum(low, jnp.where(mine, spot, per_dev - 1))
            high = jnp.maximum(high, jnp.where(mine, spot, 0))
        picked[slot, 0] = cache[low]
        picked[slot, 1] = cache[high]

    def plane_wait(dx, dy, source_core):
        x = lax.rem(my_x + dx, n_x)
        y = lax.rem(my_y + dy, Y_DIM)
        slot = (x * 2 + source_core) * Y_DIM + y
        pltpu.make_async_remote_copy(
            src_ref=plane_rows.at[slot],
            dst_ref=plane_rows.at[slot],
            send_sem=plane_send.at[0],
            recv_sem=plane_recv.at[slot],
            device_id=plane_device(slot),
            device_id_type=MESH,
        ).wait_recv()

    for target in reversed(targets):
        plane_wait(*target)

    z_rows[my_z] = jnp.sum(plane_rows[...], axis=0)

    def z_copy(dst, z):
        return pltpu.make_async_remote_copy(
            src_ref=z_rows.at[my_z],
            dst_ref=z_rows.at[dst],
            send_sem=z_send.at[z],
            recv_sem=z_recv.at[dst],
            device_id=z_device(z),
            device_id_type=MESH,
        )

    def z_start(z, carry):
        z_copy(my_z, z).start()
        return carry

    lax.fori_loop(0, my_z, z_start, 0)

    def greet_below(z, carry):
        signal(above_sem, z_device(z))
        return carry

    lax.fori_loop(0, my_z, greet_below, 0)

    def hop(src, dst, i, shift):
        return pltpu.make_async_remote_copy(
            src_ref=src,
            dst_ref=dst,
            send_sem=hop_send.at[i],
            recv_sem=hop_recv.at[i],
            device_id=device(jnp.clip(dom + shift, 0, n_dom - 1), tp),
            device_id_type=MESH,
        )

    far = n_dom - 1
    inner = jnp.logical_and(dom > 0, dom < far)
    hops = [
        (hop(picked.at[0], relay.at[0], 0, 1), dom < far - 1, inner),
        (hop(picked.at[2], relay.at[1], 1, -1), dom > 1, inner),
        (hop(picked.at[1], landed.at[1], 2, 1), dom < far, dom > 0),
        (hop(picked.at[3], landed.at[3], 3, -1), dom > 0, dom < far),
        (hop(relay.at[0], landed.at[0], 4, 1), inner, dom > 1),
        (hop(relay.at[1], landed.at[2], 5, -1), inner, dom < far - 1),
    ]

    def start_hop(i):
        pl.when(hops[i][1])(hops[i][0].start)

    def receive_hop(i):
        pl.when(hops[i][2])(hops[i][0].wait_recv)

    @pl.when(dom < far)
    def _():
        pl.semaphore_wait(next_sem, 1)

    for i in range(4):
        start_hop(i)

    receive_hop(0)
    start_hop(4)
    receive_hop(1)
    start_hop(5)

    @pl.when(my_z < n_z - 1)
    def _():
        pl.semaphore_wait(above_sem, n_z - 1 - my_z)

    lax.fori_loop(my_z + 1, n_z, z_start, 0)

    own_sum = plane_rows[my_y]
    for t in range(1, n_tp):
        own_sum = own_sum + plane_rows[t * Y_DIM + my_y]
    twist_out[0:1, :] = own_sum[:, 0:per_dev]
    twist_out[1:2, :] = pltpu.roll(own_sum, 128 - per_dev, 1)[:, 0:per_dev]
    own_weight = own_sum
    for y in range(Y_DIM):
        moved = pltpu.roll(own_sum, 128 - 4 * per_dev - y * per_dev, 1)
        own_weight = jnp.where(my_y == y, moved, own_weight)

    for i in range(2, 6):
        receive_hop(i)
    firsts = []
    for offset in OFFSETS:
        low = per_dev - 1
        for i in range(per_dev):
            spot = anc[base + i] - (base - offset * per_dev)
            theirs = jnp.logical_and(spot >= 0, spot < per_dev)
            low = jnp.minimum(low, jnp.where(theirs, spot, per_dev - 1))
        firsts.append(low)
    new_lens = jnp.zeros((1, 128), jnp.int32)
    for p in range(per_dev):
        new_lens = jnp.where(lanes == p, lens[anc[base + p]] + 2, new_lens)
        spot = anc[base + p] - base
        home = jnp.logical_and(spot >= 0, spot < per_dev)
        home_spot = jnp.clip(spot, 0, per_dev - 1)
        place = 0
        for slot, offset in enumerate(OFFSETS):
            there = spot + offset * per_dev
            theirs = jnp.logical_and(there >= 0, there < per_dev)
            second = jnp.where(there == firsts[slot], 0, 1)
            place = jnp.where(theirs, 2 * slot + second, place)
        moved = landed[place // 2, lax.rem(place, 2)]
        cache_out[p] = jnp.where(home, cache[home_spot], moved)
    len_out[...] = new_lens[:, 0:per_dev]

    for k in range(1, n_z):
        z = lax.rem(my_z + k, n_z)
        z_copy(z, z).wait_recv()
    all_weights = jnp.where((lanes >= 4 * per_dev)[None], z_rows[...], NEG_FILL)
    largest = jnp.max(jnp.max(all_weights, axis=0), axis=1, keepdims=True)
    exp_total = jnp.sum(jnp.sum(jnp.exp(all_weights - largest[None]), axis=0), axis=1, keepdims=True)
    normalized = own_weight - (largest + jnp.log(exp_total))
    norm_out[...] = normalized[:, 0:per_dev]

    for item, sends, _ in hops:
        pl.when(sends)(item.wait_send)
    for item in plane_sends:
        item.wait_send()
    for k in range(1, n_z):
        z = lax.rem(my_z + k, n_z)
        z_copy(z, z).wait_send()


def finish(*refs):
    count = (len(refs) - 1) // 2
    copies = [
        pltpu.make_async_copy(refs[i], refs[count + i], refs[-1].at[i]) for i in range(count)
    ]
    for item in copies:
        item.start()
    for item in copies:
        item.wait()


def local(
    n_dom,
    n_tp,
    queries,
    new_kv,
    gen_cache,
    prompt_kv,
    lengths,
    ancestors,
    tokens,
    twist_vector,
    twist_bias,
    prior_weights,
):
    per_dev, gen, width = gen_cache.shape
    prompt_len = prompt_kv.shape[0]
    group = queries.shape[2] // HEAD_DIM
    n_rows = 2 * group * per_dev
    n_z = n_dom // Y_DIM
    n_plane = n_tp * Y_DIM
    bias_table = twist_bias.reshape(-1, 128)
    bias_part = -(-bias_table.shape[0] // (8 * n_tp)) * 8
    any_space = pl.BlockSpec(memory_space=pl.ANY)
    vmem = pl.BlockSpec(memory_space=pltpu.VMEM)
    f32, bf16, i32 = jnp.float32, jnp.bfloat16, jnp.int32
    dma = pltpu.SemaphoreType.DMA
    shapes = (((2, per_dev), f32), ((1, per_dev), f32), (gen_cache.shape, bf16), ((1, per_dev), i32))
    results = pl.pallas_call(
        functools.partial(kernel, (n_dom, n_tp, per_dev, gen, prompt_len, group)),
        out_shape=tuple(pltpu.VMEM(*shape) for shape in shapes),
        in_specs=[any_space] * 10,
        out_specs=(vmem,) * 4,
        scratch_shapes=[
            pltpu.SMEM(ancestors.shape, i32),
            pltpu.SMEM(lengths.shape, i32),
            pltpu.SMEM(tokens.shape, i32),
            pltpu.SMEM(prior_weights.shape, f32),
            pltpu.VMEM(queries.shape, bf16),
            pltpu.VMEM(new_kv.shape, bf16),
            pltpu.VMEM(gen_cache.shape, bf16),
            pltpu.VMEM((prompt_len, HEAD_DIM), bf16),
            pltpu.VMEM((prompt_len, HEAD_DIM), bf16),
            pltpu.VMEM((group, HEAD_DIM), f32),
            pltpu.VMEM((bias_part, 128), f32),
            pltpu.VMEM((n_rows, prompt_len), f32),
            pltpu.VMEM((4, 2, gen, width), bf16),
            pltpu.VMEM((2, 2, gen, width), bf16),
            pltpu.VMEM((4, 2, gen, width), bf16),
            pltpu.VMEM((2 * per_dev, 128), f32),
            pltpu.VMEM((n_plane, 1, 128), f32),
            pltpu.VMEM((n_z, 1, 128), f32),
            dma((5,)),
            dma((4,)),
            dma((PARTS,)),
            dma((PARTS,)),
            dma((6,)),
            dma((6,)),
            dma((n_plane,)),
            dma((n_plane,)),
            dma((n_z,)),
            dma((n_z,)),
            pltpu.SemaphoreType.REGULAR,
            pltpu.SemaphoreType.REGULAR,
        ],
        compiler_params=pltpu.CompilerParams(collective_id=0, has_side_effects=True),
        name="smc_step",
    )(
        ancestors,
        lengths,
        tokens,
        prior_weights,
        queries,
        new_kv,
        gen_cache,
        prompt_kv,
        twist_vector.reshape(group, HEAD_DIM),
        bias_table,
    )
    held = [pltpu.with_memory_space_constraint(x, pltpu.VMEM) for x in results]
    twist, normalized, resampled, new_lengths = pl.pallas_call(
        finish,
        out_shape=tuple(jax.ShapeDtypeStruct(*shape) for shape in shapes),
        in_specs=[any_space] * 4,
        out_specs=(any_space,) * 4,
        scratch_shapes=[dma((4,))],
        compiler_params=pltpu.CompilerParams(vmem_limit_bytes=4 << 20),
        name="finish",
    )(*held)
    return twist, normalized.reshape(per_dev), resampled, new_lengths.reshape(per_dev)


def solution(mesh):
    in_specs = (
        P(None, "dom", "tp"),
        P(None, "dom", "tp"),
        P("dom", None, "tp"),
        P(None, "tp"),
        P(),
        P(),
        P(None, "dom"),
        P("tp"),
        P(),
        P("dom"),
    )
    out_specs = (P(None, "dom"), P("dom"), P("dom", None, "tp"), P("dom"))
    return jax.shard_map(
        functools.partial(local, mesh.shape["dom"], mesh.shape["tp"]),
        mesh=mesh,
        in_specs=in_specs,
        out_specs=out_specs,
        check_vma=False,
    )
```

```python
import functools
import math

import jax
import jax.numpy as jnp
from jax import lax
from jax.experimental import pallas as pl
from jax.experimental.pallas import tpu as pltpu
from jax.sharding import PartitionSpec as P

HEAD_DIM = 128
Y_DIM = 4
NEG_FILL = -1e30
MESH = pl.DeviceIdType.MESH
LOG2E = 1.4426950408889634
PARTS = 2
OFFSETS = (2, 1, -2, -1)


def kernel(
    sizes,
    anc_hbm,
    lens_hbm,
    toks_hbm,
    prior_hbm,
    q_hbm,
    new_hbm,
    gen_hbm,
    prompt_hbm,
    tv_hbm,
    bias_hbm,
    twist_out,
    norm_out,
    cache_out,
    len_out,
    anc,
    lens,
    toks,
    prior,
    qv,
    newv,
    cache,
    keyv,
    valv,
    tvv,
    biasv,
    scores,
    picked,
    relay,
    landed,
    bias_rows,
    plane_rows,
    z_rows,
    small_sems,
    in_sems,
    key_sems,
    hop_send,
    hop_recv,
    plane_send,
    plane_recv,
    z_send,
    z_recv,
    next_sem,
    above_sem,
):
    n_dom, n_tp, per_dev, gen, prompt_len, group = sizes
    f32, bf16 = jnp.float32, jnp.bfloat16
    n_z = n_dom // Y_DIM
    n_plane = n_tp * Y_DIM
    dom = lax.axis_index("dom")
    tp = lax.axis_index("tp")
    my_y = lax.rem(dom, Y_DIM)
    my_z = dom // Y_DIM
    base = dom * per_dev
    bias_len = bias_hbm.shape[0]
    bias_part = biasv.shape[0]
    bias_last = bias_len - (n_tp - 1) * bias_part
    key_part = prompt_len // PARTS

    def device(d, t):
        return {"dom": d, "tp": t}

    def signal(sem, target):
        pl.semaphore_signal(sem, inc=1, device_id=target, device_id_type=MESH)

    def z_device(z):
        return device(z * Y_DIM + my_y, tp)

    me = tp * Y_DIM + my_y

    def plane_slot(k):
        return lax.rem(me + k, n_plane)

    def plane_device(slot):
        return device(my_z * Y_DIM + lax.rem(slot, Y_DIM), slot // Y_DIM)

    copy = pltpu.make_async_copy
    load_q = copy(q_hbm, qv, in_sems.at[0])
    load_gen = copy(gen_hbm, cache, in_sems.at[1])
    load_new = copy(new_hbm, newv, in_sems.at[2])
    load_tv = copy(tv_hbm, tvv, in_sems.at[3])
    load_keys = [
        copy(
            prompt_hbm.at[c * key_part : (c + 1) * key_part, 0:HEAD_DIM],
            keyv.at[c * key_part : (c + 1) * key_part],
            key_sems.at[c],
        )
        for c in range(PARTS)
    ]
    load_vals = copy(prompt_hbm.at[:, HEAD_DIM : 2 * HEAD_DIM], valv, in_sems.at[4])
    load_anc = copy(anc_hbm, anc, small_sems.at[0])
    load_lens = copy(lens_hbm, lens, small_sems.at[1])
    load_toks = copy(toks_hbm, toks, small_sems.at[2])
    load_prior = copy(prior_hbm, prior, small_sems.at[3])
    bias_most = copy(
        bias_hbm.at[pl.ds(pl.multiple_of(tp * bias_part, 8), bias_part)], biasv, small_sems.at[4]
    )
    bias_rest = copy(
        bias_hbm.at[bias_len - bias_last : bias_len], biasv.at[0:bias_last], small_sems.at[4]
    )
    load_toks.start()
    load_prior.start()
    load_lens.start()
    load_q.start()

    @pl.when(tp < n_tp - 1)
    def _():
        bias_most.start()

    @pl.when(tp == n_tp - 1)
    def _():
        bias_rest.start()

    for item in load_keys:
        item.start()
    load_new.start()

    barrier = pltpu.get_barrier_semaphore()

    def greet_plane(k, carry):
        signal(barrier, plane_device(plane_slot(k)))
        return carry

    def greet_above(z, carry):
        signal(barrier, z_device(z))
        return carry

    lax.fori_loop(1, n_plane, greet_plane, 0)
    lax.fori_loop(my_z + 1, n_z, greet_above, 0)

    @pl.when(dom < n_dom - 1)
    def _():
        signal(barrier, device(dom + 1, tp))

    load_gen.start()
    load_vals.start()
    load_tv.start()
    load_anc.start()

    n_rows = 2 * group * per_dev
    to_row = lax.broadcasted_iota(jnp.int32, (n_rows, n_rows), 0)
    from_row = lax.broadcasted_iota(jnp.int32, (n_rows, n_rows), 1)
    wanted = lax.rem(to_row, 2 * group) * per_dev + to_row // (2 * group)
    order = jnp.where(from_row == wanted, 1.0, 0.0).astype(jnp.bfloat16)
    load_q.wait()
    tiles = [qv[t, :, h * HEAD_DIM : (h + 1) * HEAD_DIM] for t in range(2) for h in range(group)]
    stacked = jnp.concatenate(tiles, axis=0)
    query = jnp.dot(order, stacked, preferred_element_type=jnp.float32).astype(jnp.bfloat16)

    load_toks.wait()

    @pl.when(tp < n_tp - 1)
    def _():
        bias_most.wait()

    @pl.when(tp == n_tp - 1)
    def _():
        bias_rest.wait()

    lanes = lax.broadcasted_iota(jnp.int32, (1, 128), 1)
    bias_start = tp * (bias_part * 128)
    for p in range(per_dev):
        for t in range(2):
            local_token = toks[t, p] - bias_start
            spot = jnp.clip(lax.shift_right_arithmetic(local_token, 7), 0, bias_part - 1)
            row = biasv[pl.ds(spot, 1), :]
            bias_rows[p * 2 + t : p * 2 + t + 1, :] = jnp.where(
                lanes == local_token - spot * 128, row, 0.0
            )

    first_tp = jnp.where(tp == 0, 1.0, 0.0)
    load_prior.wait()
    weight_lane = 2 * 2 * per_dev + per_dev * my_y
    prior_row = jnp.zeros((1, 128), f32)
    for p in range(per_dev):
        prior_row = jnp.where(lanes == weight_lane + p, prior[p] * first_tp, prior_row)
    pair_ids = lax.broadcasted_iota(jnp.int32, (2 * per_dev, 128), 0)
    lane_ids = lax.broadcasted_iota(jnp.int32, (2 * per_dev, 128), 1)
    pair_step = lax.rem(pair_ids, 2)
    at_twist = lane_ids == pair_step * per_dev + pair_ids // 2
    at_weight = lane_ids == weight_lane + pair_ids // 2
    placed = jnp.where(
        at_twist, 1.0, jnp.where(at_weight, (2 * pair_step - 1).astype(f32), 0.0)
    )

    nt = (((1,), (1,)), ((), ()))
    part = 2 * group
    chunk = 512
    top = None
    for c in range(prompt_len // chunk):
        if c * chunk % key_part == 0:
            load_keys[c * chunk // key_part].wait()
        raw = lax.dot_general(
            query, keyv[c * chunk : (c + 1) * chunk, :], nt, preferred_element_type=jnp.float32
        )
        scores[:, c * chunk : (c + 1) * chunk] = raw
        for i in range(chunk // 128):
            piece = raw[:, i * 128 : (i + 1) * 128]
            top = piece if top is None else jnp.maximum(top, piece)

    load_lens.wait()
    load_new.wait()
    load_gen.wait()
    load_vals.wait()
    load_tv.wait()
    filler = jnp.zeros((128 - 2 * per_dev, HEAD_DIM), bf16)
    new_keys = jnp.concatenate([newv[0, :, 0:HEAD_DIM], newv[1, :, 0:HEAD_DIM], filler], axis=0)
    new_vals = jnp.concatenate(
        [newv[0, :, HEAD_DIM : 2 * HEAD_DIM], newv[1, :, HEAD_DIM : 2 * HEAD_DIM], filler], axis=0
    )
    new_row = lax.broadcasted_iota(jnp.int32, (n_rows, 128), 0)
    new_col = lax.broadcasted_iota(jnp.int32, (n_rows, 128), 1)
    shown = jnp.logical_and(
        lax.rem(new_col, per_dev) == new_row // (2 * group),
        new_col // per_dev <= lax.rem(new_row // group, 2),
    )
    fresh = lax.dot_general(query, new_keys, nt, preferred_element_type=f32)
    fresh = jnp.where(shown, fresh, NEG_FILL)
    own = []
    cols = lax.broadcasted_iota(jnp.int32, (part, gen), 1)
    for p in range(per_dev):
        raw = lax.dot_general(
            query[p * part : (p + 1) * part], cache[p, :, 0:HEAD_DIM], nt,
            preferred_element_type=jnp.float32,
        )
        own.append(jnp.where(cols < lens[base + p], raw, NEG_FILL))
    own = jnp.concatenate(own, axis=0)
    row_max = jnp.max(jnp.maximum(jnp.maximum(top, fresh), own), axis=1, keepdims=True)
    scale = LOG2E / math.sqrt(HEAD_DIM)
    exps = jnp.exp2((own - row_max) * scale)
    fresh_exps = jnp.exp2((fresh - row_max) * scale)
    total = exps + fresh_exps
    probs = exps.astype(jnp.bfloat16)
    mixed = []
    for p in range(per_dev):
        mixed.append(
            jnp.dot(
                probs[p * part : (p + 1) * part], cache[p, :, HEAD_DIM : 2 * HEAD_DIM],
                preferred_element_type=jnp.float32,
            )
        )
    mixed = jnp.concatenate(mixed, axis=0) + jnp.dot(
        fresh_exps.astype(bf16), new_vals, preferred_element_type=f32
    )
    block = n_rows // 2
    totals, mixes = [], []
    for r in range(2):
        lines = slice(r * block, (r + 1) * block)
        part_total, part_mixed = total[lines], mixed[lines]
        for c in range(prompt_len // chunk):
            exps = jnp.exp2((scores[lines, c * chunk : (c + 1) * chunk] - row_max[lines]) * scale)
            for i in range(chunk // 128):
                part_total = part_total + exps[:, i * 128 : (i + 1) * 128]
            part_mixed = part_mixed + jnp.dot(
                exps.astype(bf16), valv[c * chunk : (c + 1) * chunk, :], preferred_element_type=f32
            )
        totals.append(part_total)
        mixes.append(part_mixed)
    total, mixed = jnp.concatenate(totals, axis=0), jnp.concatenate(mixes, axis=0)
    row_sum = jnp.sum(total, axis=1, keepdims=True)
    mixed = mixed / row_sum
    weighted = mixed.reshape(2 * per_dev, group, HEAD_DIM) * tvv[...][None]
    pair_rows = jnp.sum(weighted, axis=1) + bias_rows[...]
    pair_col = jnp.sum(pair_rows, axis=1, keepdims=True)
    message = jnp.sum(placed * pair_col, axis=0, keepdims=True) + prior_row
    plane_rows[me] = message

    pl.semaphore_wait(
        barrier, n_plane - 1 + my_z + jnp.where(dom > 0, 1, 0)
    )

    n_x = n_tp // 2
    my_x, core = tp // 2, lax.rem(tp, 2)
    farthest = lambda n: sorted(range(n), key=lambda d: -min(d, n - d))
    targets = []
    for target_core in range(2):
        for dx in farthest(n_x):
            for dy in farthest(Y_DIM):
                if dx or dy:
                    targets.append((dx, dy, target_core))
    targets.append((0, 0, 1 - core))

    def plane_send_to(j):
        dx, dy, target_core = targets[j]
        x = lax.rem(my_x + dx, n_x)
        y = lax.rem(my_y + dy, Y_DIM)
        return pltpu.make_async_remote_copy(
            src_ref=plane_rows.at[me],
            dst_ref=plane_rows.at[me],
            send_sem=plane_send,
            recv_sem=plane_recv,
            device_id=device(my_z * Y_DIM + y, x * 2 + target_core),
            device_id_type=MESH,
        )

    plane_sends = [plane_send_to(j) for j in range(len(targets))]
    for item in plane_sends:
        item.start()

    @pl.when(dom > 0)
    def _():
        signal(next_sem, device(dom - 1, tp))

    rows = lax.broadcasted_iota(jnp.int32, (gen, 2 * HEAD_DIM), 0).astype(f32).astype(bf16)
    for p in range(per_dev):
        start = lens[base + p].astype(f32)
        at_first = jnp.full((gen, 2 * HEAD_DIM), start, f32).astype(bf16)
        at_second = jnp.full((gen, 2 * HEAD_DIM), start + 1.0, f32).astype(bf16)
        first = jnp.broadcast_to(newv[0, pl.ds(p, 1), :], (gen, 2 * HEAD_DIM))
        second = jnp.broadcast_to(newv[1, pl.ds(p, 1), :], (gen, 2 * HEAD_DIM))
        later = jnp.where(rows == at_second, second, jnp.zeros_like(second))
        cache[p] = jnp.where(
            rows < at_first, cache[p], jnp.where(rows == at_first, first, later)
        )

    load_anc.wait()
    for slot, offset in enumerate(OFFSETS):
        target = jnp.clip(dom + offset, 0, n_dom - 1) * per_dev
        low, high = per_dev - 1, 0
        for i in range(per_dev):
            spot = anc[target + i] - base
            mine = jnp.logical_and(spot >= 0, spot < per_dev)
            low = jnp.minimum(low, jnp.where(mine, spot, per_dev - 1))
            high = jnp.maximum(high, jnp.where(mine, spot, 0))
        picked[slot, 0] = cache[low]
        picked[slot, 1] = cache[high]

    all_sent = pltpu.make_async_remote_copy(
        src_ref=plane_rows.at[0 : n_plane - 1],
        dst_ref=plane_rows.at[0 : n_plane - 1],
        send_sem=plane_send,
        recv_sem=plane_recv,
        device_id=device(dom, 0),
        device_id_type=MESH,
    )
    all_sent.wait_recv()

    sums = [plane_rows[slot] for slot in range(n_plane)]
    while len(sums) > 1:
        sums = [a + b for a, b in zip(sums[::2], sums[1::2])]
    z_rows[my_z] = sums[0]

    def z_copy(dst, z):
        return pltpu.make_async_remote_copy(
            src_ref=z_rows.at[my_z],
            dst_ref=z_rows.at[dst],
            send_sem=z_send,
            recv_sem=z_recv,
            device_id=z_device(z),
            device_id_type=MESH,
        )

    def z_start(z, carry):
        z_copy(my_z, z).start()
        return carry

    lax.fori_loop(0, my_z, z_start, 0)

    def greet_below(z, carry):
        signal(above_sem, z_device(z))
        return carry

    lax.fori_loop(0, my_z, greet_below, 0)

    def hop(src, dst, i, shift):
        return pltpu.make_async_remote_copy(
            src_ref=src,
            dst_ref=dst,
            send_sem=hop_send.at[i],
            recv_sem=hop_recv.at[i],
            device_id=device(jnp.clip(dom + shift, 0, n_dom - 1), tp),
            device_id_type=MESH,
        )

    far = n_dom - 1
    inner = jnp.logical_and(dom > 0, dom < far)
    hops = [
        (hop(picked.at[0], relay.at[0], 0, 1), dom < far - 1, inner),
        (hop(picked.at[2], relay.at[1], 1, -1), dom > 1, inner),
        (hop(picked.at[1], landed.at[1], 2, 1), dom < far, dom > 0),
        (hop(picked.at[3], landed.at[3], 3, -1), dom > 0, dom < far),
        (hop(relay.at[0], landed.at[0], 4, 1), inner, dom > 1),
        (hop(relay.at[1], landed.at[2], 5, -1), inner, dom < far - 1),
    ]

    def start_hop(i):
        pl.when(hops[i][1])(hops[i][0].start)

    def receive_hop(i):
        pl.when(hops[i][2])(hops[i][0].wait_recv)

    @pl.when(dom < far)
    def _():
        pl.semaphore_wait(next_sem, 1)

    for i in range(4):
        start_hop(i)

    receive_hop(0)
    start_hop(4)
    receive_hop(1)
    start_hop(5)

    @pl.when(my_z < n_z - 1)
    def _():
        pl.semaphore_wait(above_sem, n_z - 1 - my_z)

    lax.fori_loop(my_z + 1, n_z, z_start, 0)

    own_sum = plane_rows[my_y]
    for t in range(1, n_tp):
        own_sum = own_sum + plane_rows[t * Y_DIM + my_y]
    twist_out[0:1, :] = own_sum[:, 0:per_dev]
    twist_out[1:2, :] = pltpu.roll(own_sum, 128 - per_dev, 1)[:, 0:per_dev]
    own_weight = own_sum
    for y in range(Y_DIM):
        moved = pltpu.roll(own_sum, 128 - 4 * per_dev - y * per_dev, 1)
        own_weight = jnp.where(my_y == y, moved, own_weight)

    for i in range(2, 6):
        receive_hop(i)
    firsts = []
    for offset in OFFSETS:
        low = per_dev - 1
        for i in range(per_dev):
            spot = anc[base + i] - (base - offset * per_dev)
            theirs = jnp.logical_and(spot >= 0, spot < per_dev)
            low = jnp.minimum(low, jnp.where(theirs, spot, per_dev - 1))
        firsts.append(low)
    new_lens = jnp.zeros((1, 128), jnp.int32)
    for p in range(per_dev):
        new_lens = jnp.where(lanes == p, lens[anc[base + p]] + 2, new_lens)
        spot = anc[base + p] - base
        home = jnp.logical_and(spot >= 0, spot < per_dev)
        home_spot = jnp.clip(spot, 0, per_dev - 1)
        place = 0
        for slot, offset in enumerate(OFFSETS):
            there = spot + offset * per_dev
            theirs = jnp.logical_and(there >= 0, there < per_dev)
            second = jnp.where(there == firsts[slot], 0, 1)
            place = jnp.where(theirs, 2 * slot + second, place)
        moved = landed[place // 2, lax.rem(place, 2)]
        cache_out[p] = jnp.where(home, cache[home_spot], moved)
    len_out[...] = new_lens[:, 0:per_dev]

    for item, sends, _ in hops:
        pl.when(sends)(item.wait_send)
    all_sent.wait_send()
    z_all = pltpu.make_async_remote_copy(
        src_ref=z_rows.at[0 : n_z - 1],
        dst_ref=z_rows.at[0 : n_z - 1],
        send_sem=z_send,
        recv_sem=z_recv,
        device_id=device(dom, 0),
        device_id_type=MESH,
    )
    z_all.wait_send()
    z_all.wait_recv()
    all_weights = jnp.where((lanes >= 4 * per_dev)[None], z_rows[...], NEG_FILL)
    largest = jnp.max(jnp.max(all_weights, axis=0), axis=1, keepdims=True)
    exp_total = jnp.sum(jnp.sum(jnp.exp(all_weights - largest[None]), axis=0), axis=1, keepdims=True)
    normalized = own_weight - (largest + jnp.log(exp_total))
    norm_out[...] = normalized[:, 0:per_dev]


def finish(*refs):
    count = (len(refs) - 1) // 2
    copies = [
        pltpu.make_async_copy(refs[i], refs[count + i], refs[-1].at[i]) for i in range(count)
    ]
    for item in copies:
        item.start()
    for item in copies:
        item.wait()


def local(
    n_dom,
    n_tp,
    queries,
    new_kv,
    gen_cache,
    prompt_kv,
    lengths,
    ancestors,
    tokens,
    twist_vector,
    twist_bias,
    prior_weights,
):
    per_dev, gen, width = gen_cache.shape
    prompt_len = prompt_kv.shape[0]
    group = queries.shape[2] // HEAD_DIM
    n_rows = 2 * group * per_dev
    n_z = n_dom // Y_DIM
    n_plane = n_tp * Y_DIM
    bias_table = twist_bias.reshape(-1, 128)
    bias_part = -(-bias_table.shape[0] // (8 * n_tp)) * 8
    any_space = pl.BlockSpec(memory_space=pl.ANY)
    vmem = pl.BlockSpec(memory_space=pltpu.VMEM)
    f32, bf16, i32 = jnp.float32, jnp.bfloat16, jnp.int32
    dma = pltpu.SemaphoreType.DMA
    shapes = (((2, per_dev), f32), ((1, per_dev), f32), (gen_cache.shape, bf16), ((1, per_dev), i32))
    results = pl.pallas_call(
        functools.partial(kernel, (n_dom, n_tp, per_dev, gen, prompt_len, group)),
        out_shape=tuple(pltpu.VMEM(*shape) for shape in shapes),
        in_specs=[any_space] * 10,
        out_specs=(vmem,) * 4,
        scratch_shapes=[
            pltpu.SMEM(ancestors.shape, i32),
            pltpu.SMEM(lengths.shape, i32),
            pltpu.SMEM(tokens.shape, i32),
            pltpu.SMEM(prior_weights.shape, f32),
            pltpu.VMEM(queries.shape, bf16),
            pltpu.VMEM(new_kv.shape, bf16),
            pltpu.VMEM(gen_cache.shape, bf16),
            pltpu.VMEM((prompt_len, HEAD_DIM), bf16),
            pltpu.VMEM((prompt_len, HEAD_DIM), bf16),
            pltpu.VMEM((group, HEAD_DIM), f32),
            pltpu.VMEM((bias_part, 128), f32),
            pltpu.VMEM((n_rows, prompt_len), f32),
            pltpu.VMEM((4, 2, gen, width), bf16),
            pltpu.VMEM((2, 2, gen, width), bf16),
            pltpu.VMEM((4, 2, gen, width), bf16),
            pltpu.VMEM((2 * per_dev, 128), f32),
            pltpu.VMEM((n_plane, 1, 128), f32),
            pltpu.VMEM((n_z, 1, 128), f32),
            dma((5,)),
            dma((5,)),
            dma((PARTS,)),
            dma((6,)),
            dma((6,)),
            dma,
            dma,
            dma,
            dma,
            pltpu.SemaphoreType.REGULAR,
            pltpu.SemaphoreType.REGULAR,
        ],
        compiler_params=pltpu.CompilerParams(collective_id=0, has_side_effects=True),
        name="smc_step",
    )(
        ancestors,
        lengths,
        tokens,
        prior_weights,
        queries,
        new_kv,
        gen_cache,
        prompt_kv,
        twist_vector.reshape(group, HEAD_DIM),
        bias_table,
    )
    held = [pltpu.with_memory_space_constraint(x, pltpu.VMEM) for x in results]
    twist, normalized, resampled, new_lengths = pl.pallas_call(
        finish,
        out_shape=tuple(jax.ShapeDtypeStruct(*shape) for shape in shapes),
        in_specs=[any_space] * 4,
        out_specs=(any_space,) * 4,
        scratch_shapes=[dma((4,))],
        compiler_params=pltpu.CompilerParams(vmem_limit_bytes=4 << 20),
        name="finish",
    )(*held)
    return twist, normalized.reshape(per_dev), resampled, new_lengths.reshape(per_dev)


def solution(mesh):
    in_specs = (
        P(None, "dom", "tp"),
        P(None, "dom", "tp"),
        P("dom", None, "tp"),
        P(None, "tp"),
        P(),
        P(),
        P(None, "dom"),
        P("tp"),
        P(),
        P("dom"),
    )
    out_specs = (P(None, "dom"), P("dom"), P("dom", None, "tp"), P("dom"))
    return jax.shard_map(
        functools.partial(local, mesh.shape["dom"], mesh.shape["tp"]),
        mesh=mesh,
        in_specs=in_specs,
        out_specs=out_specs,
        check_vma=False,
    )
```

```python
import functools
import math

import jax
import jax.numpy as jnp
from jax import lax
from jax.experimental import pallas as pl
from jax.experimental.pallas import tpu as pltpu
from jax.sharding import PartitionSpec as P

HEAD_DIM = 128
Y_DIM = 4
NEG_FILL = -1e30
MESH = pl.DeviceIdType.MESH
LOG2E = 1.4426950408889634
PARTS = 2
OFFSETS = (2, 1, -2, -1)


def kernel(
    sizes,
    anc_hbm,
    lens_hbm,
    toks_hbm,
    prior_hbm,
    q_hbm,
    new_hbm,
    gen_hbm,
    prompt_hbm,
    tv_hbm,
    bias_hbm,
    twist_out,
    norm_out,
    cache_out,
    len_out,
    anc,
    lens,
    toks,
    prior,
    qv,
    newv,
    cache,
    keyv,
    valv,
    tvv,
    biasv,
    scores,
    picked,
    relay,
    landed,
    bias_rows,
    plane_rows,
    z_rows,
    small_sems,
    in_sems,
    key_sems,
    hop_send,
    hop_recv,
    plane_send,
    plane_recv,
    z_send,
    z_recv,
    next_sem,
    above_sem,
):
    n_dom, n_tp, per_dev, gen, prompt_len, group = sizes
    f32, bf16 = jnp.float32, jnp.bfloat16
    n_z = n_dom // Y_DIM
    n_plane = n_tp * Y_DIM
    dom = lax.axis_index("dom")
    tp = lax.axis_index("tp")
    my_y = lax.rem(dom, Y_DIM)
    my_z = dom // Y_DIM
    base = dom * per_dev
    bias_len = bias_hbm.shape[0]
    bias_part = biasv.shape[0]
    bias_last = bias_len - (n_tp - 1) * bias_part
    key_part = prompt_len // PARTS

    def device(d, t):
        return {"dom": d, "tp": t}

    def signal(sem, target):
        pl.semaphore_signal(sem, inc=1, device_id=target, device_id_type=MESH)

    def z_device(z):
        return device(z * Y_DIM + my_y, tp)

    me = tp * Y_DIM + my_y

    copy = pltpu.make_async_copy
    load_q = copy(q_hbm, qv, in_sems.at[0])
    load_gen = copy(gen_hbm, cache, in_sems.at[1])
    load_new = copy(new_hbm, newv, in_sems.at[2])
    load_tv = copy(tv_hbm, tvv, in_sems.at[3])
    load_keys = [
        copy(
            prompt_hbm.at[c * key_part : (c + 1) * key_part, 0:HEAD_DIM],
            keyv.at[c * key_part : (c + 1) * key_part],
            key_sems.at[c],
        )
        for c in range(PARTS)
    ]
    load_vals = copy(prompt_hbm.at[:, HEAD_DIM : 2 * HEAD_DIM], valv, in_sems.at[4])
    load_anc = copy(anc_hbm, anc, small_sems.at[0])
    load_lens = copy(lens_hbm, lens, small_sems.at[1])
    load_toks = copy(toks_hbm, toks, small_sems.at[2])
    load_prior = copy(prior_hbm, prior, small_sems.at[3])
    bias_most = copy(
        bias_hbm.at[pl.ds(pl.multiple_of(tp * bias_part, 8), bias_part)], biasv, small_sems.at[4]
    )
    bias_rest = copy(
        bias_hbm.at[bias_len - bias_last : bias_len], biasv.at[0:bias_last], small_sems.at[4]
    )
    load_toks.start()
    load_prior.start()
    load_lens.start()
    load_q.start()

    @pl.when(tp < n_tp - 1)
    def _():
        bias_most.start()

    @pl.when(tp == n_tp - 1)
    def _():
        bias_rest.start()

    for item in load_keys:
        item.start()
    load_new.start()

    barrier = pltpu.get_barrier_semaphore()

    n_x = n_tp // 2
    my_x, core = tp // 2, lax.rem(tp, 2)
    farthest = lambda n: sorted(range(n), key=lambda d: -min(d, n - d))
    targets = []
    for target_core in range(2):
        for dx in farthest(n_x):
            for dy in farthest(Y_DIM):
                if dx or dy:
                    targets.append((dx, dy, target_core))
    targets.append((0, 0, 1 - core))

    def plane_target(j):
        dx, dy, target_core = targets[j]
        x = lax.rem(my_x + dx, n_x)
        y = lax.rem(my_y + dy, Y_DIM)
        return device(my_z * Y_DIM + y, x * 2 + target_core)

    for j in range(len(targets)):
        signal(barrier, plane_target(j))

    load_gen.start()
    load_vals.start()
    load_tv.start()
    load_anc.start()

    def greet_above(z, carry):
        signal(barrier, z_device(z))
        return carry

    lax.fori_loop(my_z + 1, n_z, greet_above, 0)

    @pl.when(dom < n_dom - 1)
    def _():
        signal(barrier, device(dom + 1, tp))

    n_rows = 2 * group * per_dev
    to_row = lax.broadcasted_iota(jnp.int32, (n_rows, n_rows), 0)
    from_row = lax.broadcasted_iota(jnp.int32, (n_rows, n_rows), 1)
    wanted = lax.rem(to_row, 2 * group) * per_dev + to_row // (2 * group)
    order = jnp.where(from_row == wanted, 1.0, 0.0).astype(jnp.bfloat16)
    load_q.wait()
    tiles = [qv[t, :, h * HEAD_DIM : (h + 1) * HEAD_DIM] for t in range(2) for h in range(group)]
    stacked = jnp.concatenate(tiles, axis=0)
    query = jnp.dot(order, stacked, preferred_element_type=jnp.float32).astype(jnp.bfloat16)

    load_toks.wait()

    @pl.when(tp < n_tp - 1)
    def _():
        bias_most.wait()

    @pl.when(tp == n_tp - 1)
    def _():
        bias_rest.wait()

    lanes = lax.broadcasted_iota(jnp.int32, (1, 128), 1)
    bias_start = tp * (bias_part * 128)
    for p in range(per_dev):
        for t in range(2):
            local_token = toks[t, p] - bias_start
            spot = jnp.clip(lax.shift_right_arithmetic(local_token, 7), 0, bias_part - 1)
            row = biasv[pl.ds(spot, 1), :]
            bias_rows[p * 2 + t : p * 2 + t + 1, :] = jnp.where(
                lanes == local_token - spot * 128, row, 0.0
            )

    first_tp = jnp.where(tp == 0, 1.0, 0.0)
    load_prior.wait()
    weight_lane = 2 * 2 * per_dev + per_dev * my_y
    prior_row = jnp.zeros((1, 128), f32)
    for p in range(per_dev):
        prior_row = jnp.where(lanes == weight_lane + p, prior[p] * first_tp, prior_row)
    pair_ids = lax.broadcasted_iota(jnp.int32, (2 * per_dev, 128), 0)
    lane_ids = lax.broadcasted_iota(jnp.int32, (2 * per_dev, 128), 1)
    pair_step = lax.rem(pair_ids, 2)
    at_twist = lane_ids == pair_step * per_dev + pair_ids // 2
    at_weight = lane_ids == weight_lane + pair_ids // 2
    placed = jnp.where(
        at_twist, 1.0, jnp.where(at_weight, (2 * pair_step - 1).astype(f32), 0.0)
    )

    nt = (((1,), (1,)), ((), ()))
    part = 2 * group
    chunk = 512
    top = None
    for c in range(prompt_len // chunk):
        if c * chunk % key_part == 0:
            load_keys[c * chunk // key_part].wait()
        raw = lax.dot_general(
            query, keyv[c * chunk : (c + 1) * chunk, :], nt, preferred_element_type=jnp.float32
        )
        scores[:, c * chunk : (c + 1) * chunk] = raw
        for i in range(chunk // 128):
            piece = raw[:, i * 128 : (i + 1) * 128]
            top = piece if top is None else jnp.maximum(top, piece)

    load_lens.wait()
    load_new.wait()
    load_gen.wait()
    load_vals.wait()
    load_tv.wait()
    filler = jnp.zeros((128 - 2 * per_dev, HEAD_DIM), bf16)
    new_keys = jnp.concatenate([newv[0, :, 0:HEAD_DIM], newv[1, :, 0:HEAD_DIM], filler], axis=0)
    new_vals = jnp.concatenate(
        [newv[0, :, HEAD_DIM : 2 * HEAD_DIM], newv[1, :, HEAD_DIM : 2 * HEAD_DIM], filler], axis=0
    )
    new_row = lax.broadcasted_iota(jnp.int32, (n_rows, 128), 0)
    new_col = lax.broadcasted_iota(jnp.int32, (n_rows, 128), 1)
    shown = jnp.logical_and(
        lax.rem(new_col, per_dev) == new_row // (2 * group),
        new_col // per_dev <= lax.rem(new_row // group, 2),
    )
    fresh = lax.dot_general(query, new_keys, nt, preferred_element_type=f32)
    fresh = jnp.where(shown, fresh, NEG_FILL)
    own = []
    cols = lax.broadcasted_iota(jnp.int32, (part, gen), 1)
    for p in range(per_dev):
        raw = lax.dot_general(
            query[p * part : (p + 1) * part], cache[p, :, 0:HEAD_DIM], nt,
            preferred_element_type=jnp.float32,
        )
        own.append(jnp.where(cols < lens[base + p], raw, NEG_FILL))
    own = jnp.concatenate(own, axis=0)
    row_max = jnp.max(jnp.maximum(jnp.maximum(top, fresh), own), axis=1, keepdims=True)
    scale = LOG2E / math.sqrt(HEAD_DIM)
    exps = jnp.exp2((own - row_max) * scale)
    fresh_exps = jnp.exp2((fresh - row_max) * scale)
    total = exps + fresh_exps
    probs = exps.astype(jnp.bfloat16)
    mixed = []
    for p in range(per_dev):
        mixed.append(
            jnp.dot(
                probs[p * part : (p + 1) * part], cache[p, :, HEAD_DIM : 2 * HEAD_DIM],
                preferred_element_type=jnp.float32,
            )
        )
    mixed = jnp.concatenate(mixed, axis=0) + jnp.dot(
        fresh_exps.astype(bf16), new_vals, preferred_element_type=f32
    )
    block = n_rows // 2
    totals, mixes = [], []
    for r in range(2):
        lines = slice(r * block, (r + 1) * block)
        part_total, part_mixed = total[lines], mixed[lines]
        for c in range(prompt_len // chunk):
            exps = jnp.exp2((scores[lines, c * chunk : (c + 1) * chunk] - row_max[lines]) * scale)
            for i in range(chunk // 128):
                part_total = part_total + exps[:, i * 128 : (i + 1) * 128]
            part_mixed = part_mixed + jnp.dot(
                exps.astype(bf16), valv[c * chunk : (c + 1) * chunk, :], preferred_element_type=f32
            )
        totals.append(part_total)
        mixes.append(part_mixed)
    total, mixed = jnp.concatenate(totals, axis=0), jnp.concatenate(mixes, axis=0)
    row_sum = jnp.sum(total, axis=1, keepdims=True)
    mixed = mixed / row_sum
    weighted = mixed.reshape(2 * per_dev, group, HEAD_DIM) * tvv[...][None]
    pair_rows = jnp.sum(weighted, axis=1) + bias_rows[...]
    pair_col = jnp.sum(pair_rows, axis=1, keepdims=True)
    message = jnp.sum(placed * pair_col, axis=0, keepdims=True) + prior_row
    plane_rows[me] = message

    pl.semaphore_wait(
        barrier, n_plane - 1 + my_z + jnp.where(dom > 0, 1, 0)
    )

    def plane_send_to(j):
        return pltpu.make_async_remote_copy(
            src_ref=plane_rows.at[me],
            dst_ref=plane_rows.at[me],
            send_sem=plane_send,
            recv_sem=plane_recv,
            device_id=plane_target(j),
            device_id_type=MESH,
        )

    plane_sends = [plane_send_to(j) for j in range(len(targets))]
    for item in plane_sends:
        item.start()

    @pl.when(dom > 0)
    def _():
        signal(next_sem, device(dom - 1, tp))

    rows = lax.broadcasted_iota(jnp.int32, (gen, 2 * HEAD_DIM), 0).astype(f32).astype(bf16)
    for p in range(per_dev):
        start = lens[base + p].astype(f32)
        at_first = jnp.full((gen, 2 * HEAD_DIM), start, f32).astype(bf16)
        at_second = jnp.full((gen, 2 * HEAD_DIM), start + 1.0, f32).astype(bf16)
        first = jnp.broadcast_to(newv[0, pl.ds(p, 1), :], (gen, 2 * HEAD_DIM))
        second = jnp.broadcast_to(newv[1, pl.ds(p, 1), :], (gen, 2 * HEAD_DIM))
        later = jnp.where(rows == at_second, second, jnp.zeros_like(second))
        cache[p] = jnp.where(
            rows < at_first, cache[p], jnp.where(rows == at_first, first, later)
        )

    load_anc.wait()
    for slot, offset in enumerate(OFFSETS):
        target = jnp.clip(dom + offset, 0, n_dom - 1) * per_dev
        low, high = per_dev - 1, 0
        for i in range(per_dev):
            spot = anc[target + i] - base
            mine = jnp.logical_and(spot >= 0, spot < per_dev)
            low = jnp.minimum(low, jnp.where(mine, spot, per_dev - 1))
            high = jnp.maximum(high, jnp.where(mine, spot, 0))
        picked[slot, 0] = cache[low]
        picked[slot, 1] = cache[high]

    all_sent = pltpu.make_async_remote_copy(
        src_ref=plane_rows.at[0 : n_plane - 1],
        dst_ref=plane_rows.at[0 : n_plane - 1],
        send_sem=plane_send,
        recv_sem=plane_recv,
        device_id=device(dom, 0),
        device_id_type=MESH,
    )
    all_sent.wait_recv()

    sums = [plane_rows[slot] for slot in range(n_plane)]
    while len(sums) > 1:
        sums = [a + b for a, b in zip(sums[::2], sums[1::2])]
    z_rows[my_z] = sums[0]

    def z_copy(dst, z):
        return pltpu.make_async_remote_copy(
            src_ref=z_rows.at[my_z],
            dst_ref=z_rows.at[dst],
            send_sem=z_send,
            recv_sem=z_recv,
            device_id=z_device(z),
            device_id_type=MESH,
        )

    def z_start(z, carry):
        z_copy(my_z, z).start()
        return carry

    lax.fori_loop(0, my_z, z_start, 0)

    def greet_below(z, carry):
        signal(above_sem, z_device(z))
        return carry

    lax.fori_loop(0, my_z, greet_below, 0)

    def hop(src, dst, i, shift):
        return pltpu.make_async_remote_copy(
            src_ref=src,
            dst_ref=dst,
            send_sem=hop_send.at[i],
            recv_sem=hop_recv.at[i],
            device_id=device(jnp.clip(dom + shift, 0, n_dom - 1), tp),
            device_id_type=MESH,
        )

    far = n_dom - 1
    inner = jnp.logical_and(dom > 0, dom < far)
    hops = [
        (hop(picked.at[0], relay.at[0], 0, 1), dom < far - 1, inner),
        (hop(picked.at[2], relay.at[1], 1, -1), dom > 1, inner),
        (hop(picked.at[1], landed.at[1], 2, 1), dom < far, dom > 0),
        (hop(picked.at[3], landed.at[3], 3, -1), dom > 0, dom < far),
        (hop(relay.at[0], landed.at[0], 4, 1), inner, dom > 1),
        (hop(relay.at[1], landed.at[2], 5, -1), inner, dom < far - 1),
    ]

    def start_hop(i):
        pl.when(hops[i][1])(hops[i][0].start)

    def receive_hop(i):
        pl.when(hops[i][2])(hops[i][0].wait_recv)

    @pl.when(dom < far)
    def _():
        pl.semaphore_wait(next_sem, 1)

    for i in range(4):
        start_hop(i)

    receive_hop(0)
    start_hop(4)
    receive_hop(1)
    start_hop(5)

    @pl.when(my_z < n_z - 1)
    def _():
        pl.semaphore_wait(above_sem, n_z - 1 - my_z)

    lax.fori_loop(my_z + 1, n_z, z_start, 0)

    own_sum = plane_rows[my_y]
    for t in range(1, n_tp):
        own_sum = own_sum + plane_rows[t * Y_DIM + my_y]
    twist_out[0:1, :] = own_sum[:, 0:per_dev]
    twist_out[1:2, :] = pltpu.roll(own_sum, 128 - per_dev, 1)[:, 0:per_dev]
    own_weight = own_sum
    for y in range(Y_DIM):
        moved = pltpu.roll(own_sum, 128 - 4 * per_dev - y * per_dev, 1)
        own_weight = jnp.where(my_y == y, moved, own_weight)

    for i in range(2, 6):
        receive_hop(i)
    firsts = []
    for offset in OFFSETS:
        low = per_dev - 1
        for i in range(per_dev):
            spot = anc[base + i] - (base - offset * per_dev)
            theirs = jnp.logical_and(spot >= 0, spot < per_dev)
            low = jnp.minimum(low, jnp.where(theirs, spot, per_dev - 1))
        firsts.append(low)
    new_lens = jnp.zeros((1, 128), jnp.int32)
    for p in range(per_dev):
        new_lens = jnp.where(lanes == p, lens[anc[base + p]] + 2, new_lens)
        spot = anc[base + p] - base
        home = jnp.logical_and(spot >= 0, spot < per_dev)
        home_spot = jnp.clip(spot, 0, per_dev - 1)
        place = 0
        for slot, offset in enumerate(OFFSETS):
            there = spot + offset * per_dev
            theirs = jnp.logical_and(there >= 0, there < per_dev)
            second = jnp.where(there == firsts[slot], 0, 1)
            place = jnp.where(theirs, 2 * slot + second, place)
        moved = landed[place // 2, lax.rem(place, 2)]
        cache_out[p] = jnp.where(home, cache[home_spot], moved)
    len_out[...] = new_lens[:, 0:per_dev]

    for item, sends, _ in hops:
        pl.when(sends)(item.wait_send)
    all_sent.wait_send()
    z_all = pltpu.make_async_remote_copy(
        src_ref=z_rows.at[0 : n_z - 1],
        dst_ref=z_rows.at[0 : n_z - 1],
        send_sem=z_send,
        recv_sem=z_recv,
        device_id=device(dom, 0),
        device_id_type=MESH,
    )
    z_all.wait_send()
    z_all.wait_recv()
    all_weights = jnp.where((lanes >= 4 * per_dev)[None], z_rows[...], NEG_FILL)
    largest = jnp.max(jnp.max(all_weights, axis=0), axis=1, keepdims=True)
    exp_total = jnp.sum(jnp.sum(jnp.exp(all_weights - largest[None]), axis=0), axis=1, keepdims=True)
    normalized = own_weight - (largest + jnp.log(exp_total))
    norm_out[...] = normalized[:, 0:per_dev]


def finish(*refs):
    count = (len(refs) - 1) // 2
    copies = [
        pltpu.make_async_copy(refs[i], refs[count + i], refs[-1].at[i]) for i in range(count)
    ]
    for item in copies:
        item.start()
    for item in copies:
        item.wait()


def local(
    n_dom,
    n_tp,
    queries,
    new_kv,
    gen_cache,
    prompt_kv,
    lengths,
    ancestors,
    tokens,
    twist_vector,
    twist_bias,
    prior_weights,
):
    per_dev, gen, width = gen_cache.shape
    prompt_len = prompt_kv.shape[0]
    group = queries.shape[2] // HEAD_DIM
    n_rows = 2 * group * per_dev
    n_z = n_dom // Y_DIM
    n_plane = n_tp * Y_DIM
    bias_table = twist_bias.reshape(-1, 128)
    bias_part = -(-bias_table.shape[0] // (8 * n_tp)) * 8
    any_space = pl.BlockSpec(memory_space=pl.ANY)
    vmem = pl.BlockSpec(memory_space=pltpu.VMEM)
    f32, bf16, i32 = jnp.float32, jnp.bfloat16, jnp.int32
    dma = pltpu.SemaphoreType.DMA
    shapes = (((2, per_dev), f32), ((1, per_dev), f32), (gen_cache.shape, bf16), ((1, per_dev), i32))
    results = pl.pallas_call(
        functools.partial(kernel, (n_dom, n_tp, per_dev, gen, prompt_len, group)),
        out_shape=tuple(pltpu.VMEM(*shape) for shape in shapes),
        in_specs=[any_space] * 10,
        out_specs=(vmem,) * 4,
        scratch_shapes=[
            pltpu.SMEM(ancestors.shape, i32),
            pltpu.SMEM(lengths.shape, i32),
            pltpu.SMEM(tokens.shape, i32),
            pltpu.SMEM(prior_weights.shape, f32),
            pltpu.VMEM(queries.shape, bf16),
            pltpu.VMEM(new_kv.shape, bf16),
            pltpu.VMEM(gen_cache.shape, bf16),
            pltpu.VMEM((prompt_len, HEAD_DIM), bf16),
            pltpu.VMEM((prompt_len, HEAD_DIM), bf16),
            pltpu.VMEM((group, HEAD_DIM), f32),
            pltpu.VMEM((bias_part, 128), f32),
            pltpu.VMEM((n_rows, prompt_len), f32),
            pltpu.VMEM((4, 2, gen, width), bf16),
            pltpu.VMEM((2, 2, gen, width), bf16),
            pltpu.VMEM((4, 2, gen, width), bf16),
            pltpu.VMEM((2 * per_dev, 128), f32),
            pltpu.VMEM((n_plane, 1, 128), f32),
            pltpu.VMEM((n_z, 1, 128), f32),
            dma((5,)),
            dma((5,)),
            dma((PARTS,)),
            dma((6,)),
            dma((6,)),
            dma,
            dma,
            dma,
            dma,
            pltpu.SemaphoreType.REGULAR,
            pltpu.SemaphoreType.REGULAR,
        ],
        compiler_params=pltpu.CompilerParams(collective_id=0, has_side_effects=True),
        name="smc_step",
    )(
        ancestors,
        lengths,
        tokens,
        prior_weights,
        queries,
        new_kv,
        gen_cache,
        prompt_kv,
        twist_vector.reshape(group, HEAD_DIM),
        bias_table,
    )
    held = [pltpu.with_memory_space_constraint(x, pltpu.VMEM) for x in results]
    twist, normalized, resampled, new_lengths = pl.pallas_call(
        finish,
        out_shape=tuple(jax.ShapeDtypeStruct(*shape) for shape in shapes),
        in_specs=[any_space] * 4,
        out_specs=(any_space,) * 4,
        scratch_shapes=[dma((4,))],
        compiler_params=pltpu.CompilerParams(vmem_limit_bytes=4 << 20),
        name="finish",
    )(*held)
    return twist, normalized.reshape(per_dev), resampled, new_lengths.reshape(per_dev)


def solution(mesh):
    in_specs = (
        P(None, "dom", "tp"),
        P(None, "dom", "tp"),
        P("dom", None, "tp"),
        P(None, "tp"),
        P(),
        P(),
        P(None, "dom"),
        P("tp"),
        P(),
        P("dom"),
    )
    out_specs = (P(None, "dom"), P("dom"), P("dom", None, "tp"), P("dom"))
    return jax.shard_map(
        functools.partial(local, mesh.shape["dom"], mesh.shape["tp"]),
        mesh=mesh,
        in_specs=in_specs,
        out_specs=out_specs,
        check_vma=False,
    )
```

```python
import functools
import math

import jax
import jax.numpy as jnp
from jax import lax
from jax.experimental import pallas as pl
from jax.experimental.pallas import tpu as pltpu
from jax.sharding import PartitionSpec as P

HEAD_DIM = 128
Y_DIM = 4
NEG_FILL = -1e30
MESH = pl.DeviceIdType.MESH
LOG2E = 1.4426950408889634
PARTS = 2
OFFSETS = (2, 1, -2, -1)


def kernel(
    sizes,
    anc_hbm,
    lens_hbm,
    toks_hbm,
    prior_hbm,
    q_hbm,
    new_hbm,
    gen_hbm,
    prompt_hbm,
    tv_hbm,
    bias_hbm,
    twist_out,
    norm_out,
    cache_out,
    len_out,
    anc,
    lens,
    toks,
    prior,
    qv,
    newv,
    cache,
    keyv,
    valv,
    tvv,
    biasv,
    scores,
    picked,
    relay,
    landed,
    bias_rows,
    plane_rows,
    z_rows,
    small_sems,
    in_sems,
    key_sems,
    hop_send,
    hop_recv,
    plane_send,
    plane_recv,
    z_send,
    z_recv,
    next_sem,
    above_sem,
):
    n_dom, n_tp, per_dev, gen, prompt_len, group = sizes
    f32, bf16 = jnp.float32, jnp.bfloat16
    n_z = n_dom // Y_DIM
    n_plane = n_tp * Y_DIM
    dom = lax.axis_index("dom")
    tp = lax.axis_index("tp")
    my_y = lax.rem(dom, Y_DIM)
    my_z = dom // Y_DIM
    base = dom * per_dev
    bias_len = bias_hbm.shape[0]
    bias_part = biasv.shape[0]
    bias_last = bias_len - (n_tp - 1) * bias_part
    key_part = prompt_len // PARTS

    def device(d, t):
        return {"dom": d, "tp": t}

    def signal(sem, target):
        pl.semaphore_signal(sem, inc=1, device_id=target, device_id_type=MESH)

    def z_device(z):
        return device(z * Y_DIM + my_y, tp)

    me = tp * Y_DIM + my_y

    copy = pltpu.make_async_copy
    load_q = copy(q_hbm, qv, in_sems.at[0])
    load_gen = copy(gen_hbm, cache, in_sems.at[1])
    load_new = copy(new_hbm, newv, in_sems.at[2])
    load_tv = copy(tv_hbm, tvv, in_sems.at[3])
    load_keys = [
        copy(
            prompt_hbm.at[c * key_part : (c + 1) * key_part, 0:HEAD_DIM],
            keyv.at[c * key_part : (c + 1) * key_part],
            key_sems.at[c],
        )
        for c in range(PARTS)
    ]
    load_vals = copy(prompt_hbm.at[:, HEAD_DIM : 2 * HEAD_DIM], valv, in_sems.at[4])
    load_anc = copy(anc_hbm, anc, small_sems.at[0])
    load_lens = copy(lens_hbm, lens, small_sems.at[1])
    load_toks = copy(toks_hbm, toks, small_sems.at[2])
    load_prior = copy(prior_hbm, prior, small_sems.at[3])
    bias_most = copy(
        bias_hbm.at[pl.ds(pl.multiple_of(tp * bias_part, 8), bias_part)], biasv, small_sems.at[4]
    )
    bias_rest = copy(
        bias_hbm.at[bias_len - bias_last : bias_len], biasv.at[0:bias_last], small_sems.at[4]
    )
    load_q.start()
    for item in load_keys:
        item.start()
    load_toks.start()
    load_prior.start()
    load_lens.start()

    @pl.when(tp < n_tp - 1)
    def _():
        bias_most.start()

    @pl.when(tp == n_tp - 1)
    def _():
        bias_rest.start()

    load_new.start()

    barrier = pltpu.get_barrier_semaphore()

    n_x = n_tp // 2
    my_x, core = tp // 2, lax.rem(tp, 2)
    farthest = lambda n: sorted(range(n), key=lambda d: -min(d, n - d))
    targets = []
    for target_core in range(2):
        for dx in farthest(n_x):
            for dy in farthest(Y_DIM):
                if dx or dy:
                    targets.append((dx, dy, target_core))
    targets.append((0, 0, 1 - core))

    def plane_target(j):
        dx, dy, target_core = targets[j]
        x = lax.rem(my_x + dx, n_x)
        y = lax.rem(my_y + dy, Y_DIM)
        return device(my_z * Y_DIM + y, x * 2 + target_core)

    for j in range(len(targets)):
        signal(barrier, plane_target(j))

    load_gen.start()
    load_vals.start()
    load_tv.start()
    load_anc.start()

    def greet_above(z, carry):
        signal(barrier, z_device(z))
        return carry

    lax.fori_loop(my_z + 1, n_z, greet_above, 0)

    @pl.when(dom < n_dom - 1)
    def _():
        signal(barrier, device(dom + 1, tp))

    n_rows = 2 * group * per_dev
    to_row = lax.broadcasted_iota(jnp.int32, (n_rows, n_rows), 0)
    from_row = lax.broadcasted_iota(jnp.int32, (n_rows, n_rows), 1)
    wanted = lax.rem(to_row, 2 * group) * per_dev + to_row // (2 * group)
    order = jnp.where(from_row == wanted, 1.0, 0.0).astype(jnp.bfloat16)
    load_q.wait()
    tiles = [qv[t, :, h * HEAD_DIM : (h + 1) * HEAD_DIM] for t in range(2) for h in range(group)]
    stacked = jnp.concatenate(tiles, axis=0)
    query = jnp.dot(order, stacked, preferred_element_type=jnp.float32).astype(jnp.bfloat16)

    nt = (((1,), (1,)), ((), ()))
    part = 2 * group
    chunk = 512
    top = None
    for c in range(prompt_len // chunk):
        if c * chunk % key_part == 0:
            load_keys[c * chunk // key_part].wait()
        raw = lax.dot_general(
            query, keyv[c * chunk : (c + 1) * chunk, :], nt, preferred_element_type=jnp.float32
        )
        scores[:, c * chunk : (c + 1) * chunk] = raw
        for i in range(chunk // 128):
            piece = raw[:, i * 128 : (i + 1) * 128]
            top = piece if top is None else jnp.maximum(top, piece)

    load_toks.wait()

    @pl.when(tp < n_tp - 1)
    def _():
        bias_most.wait()

    @pl.when(tp == n_tp - 1)
    def _():
        bias_rest.wait()

    load_prior.wait()
    load_lens.wait()
    load_new.wait()
    load_gen.wait()
    load_vals.wait()
    load_tv.wait()
    filler = jnp.zeros((128 - 2 * per_dev, HEAD_DIM), bf16)
    new_keys = jnp.concatenate([newv[0, :, 0:HEAD_DIM], newv[1, :, 0:HEAD_DIM], filler], axis=0)
    new_vals = jnp.concatenate(
        [newv[0, :, HEAD_DIM : 2 * HEAD_DIM], newv[1, :, HEAD_DIM : 2 * HEAD_DIM], filler], axis=0
    )
    new_row = lax.broadcasted_iota(jnp.int32, (n_rows, 128), 0)
    new_col = lax.broadcasted_iota(jnp.int32, (n_rows, 128), 1)
    shown = jnp.logical_and(
        lax.rem(new_col, per_dev) == new_row // (2 * group),
        new_col // per_dev <= lax.rem(new_row // group, 2),
    )
    fresh = lax.dot_general(query, new_keys, nt, preferred_element_type=f32)
    fresh = jnp.where(shown, fresh, NEG_FILL)
    own = []
    cols = lax.broadcasted_iota(jnp.int32, (part, gen), 1)
    for p in range(per_dev):
        raw = lax.dot_general(
            query[p * part : (p + 1) * part], cache[p, :, 0:HEAD_DIM], nt,
            preferred_element_type=jnp.float32,
        )
        own.append(jnp.where(cols < lens[base + p], raw, NEG_FILL))
    own = jnp.concatenate(own, axis=0)
    row_max = jnp.max(jnp.maximum(jnp.maximum(top, fresh), own), axis=1, keepdims=True)
    scale = LOG2E / math.sqrt(HEAD_DIM)
    exps = jnp.exp2((own - row_max) * scale)
    fresh_exps = jnp.exp2((fresh - row_max) * scale)
    total = exps + fresh_exps
    probs = exps.astype(jnp.bfloat16)
    mixed = []
    for p in range(per_dev):
        mixed.append(
            jnp.dot(
                probs[p * part : (p + 1) * part], cache[p, :, HEAD_DIM : 2 * HEAD_DIM],
                preferred_element_type=jnp.float32,
            )
        )
    mixed = jnp.concatenate(mixed, axis=0) + jnp.dot(
        fresh_exps.astype(bf16), new_vals, preferred_element_type=f32
    )
    block = n_rows // 2
    totals, mixes = [], []
    for r in range(2):
        lines = slice(r * block, (r + 1) * block)
        part_total, part_mixed = total[lines], mixed[lines]
        for c in range(prompt_len // chunk):
            exps = jnp.exp2((scores[lines, c * chunk : (c + 1) * chunk] - row_max[lines]) * scale)
            for i in range(chunk // 128):
                part_total = part_total + exps[:, i * 128 : (i + 1) * 128]
            part_mixed = part_mixed + jnp.dot(
                exps.astype(bf16), valv[c * chunk : (c + 1) * chunk, :], preferred_element_type=f32
            )
        totals.append(part_total)
        mixes.append(part_mixed)
    total, mixed = jnp.concatenate(totals, axis=0), jnp.concatenate(mixes, axis=0)
    lanes = lax.broadcasted_iota(jnp.int32, (1, 128), 1)
    bias_start = tp * (bias_part * 128)
    for p in range(per_dev):
        for t in range(2):
            local_token = toks[t, p] - bias_start
            spot = jnp.clip(lax.shift_right_arithmetic(local_token, 7), 0, bias_part - 1)
            row = biasv[pl.ds(spot, 1), :]
            bias_rows[p * 2 + t : p * 2 + t + 1, :] = jnp.where(
                lanes == local_token - spot * 128, row, 0.0
            )

    first_tp = jnp.where(tp == 0, 1.0, 0.0)
    weight_lane = 2 * 2 * per_dev + per_dev * my_y
    prior_row = jnp.zeros((1, 128), f32)
    for p in range(per_dev):
        prior_row = jnp.where(lanes == weight_lane + p, prior[p] * first_tp, prior_row)
    pair_ids = lax.broadcasted_iota(jnp.int32, (2 * per_dev, 128), 0)
    lane_ids = lax.broadcasted_iota(jnp.int32, (2 * per_dev, 128), 1)
    pair_step = lax.rem(pair_ids, 2)
    at_twist = lane_ids == pair_step * per_dev + pair_ids // 2
    at_weight = lane_ids == weight_lane + pair_ids // 2
    placed = jnp.where(
        at_twist, 1.0, jnp.where(at_weight, (2 * pair_step - 1).astype(f32), 0.0)
    )

    row_sum = jnp.sum(total, axis=1, keepdims=True)
    mixed = mixed / row_sum
    weighted = mixed.reshape(2 * per_dev, group, HEAD_DIM) * tvv[...][None]
    pair_rows = jnp.sum(weighted, axis=1) + bias_rows[...]
    pair_col = jnp.sum(pair_rows, axis=1, keepdims=True)
    message = jnp.sum(placed * pair_col, axis=0, keepdims=True) + prior_row
    plane_rows[me] = message

    pl.semaphore_wait(
        barrier, n_plane - 1 + my_z + jnp.where(dom > 0, 1, 0)
    )

    def plane_send_to(j):
        return pltpu.make_async_remote_copy(
            src_ref=plane_rows.at[me],
            dst_ref=plane_rows.at[me],
            send_sem=plane_send,
            recv_sem=plane_recv,
            device_id=plane_target(j),
            device_id_type=MESH,
        )

    plane_sends = [plane_send_to(j) for j in range(len(targets))]
    for item in plane_sends:
        item.start()

    @pl.when(dom > 0)
    def _():
        signal(next_sem, device(dom - 1, tp))

    rows = lax.broadcasted_iota(jnp.int32, (gen, 2 * HEAD_DIM), 0).astype(f32).astype(bf16)
    for p in range(per_dev):
        start = lens[base + p].astype(f32)
        at_first = jnp.full((gen, 2 * HEAD_DIM), start, f32).astype(bf16)
        at_second = jnp.full((gen, 2 * HEAD_DIM), start + 1.0, f32).astype(bf16)
        first = jnp.broadcast_to(newv[0, pl.ds(p, 1), :], (gen, 2 * HEAD_DIM))
        second = jnp.broadcast_to(newv[1, pl.ds(p, 1), :], (gen, 2 * HEAD_DIM))
        later = jnp.where(rows == at_second, second, jnp.zeros_like(second))
        cache[p] = jnp.where(
            rows < at_first, cache[p], jnp.where(rows == at_first, first, later)
        )

    load_anc.wait()
    for slot, offset in enumerate(OFFSETS):
        target = jnp.clip(dom + offset, 0, n_dom - 1) * per_dev
        low, high = per_dev - 1, 0
        for i in range(per_dev):
            spot = anc[target + i] - base
            mine = jnp.logical_and(spot >= 0, spot < per_dev)
            low = jnp.minimum(low, jnp.where(mine, spot, per_dev - 1))
            high = jnp.maximum(high, jnp.where(mine, spot, 0))
        picked[slot, 0] = cache[low]
        picked[slot, 1] = cache[high]

    all_sent = pltpu.make_async_remote_copy(
        src_ref=plane_rows.at[0 : n_plane - 1],
        dst_ref=plane_rows.at[0 : n_plane - 1],
        send_sem=plane_send,
        recv_sem=plane_recv,
        device_id=device(dom, 0),
        device_id_type=MESH,
    )
    all_sent.wait_recv()

    sums = [plane_rows[slot] for slot in range(n_plane)]
    while len(sums) > 1:
        sums = [a + b for a, b in zip(sums[::2], sums[1::2])]
    z_rows[my_z] = sums[0]

    def z_copy(dst, z):
        return pltpu.make_async_remote_copy(
            src_ref=z_rows.at[my_z],
            dst_ref=z_rows.at[dst],
            send_sem=z_send,
            recv_sem=z_recv,
            device_id=z_device(z),
            device_id_type=MESH,
        )

    def z_start(z, carry):
        z_copy(my_z, z).start()
        return carry

    lax.fori_loop(0, my_z, z_start, 0)

    def greet_below(z, carry):
        signal(above_sem, z_device(z))
        return carry

    lax.fori_loop(0, my_z, greet_below, 0)

    def hop(src, dst, i, shift):
        return pltpu.make_async_remote_copy(
            src_ref=src,
            dst_ref=dst,
            send_sem=hop_send.at[i],
            recv_sem=hop_recv.at[i],
            device_id=device(jnp.clip(dom + shift, 0, n_dom - 1), tp),
            device_id_type=MESH,
        )

    far = n_dom - 1
    inner = jnp.logical_and(dom > 0, dom < far)
    hops = [
        (hop(picked.at[0], relay.at[0], 0, 1), dom < far - 1, inner),
        (hop(picked.at[2], relay.at[1], 1, -1), dom > 1, inner),
        (hop(picked.at[1], landed.at[1], 2, 1), dom < far, dom > 0),
        (hop(picked.at[3], landed.at[3], 3, -1), dom > 0, dom < far),
        (hop(relay.at[0], landed.at[0], 4, 1), inner, dom > 1),
        (hop(relay.at[1], landed.at[2], 5, -1), inner, dom < far - 1),
    ]

    def start_hop(i):
        pl.when(hops[i][1])(hops[i][0].start)

    def receive_hop(i):
        pl.when(hops[i][2])(hops[i][0].wait_recv)

    @pl.when(dom < far)
    def _():
        pl.semaphore_wait(next_sem, 1)

    for i in range(4):
        start_hop(i)

    receive_hop(0)
    start_hop(4)
    receive_hop(1)
    start_hop(5)

    @pl.when(my_z < n_z - 1)
    def _():
        pl.semaphore_wait(above_sem, n_z - 1 - my_z)

    lax.fori_loop(my_z + 1, n_z, z_start, 0)

    own_sum = plane_rows[my_y]
    for t in range(1, n_tp):
        own_sum = own_sum + plane_rows[t * Y_DIM + my_y]
    twist_out[0:1, :] = own_sum[:, 0:per_dev]
    twist_out[1:2, :] = pltpu.roll(own_sum, 128 - per_dev, 1)[:, 0:per_dev]
    own_weight = own_sum
    for y in range(Y_DIM):
        moved = pltpu.roll(own_sum, 128 - 4 * per_dev - y * per_dev, 1)
        own_weight = jnp.where(my_y == y, moved, own_weight)

    for i in range(2, 6):
        receive_hop(i)
    firsts = []
    for offset in OFFSETS:
        low = per_dev - 1
        for i in range(per_dev):
            spot = anc[base + i] - (base - offset * per_dev)
            theirs = jnp.logical_and(spot >= 0, spot < per_dev)
            low = jnp.minimum(low, jnp.where(theirs, spot, per_dev - 1))
        firsts.append(low)
    new_lens = jnp.zeros((1, 128), jnp.int32)
    for p in range(per_dev):
        new_lens = jnp.where(lanes == p, lens[anc[base + p]] + 2, new_lens)
        spot = anc[base + p] - base
        home = jnp.logical_and(spot >= 0, spot < per_dev)
        home_spot = jnp.clip(spot, 0, per_dev - 1)
        place = 0
        for slot, offset in enumerate(OFFSETS):
            there = spot + offset * per_dev
            theirs = jnp.logical_and(there >= 0, there < per_dev)
            second = jnp.where(there == firsts[slot], 0, 1)
            place = jnp.where(theirs, 2 * slot + second, place)
        moved = landed[place // 2, lax.rem(place, 2)]
        cache_out[p] = jnp.where(home, cache[home_spot], moved)
    len_out[...] = new_lens[:, 0:per_dev]

    for item, sends, _ in hops:
        pl.when(sends)(item.wait_send)
    all_sent.wait_send()
    z_all = pltpu.make_async_remote_copy(
        src_ref=z_rows.at[0 : n_z - 1],
        dst_ref=z_rows.at[0 : n_z - 1],
        send_sem=z_send,
        recv_sem=z_recv,
        device_id=device(dom, 0),
        device_id_type=MESH,
    )
    z_all.wait_send()
    z_all.wait_recv()
    all_weights = jnp.where((lanes >= 4 * per_dev)[None], z_rows[...], NEG_FILL)
    largest = jnp.max(jnp.max(all_weights, axis=0), axis=1, keepdims=True)
    exp_total = jnp.sum(jnp.sum(jnp.exp(all_weights - largest[None]), axis=0), axis=1, keepdims=True)
    normalized = own_weight - (largest + jnp.log(exp_total))
    norm_out[...] = normalized[:, 0:per_dev]


def finish(*refs):
    count = (len(refs) - 1) // 2
    copies = [
        pltpu.make_async_copy(refs[i], refs[count + i], refs[-1].at[i]) for i in range(count)
    ]
    for item in copies:
        item.start()
    for item in copies:
        item.wait()


def local(
    n_dom,
    n_tp,
    queries,
    new_kv,
    gen_cache,
    prompt_kv,
    lengths,
    ancestors,
    tokens,
    twist_vector,
    twist_bias,
    prior_weights,
):
    per_dev, gen, width = gen_cache.shape
    prompt_len = prompt_kv.shape[0]
    group = queries.shape[2] // HEAD_DIM
    n_rows = 2 * group * per_dev
    n_z = n_dom // Y_DIM
    n_plane = n_tp * Y_DIM
    bias_table = twist_bias.reshape(-1, 128)
    bias_part = -(-bias_table.shape[0] // (8 * n_tp)) * 8
    any_space = pl.BlockSpec(memory_space=pl.ANY)
    vmem = pl.BlockSpec(memory_space=pltpu.VMEM)
    f32, bf16, i32 = jnp.float32, jnp.bfloat16, jnp.int32
    dma = pltpu.SemaphoreType.DMA
    shapes = (((2, per_dev), f32), ((1, per_dev), f32), (gen_cache.shape, bf16), ((1, per_dev), i32))
    results = pl.pallas_call(
        functools.partial(kernel, (n_dom, n_tp, per_dev, gen, prompt_len, group)),
        out_shape=tuple(pltpu.VMEM(*shape) for shape in shapes),
        in_specs=[any_space] * 10,
        out_specs=(vmem,) * 4,
        scratch_shapes=[
            pltpu.SMEM(ancestors.shape, i32),
            pltpu.SMEM(lengths.shape, i32),
            pltpu.SMEM(tokens.shape, i32),
            pltpu.SMEM(prior_weights.shape, f32),
            pltpu.VMEM(queries.shape, bf16),
            pltpu.VMEM(new_kv.shape, bf16),
            pltpu.VMEM(gen_cache.shape, bf16),
            pltpu.VMEM((prompt_len, HEAD_DIM), bf16),
            pltpu.VMEM((prompt_len, HEAD_DIM), bf16),
            pltpu.VMEM((group, HEAD_DIM), f32),
            pltpu.VMEM((bias_part, 128), f32),
            pltpu.VMEM((n_rows, prompt_len), f32),
            pltpu.VMEM((4, 2, gen, width), bf16),
            pltpu.VMEM((2, 2, gen, width), bf16),
            pltpu.VMEM((4, 2, gen, width), bf16),
            pltpu.VMEM((2 * per_dev, 128), f32),
            pltpu.VMEM((n_plane, 1, 128), f32),
            pltpu.VMEM((n_z, 1, 128), f32),
            dma((5,)),
            dma((5,)),
            dma((PARTS,)),
            dma((6,)),
            dma((6,)),
            dma,
            dma,
            dma,
            dma,
            pltpu.SemaphoreType.REGULAR,
            pltpu.SemaphoreType.REGULAR,
        ],
        compiler_params=pltpu.CompilerParams(collective_id=0, has_side_effects=True),
        name="smc_step",
    )(
        ancestors,
        lengths,
        tokens,
        prior_weights,
        queries,
        new_kv,
        gen_cache,
        prompt_kv,
        twist_vector.reshape(group, HEAD_DIM),
        bias_table,
    )
    held = [pltpu.with_memory_space_constraint(x, pltpu.VMEM) for x in results]
    twist, normalized, resampled, new_lengths = pl.pallas_call(
        finish,
        out_shape=tuple(jax.ShapeDtypeStruct(*shape) for shape in shapes),
        in_specs=[any_space] * 4,
        out_specs=(any_space,) * 4,
        scratch_shapes=[dma((4,))],
        compiler_params=pltpu.CompilerParams(vmem_limit_bytes=4 << 20),
        name="finish",
    )(*held)
    return twist, normalized.reshape(per_dev), resampled, new_lengths.reshape(per_dev)


def solution(mesh):
    in_specs = (
        P(None, "dom", "tp"),
        P(None, "dom", "tp"),
        P("dom", None, "tp"),
        P(None, "tp"),
        P(),
        P(),
        P(None, "dom"),
        P("tp"),
        P(),
        P("dom"),
    )
    out_specs = (P(None, "dom"), P("dom"), P("dom", None, "tp"), P("dom"))
    return jax.shard_map(
        functools.partial(local, mesh.shape["dom"], mesh.shape["tp"]),
        mesh=mesh,
        in_specs=in_specs,
        out_specs=out_specs,
        check_vma=False,
    )
```

```python
import functools
import math

import jax
import jax.numpy as jnp
from jax import lax
from jax.experimental import pallas as pl
from jax.experimental.pallas import tpu as pltpu
from jax.sharding import PartitionSpec as P

HEAD_DIM = 128
Y_DIM = 4
NEG_FILL = -1e30
MESH = pl.DeviceIdType.MESH
LOG2E = 1.4426950408889634
PARTS = 1
OFFSETS = (2, 1, -2, -1)


def kernel(
    sizes,
    anc_hbm,
    lens_hbm,
    toks_hbm,
    prior_hbm,
    q_hbm,
    new_hbm,
    gen_hbm,
    prompt_hbm,
    tv_hbm,
    bias_hbm,
    twist_out,
    norm_out,
    cache_out,
    len_out,
    anc,
    lens,
    toks,
    prior,
    qv,
    newv,
    cache,
    keyv,
    valv,
    tvv,
    biasv,
    scores,
    picked,
    relay,
    landed,
    bias_rows,
    plane_rows,
    z_rows,
    small_sems,
    in_sems,
    key_sems,
    hop_send,
    hop_recv,
    plane_send,
    plane_recv,
    z_send,
    z_recv,
    next_sem,
    above_sem,
):
    n_dom, n_tp, per_dev, gen, prompt_len, group = sizes
    f32, bf16 = jnp.float32, jnp.bfloat16
    n_z = n_dom // Y_DIM
    n_plane = n_tp * Y_DIM
    dom = lax.axis_index("dom")
    tp = lax.axis_index("tp")
    my_y = lax.rem(dom, Y_DIM)
    my_z = dom // Y_DIM
    base = dom * per_dev
    bias_len = bias_hbm.shape[0]
    bias_part = biasv.shape[0]
    bias_last = bias_len - (n_tp - 1) * bias_part
    key_part = prompt_len // PARTS

    def device(d, t):
        return {"dom": d, "tp": t}

    def signal(sem, target):
        pl.semaphore_signal(sem, inc=1, device_id=target, device_id_type=MESH)

    def z_device(z):
        return device(z * Y_DIM + my_y, tp)

    me = tp * Y_DIM + my_y

    copy = pltpu.make_async_copy
    load_q = copy(q_hbm, qv, in_sems.at[0])
    load_gen = copy(gen_hbm, cache, in_sems.at[1])
    load_new = copy(new_hbm, newv, in_sems.at[2])
    load_tv = copy(tv_hbm, tvv, in_sems.at[3])
    load_keys = [
        copy(
            prompt_hbm.at[c * key_part : (c + 1) * key_part, 0:HEAD_DIM],
            keyv.at[c * key_part : (c + 1) * key_part],
            key_sems.at[c],
        )
        for c in range(PARTS)
    ]
    load_vals = copy(prompt_hbm.at[:, HEAD_DIM : 2 * HEAD_DIM], valv, in_sems.at[4])
    load_anc = copy(anc_hbm, anc, small_sems.at[0])
    load_lens = copy(lens_hbm, lens, small_sems.at[1])
    load_toks = copy(toks_hbm, toks, small_sems.at[2])
    load_prior = copy(prior_hbm, prior, small_sems.at[3])
    bias_most = copy(
        bias_hbm.at[pl.ds(pl.multiple_of(tp * bias_part, 8), bias_part)], biasv, small_sems.at[4]
    )
    bias_rest = copy(
        bias_hbm.at[bias_len - bias_last : bias_len], biasv.at[0:bias_last], small_sems.at[4]
    )
    load_q.start()
    for item in load_keys:
        item.start()
    load_toks.start()
    load_prior.start()
    load_lens.start()

    @pl.when(tp < n_tp - 1)
    def _():
        bias_most.start()

    @pl.when(tp == n_tp - 1)
    def _():
        bias_rest.start()

    load_new.start()

    barrier = pltpu.get_barrier_semaphore()

    n_x = n_tp // 2
    my_x, core = tp // 2, lax.rem(tp, 2)
    farthest = lambda n: sorted(range(n), key=lambda d: -min(d, n - d))
    targets = []
    for target_core in range(2):
        for dx in farthest(n_x):
            for dy in farthest(Y_DIM):
                if dx or dy:
                    targets.append((dx, dy, target_core))
    targets.append((0, 0, 1 - core))

    def plane_target(j):
        dx, dy, target_core = targets[j]
        x = lax.rem(my_x + dx, n_x)
        y = lax.rem(my_y + dy, Y_DIM)
        return device(my_z * Y_DIM + y, x * 2 + target_core)

    for j in range(len(targets)):
        signal(barrier, plane_target(j))

    load_gen.start()
    load_vals.start()
    load_tv.start()
    load_anc.start()

    def greet_above(z, carry):
        signal(barrier, z_device(z))
        return carry

    lax.fori_loop(my_z + 1, n_z, greet_above, 0)

    @pl.when(dom < n_dom - 1)
    def _():
        signal(barrier, device(dom + 1, tp))

    n_rows = 2 * group * per_dev
    to_row = lax.broadcasted_iota(jnp.int32, (n_rows, n_rows), 0)
    from_row = lax.broadcasted_iota(jnp.int32, (n_rows, n_rows), 1)
    wanted = lax.rem(to_row, 2 * group) * per_dev + to_row // (2 * group)
    order = jnp.where(from_row == wanted, 1.0, 0.0).astype(jnp.bfloat16)
    load_q.wait()
    tiles = [qv[t, :, h * HEAD_DIM : (h + 1) * HEAD_DIM] for t in range(2) for h in range(group)]
    stacked = jnp.concatenate(tiles, axis=0)
    query = jnp.dot(order, stacked, preferred_element_type=jnp.float32).astype(jnp.bfloat16)

    nt = (((1,), (1,)), ((), ()))
    part = 2 * group
    chunk = 512
    top = None
    for c in range(prompt_len // chunk):
        if c * chunk % key_part == 0:
            load_keys[c * chunk // key_part].wait()
        raw = lax.dot_general(
            query, keyv[c * chunk : (c + 1) * chunk, :], nt, preferred_element_type=jnp.float32
        )
        scores[:, c * chunk : (c + 1) * chunk] = raw
        for i in range(chunk // 128):
            piece = raw[:, i * 128 : (i + 1) * 128]
            top = piece if top is None else jnp.maximum(top, piece)

    load_toks.wait()

    @pl.when(tp < n_tp - 1)
    def _():
        bias_most.wait()

    @pl.when(tp == n_tp - 1)
    def _():
        bias_rest.wait()

    load_prior.wait()
    load_lens.wait()
    load_new.wait()
    load_gen.wait()
    load_vals.wait()
    load_tv.wait()
    filler = jnp.zeros((128 - 2 * per_dev, HEAD_DIM), bf16)
    new_keys = jnp.concatenate([newv[0, :, 0:HEAD_DIM], newv[1, :, 0:HEAD_DIM], filler], axis=0)
    new_vals = jnp.concatenate(
        [newv[0, :, HEAD_DIM : 2 * HEAD_DIM], newv[1, :, HEAD_DIM : 2 * HEAD_DIM], filler], axis=0
    )
    new_row = lax.broadcasted_iota(jnp.int32, (n_rows, 128), 0)
    new_col = lax.broadcasted_iota(jnp.int32, (n_rows, 128), 1)
    shown = jnp.logical_and(
        lax.rem(new_col, per_dev) == new_row // (2 * group),
        new_col // per_dev <= lax.rem(new_row // group, 2),
    )
    fresh = lax.dot_general(query, new_keys, nt, preferred_element_type=f32)
    fresh = jnp.where(shown, fresh, NEG_FILL)
    own = []
    cols = lax.broadcasted_iota(jnp.int32, (part, gen), 1)
    for p in range(per_dev):
        raw = lax.dot_general(
            query[p * part : (p + 1) * part], cache[p, :, 0:HEAD_DIM], nt,
            preferred_element_type=jnp.float32,
        )
        own.append(jnp.where(cols < lens[base + p], raw, NEG_FILL))
    own = jnp.concatenate(own, axis=0)
    row_max = jnp.max(jnp.maximum(jnp.maximum(top, fresh), own), axis=1, keepdims=True)
    scale = LOG2E / math.sqrt(HEAD_DIM)
    exps = jnp.exp2((own - row_max) * scale)
    fresh_exps = jnp.exp2((fresh - row_max) * scale)
    total = exps + fresh_exps
    probs = exps.astype(jnp.bfloat16)
    mixed = []
    for p in range(per_dev):
        mixed.append(
            jnp.dot(
                probs[p * part : (p + 1) * part], cache[p, :, HEAD_DIM : 2 * HEAD_DIM],
                preferred_element_type=jnp.float32,
            )
        )
    mixed = jnp.concatenate(mixed, axis=0) + jnp.dot(
        fresh_exps.astype(bf16), new_vals, preferred_element_type=f32
    )
    block = n_rows // 2
    totals, mixes = [], []
    for r in range(2):
        lines = slice(r * block, (r + 1) * block)
        part_total, part_mixed = total[lines], mixed[lines]
        for c in range(prompt_len // chunk):
            exps = jnp.exp2((scores[lines, c * chunk : (c + 1) * chunk] - row_max[lines]) * scale)
            for i in range(chunk // 128):
                part_total = part_total + exps[:, i * 128 : (i + 1) * 128]
            part_mixed = part_mixed + jnp.dot(
                exps.astype(bf16), valv[c * chunk : (c + 1) * chunk, :], preferred_element_type=f32
            )
        totals.append(part_total)
        mixes.append(part_mixed)
    total, mixed = jnp.concatenate(totals, axis=0), jnp.concatenate(mixes, axis=0)
    lanes = lax.broadcasted_iota(jnp.int32, (1, 128), 1)
    bias_start = tp * (bias_part * 128)
    for p in range(per_dev):
        for t in range(2):
            local_token = toks[t, p] - bias_start
            spot = jnp.clip(lax.shift_right_arithmetic(local_token, 7), 0, bias_part - 1)
            row = biasv[pl.ds(spot, 1), :]
            bias_rows[p * 2 + t : p * 2 + t + 1, :] = jnp.where(
                lanes == local_token - spot * 128, row, 0.0
            )

    first_tp = jnp.where(tp == 0, 1.0, 0.0)
    weight_lane = 2 * 2 * per_dev + per_dev * my_y
    prior_row = jnp.zeros((1, 128), f32)
    for p in range(per_dev):
        prior_row = jnp.where(lanes == weight_lane + p, prior[p] * first_tp, prior_row)
    pair_ids = lax.broadcasted_iota(jnp.int32, (2 * per_dev, 128), 0)
    lane_ids = lax.broadcasted_iota(jnp.int32, (2 * per_dev, 128), 1)
    pair_step = lax.rem(pair_ids, 2)
    at_twist = lane_ids == pair_step * per_dev + pair_ids // 2
    at_weight = lane_ids == weight_lane + pair_ids // 2
    placed = jnp.where(
        at_twist, 1.0, jnp.where(at_weight, (2 * pair_step - 1).astype(f32), 0.0)
    )

    row_sum = jnp.sum(total, axis=1, keepdims=True)
    mixed = mixed / row_sum
    weighted = mixed.reshape(2 * per_dev, group, HEAD_DIM) * tvv[...][None]
    pair_rows = jnp.sum(weighted, axis=1) + bias_rows[...]
    pair_col = jnp.sum(pair_rows, axis=1, keepdims=True)
    message = jnp.sum(placed * pair_col, axis=0, keepdims=True) + prior_row
    plane_rows[me] = message

    pl.semaphore_wait(
        barrier, n_plane - 1 + my_z + jnp.where(dom > 0, 1, 0)
    )

    def plane_send_to(j):
        return pltpu.make_async_remote_copy(
            src_ref=plane_rows.at[me],
            dst_ref=plane_rows.at[me],
            send_sem=plane_send,
            recv_sem=plane_recv,
            device_id=plane_target(j),
            device_id_type=MESH,
        )

    plane_sends = [plane_send_to(j) for j in range(len(targets))]
    for item in plane_sends:
        item.start()

    @pl.when(dom > 0)
    def _():
        signal(next_sem, device(dom - 1, tp))

    rows = lax.broadcasted_iota(jnp.int32, (gen, 2 * HEAD_DIM), 0).astype(f32).astype(bf16)
    for p in range(per_dev):
        start = lens[base + p].astype(f32)
        at_first = jnp.full((gen, 2 * HEAD_DIM), start, f32).astype(bf16)
        at_second = jnp.full((gen, 2 * HEAD_DIM), start + 1.0, f32).astype(bf16)
        first = jnp.broadcast_to(newv[0, pl.ds(p, 1), :], (gen, 2 * HEAD_DIM))
        second = jnp.broadcast_to(newv[1, pl.ds(p, 1), :], (gen, 2 * HEAD_DIM))
        later = jnp.where(rows == at_second, second, jnp.zeros_like(second))
        cache[p] = jnp.where(
            rows < at_first, cache[p], jnp.where(rows == at_first, first, later)
        )

    load_anc.wait()
    for slot, offset in enumerate(OFFSETS):
        target = jnp.clip(dom + offset, 0, n_dom - 1) * per_dev
        low, high = per_dev - 1, 0
        for i in range(per_dev):
            spot = anc[target + i] - base
            mine = jnp.logical_and(spot >= 0, spot < per_dev)
            low = jnp.minimum(low, jnp.where(mine, spot, per_dev - 1))
            high = jnp.maximum(high, jnp.where(mine, spot, 0))
        picked[slot, 0] = cache[low]
        picked[slot, 1] = cache[high]

    all_sent = pltpu.make_async_remote_copy(
        src_ref=plane_rows.at[0 : n_plane - 1],
        dst_ref=plane_rows.at[0 : n_plane - 1],
        send_sem=plane_send,
        recv_sem=plane_recv,
        device_id=device(dom, 0),
        device_id_type=MESH,
    )
    all_sent.wait_recv()

    sums = [plane_rows[slot] for slot in range(n_plane)]
    while len(sums) > 1:
        sums = [a + b for a, b in zip(sums[::2], sums[1::2])]
    z_rows[my_z] = sums[0]

    def z_copy(dst, z):
        return pltpu.make_async_remote_copy(
            src_ref=z_rows.at[my_z],
            dst_ref=z_rows.at[dst],
            send_sem=z_send,
            recv_sem=z_recv,
            device_id=z_device(z),
            device_id_type=MESH,
        )

    def z_start(z, carry):
        z_copy(my_z, z).start()
        return carry

    lax.fori_loop(0, my_z, z_start, 0)

    def greet_below(z, carry):
        signal(above_sem, z_device(z))
        return carry

    lax.fori_loop(0, my_z, greet_below, 0)

    def hop(src, dst, i, shift):
        return pltpu.make_async_remote_copy(
            src_ref=src,
            dst_ref=dst,
            send_sem=hop_send.at[i],
            recv_sem=hop_recv.at[i],
            device_id=device(jnp.clip(dom + shift, 0, n_dom - 1), tp),
            device_id_type=MESH,
        )

    far = n_dom - 1
    inner = jnp.logical_and(dom > 0, dom < far)
    hops = [
        (hop(picked.at[0], relay.at[0], 0, 1), dom < far - 1, inner),
        (hop(picked.at[2], relay.at[1], 1, -1), dom > 1, inner),
        (hop(picked.at[1], landed.at[1], 2, 1), dom < far, dom > 0),
        (hop(picked.at[3], landed.at[3], 3, -1), dom > 0, dom < far),
        (hop(relay.at[0], landed.at[0], 4, 1), inner, dom > 1),
        (hop(relay.at[1], landed.at[2], 5, -1), inner, dom < far - 1),
    ]

    def start_hop(i):
        pl.when(hops[i][1])(hops[i][0].start)

    def receive_hop(i):
        pl.when(hops[i][2])(hops[i][0].wait_recv)

    @pl.when(dom < far)
    def _():
        pl.semaphore_wait(next_sem, 1)

    for i in range(4):
        start_hop(i)

    receive_hop(0)
    start_hop(4)
    receive_hop(1)
    start_hop(5)

    @pl.when(my_z < n_z - 1)
    def _():
        pl.semaphore_wait(above_sem, n_z - 1 - my_z)

    lax.fori_loop(my_z + 1, n_z, z_start, 0)

    own_sum = plane_rows[my_y]
    for t in range(1, n_tp):
        own_sum = own_sum + plane_rows[t * Y_DIM + my_y]
    twist_out[0:1, :] = own_sum[:, 0:per_dev]
    twist_out[1:2, :] = pltpu.roll(own_sum, 128 - per_dev, 1)[:, 0:per_dev]
    own_weight = own_sum
    for y in range(Y_DIM):
        moved = pltpu.roll(own_sum, 128 - 4 * per_dev - y * per_dev, 1)
        own_weight = jnp.where(my_y == y, moved, own_weight)

    for i in range(2, 6):
        receive_hop(i)
    firsts = []
    for offset in OFFSETS:
        low = per_dev - 1
        for i in range(per_dev):
            spot = anc[base + i] - (base - offset * per_dev)
            theirs = jnp.logical_and(spot >= 0, spot < per_dev)
            low = jnp.minimum(low, jnp.where(theirs, spot, per_dev - 1))
        firsts.append(low)
    new_lens = jnp.zeros((1, 128), jnp.int32)
    for p in range(per_dev):
        new_lens = jnp.where(lanes == p, lens[anc[base + p]] + 2, new_lens)
        spot = anc[base + p] - base
        home = jnp.logical_and(spot >= 0, spot < per_dev)
        home_spot = jnp.clip(spot, 0, per_dev - 1)
        place = 0
        for slot, offset in enumerate(OFFSETS):
            there = spot + offset * per_dev
            theirs = jnp.logical_and(there >= 0, there < per_dev)
            second = jnp.where(there == firsts[slot], 0, 1)
            place = jnp.where(theirs, 2 * slot + second, place)
        moved = landed[place // 2, lax.rem(place, 2)]
        cache_out[p] = jnp.where(home, cache[home_spot], moved)
    len_out[...] = new_lens[:, 0:per_dev]

    for item, sends, _ in hops:
        pl.when(sends)(item.wait_send)
    all_sent.wait_send()
    z_all = pltpu.make_async_remote_copy(
        src_ref=z_rows.at[0 : n_z - 1],
        dst_ref=z_rows.at[0 : n_z - 1],
        send_sem=z_send,
        recv_sem=z_recv,
        device_id=device(dom, 0),
        device_id_type=MESH,
    )
    z_all.wait_send()
    z_all.wait_recv()
    all_weights = jnp.where((lanes >= 4 * per_dev)[None], z_rows[...], NEG_FILL)
    largest = jnp.max(jnp.max(all_weights, axis=0), axis=1, keepdims=True)
    exp_total = jnp.sum(jnp.sum(jnp.exp(all_weights - largest[None]), axis=0), axis=1, keepdims=True)
    normalized = own_weight - (largest + jnp.log(exp_total))
    norm_out[...] = normalized[:, 0:per_dev]


def finish(*refs):
    count = (len(refs) - 1) // 2
    copies = [
        pltpu.make_async_copy(refs[i], refs[count + i], refs[-1].at[i]) for i in range(count)
    ]
    for item in copies:
        item.start()
    for item in copies:
        item.wait()


def local(
    n_dom,
    n_tp,
    queries,
    new_kv,
    gen_cache,
    prompt_kv,
    lengths,
    ancestors,
    tokens,
    twist_vector,
    twist_bias,
    prior_weights,
):
    per_dev, gen, width = gen_cache.shape
    prompt_len = prompt_kv.shape[0]
    group = queries.shape[2] // HEAD_DIM
    n_rows = 2 * group * per_dev
    n_z = n_dom // Y_DIM
    n_plane = n_tp * Y_DIM
    bias_table = twist_bias.reshape(-1, 128)
    bias_part = -(-bias_table.shape[0] // (8 * n_tp)) * 8
    any_space = pl.BlockSpec(memory_space=pl.ANY)
    vmem = pl.BlockSpec(memory_space=pltpu.VMEM)
    f32, bf16, i32 = jnp.float32, jnp.bfloat16, jnp.int32
    dma = pltpu.SemaphoreType.DMA
    shapes = (((2, per_dev), f32), ((1, per_dev), f32), (gen_cache.shape, bf16), ((1, per_dev), i32))
    results = pl.pallas_call(
        functools.partial(kernel, (n_dom, n_tp, per_dev, gen, prompt_len, group)),
        out_shape=tuple(pltpu.VMEM(*shape) for shape in shapes),
        in_specs=[any_space] * 10,
        out_specs=(vmem,) * 4,
        scratch_shapes=[
            pltpu.SMEM(ancestors.shape, i32),
            pltpu.SMEM(lengths.shape, i32),
            pltpu.SMEM(tokens.shape, i32),
            pltpu.SMEM(prior_weights.shape, f32),
            pltpu.VMEM(queries.shape, bf16),
            pltpu.VMEM(new_kv.shape, bf16),
            pltpu.VMEM(gen_cache.shape, bf16),
            pltpu.VMEM((prompt_len, HEAD_DIM), bf16),
            pltpu.VMEM((prompt_len, HEAD_DIM), bf16),
            pltpu.VMEM((group, HEAD_DIM), f32),
            pltpu.VMEM((bias_part, 128), f32),
            pltpu.VMEM((n_rows, prompt_len), f32),
            pltpu.VMEM((4, 2, gen, width), bf16),
            pltpu.VMEM((2, 2, gen, width), bf16),
            pltpu.VMEM((4, 2, gen, width), bf16),
            pltpu.VMEM((2 * per_dev, 128), f32),
            pltpu.VMEM((n_plane, 1, 128), f32),
            pltpu.VMEM((n_z, 1, 128), f32),
            dma((5,)),
            dma((5,)),
            dma((PARTS,)),
            dma((6,)),
            dma((6,)),
            dma,
            dma,
            dma,
            dma,
            pltpu.SemaphoreType.REGULAR,
            pltpu.SemaphoreType.REGULAR,
        ],
        compiler_params=pltpu.CompilerParams(collective_id=0, has_side_effects=True),
        name="smc_step",
    )(
        ancestors,
        lengths,
        tokens,
        prior_weights,
        queries,
        new_kv,
        gen_cache,
        prompt_kv,
        twist_vector.reshape(group, HEAD_DIM),
        bias_table,
    )
    held = [pltpu.with_memory_space_constraint(x, pltpu.VMEM) for x in results]
    twist, normalized, resampled, new_lengths = pl.pallas_call(
        finish,
        out_shape=tuple(jax.ShapeDtypeStruct(*shape) for shape in shapes),
        in_specs=[any_space] * 4,
        out_specs=(any_space,) * 4,
        scratch_shapes=[dma((4,))],
        compiler_params=pltpu.CompilerParams(vmem_limit_bytes=4 << 20),
        name="finish",
    )(*held)
    return twist, normalized.reshape(per_dev), resampled, new_lengths.reshape(per_dev)


def solution(mesh):
    in_specs = (
        P(None, "dom", "tp"),
        P(None, "dom", "tp"),
        P("dom", None, "tp"),
        P(None, "tp"),
        P(),
        P(),
        P(None, "dom"),
        P("tp"),
        P(),
        P("dom"),
    )
    out_specs = (P(None, "dom"), P("dom"), P("dom", None, "tp"), P("dom"))
    return jax.shard_map(
        functools.partial(local, mesh.shape["dom"], mesh.shape["tp"]),
        mesh=mesh,
        in_specs=in_specs,
        out_specs=out_specs,
        check_vma=False,
    )
```

```python
import functools
import math

import jax
import jax.numpy as jnp
from jax import lax
from jax.experimental import pallas as pl
from jax.experimental.pallas import tpu as pltpu
from jax.sharding import PartitionSpec as P

HEAD_DIM = 128
Y_DIM = 4
NEG_FILL = -1e30
MESH = pl.DeviceIdType.MESH
LOG2E = 1.4426950408889634
PARTS = 2
OFFSETS = (2, 1, -2, -1)


def kernel(
    sizes,
    anc_hbm,
    lens_hbm,
    toks_hbm,
    prior_hbm,
    q_hbm,
    new_hbm,
    gen_hbm,
    prompt_hbm,
    tv_hbm,
    bias_hbm,
    twist_out,
    norm_out,
    cache_out,
    len_out,
    anc,
    lens,
    toks,
    prior,
    qv,
    newv,
    cache,
    keyv,
    valv,
    tvv,
    biasv,
    scores,
    picked,
    relay,
    landed,
    bias_rows,
    plane_rows,
    z_rows,
    small_sems,
    in_sems,
    key_sems,
    hop_send,
    hop_recv,
    plane_send,
    plane_recv,
    z_send,
    z_recv,
    next_sem,
    above_sem,
):
    n_dom, n_tp, per_dev, gen, prompt_len, group = sizes
    f32, bf16 = jnp.float32, jnp.bfloat16
    n_z = n_dom // Y_DIM
    n_plane = n_tp * Y_DIM
    dom = lax.axis_index("dom")
    tp = lax.axis_index("tp")
    my_y = lax.rem(dom, Y_DIM)
    my_z = dom // Y_DIM
    base = dom * per_dev
    bias_len = bias_hbm.shape[0]
    bias_part = biasv.shape[0]
    bias_last = bias_len - (n_tp - 1) * bias_part
    key_part = prompt_len // PARTS

    def device(d, t):
        return {"dom": d, "tp": t}

    def signal(sem, target):
        pl.semaphore_signal(sem, inc=1, device_id=target, device_id_type=MESH)

    def z_device(z):
        return device(z * Y_DIM + my_y, tp)

    me = tp * Y_DIM + my_y

    copy = pltpu.make_async_copy
    load_q = copy(q_hbm, qv, in_sems.at[0])
    load_gen = copy(gen_hbm, cache, in_sems.at[1])
    load_new = copy(new_hbm, newv, in_sems.at[2])
    load_tv = copy(tv_hbm, tvv, in_sems.at[3])
    load_keys = [
        copy(
            prompt_hbm.at[c * key_part : (c + 1) * key_part, 0:HEAD_DIM],
            keyv.at[c * key_part : (c + 1) * key_part],
            key_sems.at[c],
        )
        for c in range(PARTS)
    ]
    load_vals = copy(prompt_hbm.at[:, HEAD_DIM : 2 * HEAD_DIM], valv, in_sems.at[4])
    load_anc = copy(anc_hbm, anc, small_sems.at[0])
    load_lens = copy(lens_hbm, lens, small_sems.at[1])
    load_toks = copy(toks_hbm, toks, small_sems.at[2])
    load_prior = copy(prior_hbm, prior, small_sems.at[3])
    bias_most = copy(
        bias_hbm.at[pl.ds(pl.multiple_of(tp * bias_part, 8), bias_part)], biasv, small_sems.at[4]
    )
    bias_rest = copy(
        bias_hbm.at[bias_len - bias_last : bias_len], biasv.at[0:bias_last], small_sems.at[4]
    )
    load_q.start()
    for item in load_keys:
        item.start()
    load_toks.start()
    load_prior.start()
    load_lens.start()

    @pl.when(tp < n_tp - 1)
    def _():
        bias_most.start()

    @pl.when(tp == n_tp - 1)
    def _():
        bias_rest.start()

    load_new.start()
    load_gen.start()
    load_vals.start()
    load_tv.start()
    load_anc.start()

    barrier = pltpu.get_barrier_semaphore()

    n_x = n_tp // 2
    my_x, core = tp // 2, lax.rem(tp, 2)
    farthest = lambda n: sorted(range(n), key=lambda d: -min(d, n - d))
    targets = []
    for target_core in range(2):
        for dx in farthest(n_x):
            for dy in farthest(Y_DIM):
                if dx or dy:
                    targets.append((dx, dy, target_core))
    targets.append((0, 0, 1 - core))

    def plane_target(j):
        dx, dy, target_core = targets[j]
        x = lax.rem(my_x + dx, n_x)
        y = lax.rem(my_y + dy, Y_DIM)
        return device(my_z * Y_DIM + y, x * 2 + target_core)

    for j in range(len(targets)):
        signal(barrier, plane_target(j))

    def greet_above(z, carry):
        signal(barrier, z_device(z))
        return carry

    lax.fori_loop(my_z + 1, n_z, greet_above, 0)

    @pl.when(dom < n_dom - 1)
    def _():
        signal(barrier, device(dom + 1, tp))

    n_rows = 2 * group * per_dev
    to_row = lax.broadcasted_iota(jnp.int32, (n_rows, n_rows), 0)
    from_row = lax.broadcasted_iota(jnp.int32, (n_rows, n_rows), 1)
    wanted = lax.rem(to_row, 2 * group) * per_dev + to_row // (2 * group)
    order = jnp.where(from_row == wanted, 1.0, 0.0).astype(jnp.bfloat16)
    load_q.wait()
    tiles = [qv[t, :, h * HEAD_DIM : (h + 1) * HEAD_DIM] for t in range(2) for h in range(group)]
    stacked = jnp.concatenate(tiles, axis=0)
    query = jnp.dot(order, stacked, preferred_element_type=jnp.float32).astype(jnp.bfloat16)

    nt = (((1,), (1,)), ((), ()))
    part = 2 * group
    chunk = 512
    top = None
    for c in range(prompt_len // chunk):
        if c * chunk % key_part == 0:
            load_keys[c * chunk // key_part].wait()
        raw = lax.dot_general(
            query, keyv[c * chunk : (c + 1) * chunk, :], nt, preferred_element_type=jnp.float32
        )
        scores[:, c * chunk : (c + 1) * chunk] = raw
        for i in range(chunk // 128):
            piece = raw[:, i * 128 : (i + 1) * 128]
            top = piece if top is None else jnp.maximum(top, piece)

    load_toks.wait()

    @pl.when(tp < n_tp - 1)
    def _():
        bias_most.wait()

    @pl.when(tp == n_tp - 1)
    def _():
        bias_rest.wait()

    load_prior.wait()
    load_lens.wait()
    load_new.wait()
    load_gen.wait()
    load_vals.wait()
    load_tv.wait()
    filler = jnp.zeros((128 - 2 * per_dev, HEAD_DIM), bf16)
    new_keys = jnp.concatenate([newv[0, :, 0:HEAD_DIM], newv[1, :, 0:HEAD_DIM], filler], axis=0)
    new_vals = jnp.concatenate(
        [newv[0, :, HEAD_DIM : 2 * HEAD_DIM], newv[1, :, HEAD_DIM : 2 * HEAD_DIM], filler], axis=0
    )
    new_row = lax.broadcasted_iota(jnp.int32, (n_rows, 128), 0)
    new_col = lax.broadcasted_iota(jnp.int32, (n_rows, 128), 1)
    shown = jnp.logical_and(
        lax.rem(new_col, per_dev) == new_row // (2 * group),
        new_col // per_dev <= lax.rem(new_row // group, 2),
    )
    fresh = lax.dot_general(query, new_keys, nt, preferred_element_type=f32)
    fresh = jnp.where(shown, fresh, NEG_FILL)
    own = []
    cols = lax.broadcasted_iota(jnp.int32, (part, gen), 1)
    for p in range(per_dev):
        raw = lax.dot_general(
            query[p * part : (p + 1) * part], cache[p, :, 0:HEAD_DIM], nt,
            preferred_element_type=jnp.float32,
        )
        own.append(jnp.where(cols < lens[base + p], raw, NEG_FILL))
    own = jnp.concatenate(own, axis=0)
    row_max = jnp.max(jnp.maximum(jnp.maximum(top, fresh), own), axis=1, keepdims=True)
    scale = LOG2E / math.sqrt(HEAD_DIM)
    exps = jnp.exp2((own - row_max) * scale)
    fresh_exps = jnp.exp2((fresh - row_max) * scale)
    total = exps + fresh_exps
    probs = exps.astype(jnp.bfloat16)
    mixed = []
    for p in range(per_dev):
        mixed.append(
            jnp.dot(
                probs[p * part : (p + 1) * part], cache[p, :, HEAD_DIM : 2 * HEAD_DIM],
                preferred_element_type=jnp.float32,
            )
        )
    mixed = jnp.concatenate(mixed, axis=0) + jnp.dot(
        fresh_exps.astype(bf16), new_vals, preferred_element_type=f32
    )
    block = n_rows // 2
    totals, mixes = [], []
    for r in range(2):
        lines = slice(r * block, (r + 1) * block)
        part_total, part_mixed = total[lines], mixed[lines]
        for c in range(prompt_len // chunk):
            exps = jnp.exp2((scores[lines, c * chunk : (c + 1) * chunk] - row_max[lines]) * scale)
            for i in range(chunk // 128):
                part_total = part_total + exps[:, i * 128 : (i + 1) * 128]
            part_mixed = part_mixed + jnp.dot(
                exps.astype(bf16), valv[c * chunk : (c + 1) * chunk, :], preferred_element_type=f32
            )
        totals.append(part_total)
        mixes.append(part_mixed)
    total, mixed = jnp.concatenate(totals, axis=0), jnp.concatenate(mixes, axis=0)
    lanes = lax.broadcasted_iota(jnp.int32, (1, 128), 1)
    bias_start = tp * (bias_part * 128)
    for p in range(per_dev):
        for t in range(2):
            local_token = toks[t, p] - bias_start
            spot = jnp.clip(lax.shift_right_arithmetic(local_token, 7), 0, bias_part - 1)
            row = biasv[pl.ds(spot, 1), :]
            bias_rows[p * 2 + t : p * 2 + t + 1, :] = jnp.where(
                lanes == local_token - spot * 128, row, 0.0
            )

    first_tp = jnp.where(tp == 0, 1.0, 0.0)
    weight_lane = 2 * 2 * per_dev + per_dev * my_y
    prior_row = jnp.zeros((1, 128), f32)
    for p in range(per_dev):
        prior_row = jnp.where(lanes == weight_lane + p, prior[p] * first_tp, prior_row)
    pair_ids = lax.broadcasted_iota(jnp.int32, (2 * per_dev, 128), 0)
    lane_ids = lax.broadcasted_iota(jnp.int32, (2 * per_dev, 128), 1)
    pair_step = lax.rem(pair_ids, 2)
    at_twist = lane_ids == pair_step * per_dev + pair_ids // 2
    at_weight = lane_ids == weight_lane + pair_ids // 2
    placed = jnp.where(
        at_twist, 1.0, jnp.where(at_weight, (2 * pair_step - 1).astype(f32), 0.0)
    )

    row_sum = jnp.sum(total, axis=1, keepdims=True)
    mixed = mixed / row_sum
    weighted = mixed.reshape(2 * per_dev, group, HEAD_DIM) * tvv[...][None]
    pair_rows = jnp.sum(weighted, axis=1) + bias_rows[...]
    pair_col = jnp.sum(pair_rows, axis=1, keepdims=True)
    message = jnp.sum(placed * pair_col, axis=0, keepdims=True) + prior_row
    plane_rows[me] = message

    pl.semaphore_wait(
        barrier, n_plane - 1 + my_z + jnp.where(dom > 0, 1, 0)
    )

    def plane_send_to(j):
        return pltpu.make_async_remote_copy(
            src_ref=plane_rows.at[me],
            dst_ref=plane_rows.at[me],
            send_sem=plane_send,
            recv_sem=plane_recv,
            device_id=plane_target(j),
            device_id_type=MESH,
        )

    plane_sends = [plane_send_to(j) for j in range(len(targets))]
    for item in plane_sends:
        item.start()

    @pl.when(dom > 0)
    def _():
        signal(next_sem, device(dom - 1, tp))

    rows = lax.broadcasted_iota(jnp.int32, (gen, 2 * HEAD_DIM), 0).astype(f32).astype(bf16)
    for p in range(per_dev):
        start = lens[base + p].astype(f32)
        at_first = jnp.full((gen, 2 * HEAD_DIM), start, f32).astype(bf16)
        at_second = jnp.full((gen, 2 * HEAD_DIM), start + 1.0, f32).astype(bf16)
        first = jnp.broadcast_to(newv[0, pl.ds(p, 1), :], (gen, 2 * HEAD_DIM))
        second = jnp.broadcast_to(newv[1, pl.ds(p, 1), :], (gen, 2 * HEAD_DIM))
        later = jnp.where(rows == at_second, second, jnp.zeros_like(second))
        cache[p] = jnp.where(
            rows < at_first, cache[p], jnp.where(rows == at_first, first, later)
        )

    load_anc.wait()
    for slot, offset in enumerate(OFFSETS):
        target = jnp.clip(dom + offset, 0, n_dom - 1) * per_dev
        low, high = per_dev - 1, 0
        for i in range(per_dev):
            spot = anc[target + i] - base
            mine = jnp.logical_and(spot >= 0, spot < per_dev)
            low = jnp.minimum(low, jnp.where(mine, spot, per_dev - 1))
            high = jnp.maximum(high, jnp.where(mine, spot, 0))
        picked[slot, 0] = cache[low]
        picked[slot, 1] = cache[high]

    all_sent = pltpu.make_async_remote_copy(
        src_ref=plane_rows.at[0 : n_plane - 1],
        dst_ref=plane_rows.at[0 : n_plane - 1],
        send_sem=plane_send,
        recv_sem=plane_recv,
        device_id=device(dom, 0),
        device_id_type=MESH,
    )
    all_sent.wait_recv()

    sums = [plane_rows[slot] for slot in range(n_plane)]
    while len(sums) > 1:
        sums = [a + b for a, b in zip(sums[::2], sums[1::2])]
    z_rows[my_z] = sums[0]

    def z_copy(dst, z):
        return pltpu.make_async_remote_copy(
            src_ref=z_rows.at[my_z],
            dst_ref=z_rows.at[dst],
            send_sem=z_send,
            recv_sem=z_recv,
            device_id=z_device(z),
            device_id_type=MESH,
        )

    def z_start(z, carry):
        z_copy(my_z, z).start()
        return carry

    lax.fori_loop(0, my_z, z_start, 0)

    def greet_below(z, carry):
        signal(above_sem, z_device(z))
        return carry

    lax.fori_loop(0, my_z, greet_below, 0)

    def hop(src, dst, i, shift):
        return pltpu.make_async_remote_copy(
            src_ref=src,
            dst_ref=dst,
            send_sem=hop_send.at[i],
            recv_sem=hop_recv.at[i],
            device_id=device(jnp.clip(dom + shift, 0, n_dom - 1), tp),
            device_id_type=MESH,
        )

    far = n_dom - 1
    inner = jnp.logical_and(dom > 0, dom < far)
    hops = [
        (hop(picked.at[0], relay.at[0], 0, 1), dom < far - 1, inner),
        (hop(picked.at[2], relay.at[1], 1, -1), dom > 1, inner),
        (hop(picked.at[1], landed.at[1], 2, 1), dom < far, dom > 0),
        (hop(picked.at[3], landed.at[3], 3, -1), dom > 0, dom < far),
        (hop(relay.at[0], landed.at[0], 4, 1), inner, dom > 1),
        (hop(relay.at[1], landed.at[2], 5, -1), inner, dom < far - 1),
    ]

    def start_hop(i):
        pl.when(hops[i][1])(hops[i][0].start)

    def receive_hop(i):
        pl.when(hops[i][2])(hops[i][0].wait_recv)

    @pl.when(dom < far)
    def _():
        pl.semaphore_wait(next_sem, 1)

    for i in range(4):
        start_hop(i)

    receive_hop(0)
    start_hop(4)
    receive_hop(1)
    start_hop(5)

    @pl.when(my_z < n_z - 1)
    def _():
        pl.semaphore_wait(above_sem, n_z - 1 - my_z)

    lax.fori_loop(my_z + 1, n_z, z_start, 0)

    own_sum = plane_rows[my_y]
    for t in range(1, n_tp):
        own_sum = own_sum + plane_rows[t * Y_DIM + my_y]
    twist_out[0:1, :] = own_sum[:, 0:per_dev]
    twist_out[1:2, :] = pltpu.roll(own_sum, 128 - per_dev, 1)[:, 0:per_dev]
    own_weight = own_sum
    for y in range(Y_DIM):
        moved = pltpu.roll(own_sum, 128 - 4 * per_dev - y * per_dev, 1)
        own_weight = jnp.where(my_y == y, moved, own_weight)

    for i in range(2, 6):
        receive_hop(i)
    firsts = []
    for offset in OFFSETS:
        low = per_dev - 1
        for i in range(per_dev):
            spot = anc[base + i] - (base - offset * per_dev)
            theirs = jnp.logical_and(spot >= 0, spot < per_dev)
            low = jnp.minimum(low, jnp.where(theirs, spot, per_dev - 1))
        firsts.append(low)
    new_lens = jnp.zeros((1, 128), jnp.int32)
    for p in range(per_dev):
        new_lens = jnp.where(lanes == p, lens[anc[base + p]] + 2, new_lens)
        spot = anc[base + p] - base
        home = jnp.logical_and(spot >= 0, spot < per_dev)
        home_spot = jnp.clip(spot, 0, per_dev - 1)
        place = 0
        for slot, offset in enumerate(OFFSETS):
            there = spot + offset * per_dev
            theirs = jnp.logical_and(there >= 0, there < per_dev)
            second = jnp.where(there == firsts[slot], 0, 1)
            place = jnp.where(theirs, 2 * slot + second, place)
        moved = landed[place // 2, lax.rem(place, 2)]
        cache_out[p] = jnp.where(home, cache[home_spot], moved)
    len_out[...] = new_lens[:, 0:per_dev]

    for item, sends, _ in hops:
        pl.when(sends)(item.wait_send)
    all_sent.wait_send()
    z_all = pltpu.make_async_remote_copy(
        src_ref=z_rows.at[0 : n_z - 1],
        dst_ref=z_rows.at[0 : n_z - 1],
        send_sem=z_send,
        recv_sem=z_recv,
        device_id=device(dom, 0),
        device_id_type=MESH,
    )
    z_all.wait_send()
    z_all.wait_recv()
    all_weights = jnp.where((lanes >= 4 * per_dev)[None], z_rows[...], NEG_FILL)
    largest = jnp.max(jnp.max(all_weights, axis=0), axis=1, keepdims=True)
    exp_total = jnp.sum(jnp.sum(jnp.exp(all_weights - largest[None]), axis=0), axis=1, keepdims=True)
    normalized = own_weight - (largest + jnp.log(exp_total))
    norm_out[...] = normalized[:, 0:per_dev]


def finish(*refs):
    count = (len(refs) - 1) // 2
    copies = [
        pltpu.make_async_copy(refs[i], refs[count + i], refs[-1].at[i]) for i in range(count)
    ]
    for item in copies:
        item.start()
    for item in copies:
        item.wait()


def local(
    n_dom,
    n_tp,
    queries,
    new_kv,
    gen_cache,
    prompt_kv,
    lengths,
    ancestors,
    tokens,
    twist_vector,
    twist_bias,
    prior_weights,
):
    per_dev, gen, width = gen_cache.shape
    prompt_len = prompt_kv.shape[0]
    group = queries.shape[2] // HEAD_DIM
    n_rows = 2 * group * per_dev
    n_z = n_dom // Y_DIM
    n_plane = n_tp * Y_DIM
    bias_table = twist_bias.reshape(-1, 128)
    bias_part = -(-bias_table.shape[0] // (8 * n_tp)) * 8
    any_space = pl.BlockSpec(memory_space=pl.ANY)
    vmem = pl.BlockSpec(memory_space=pltpu.VMEM)
    f32, bf16, i32 = jnp.float32, jnp.bfloat16, jnp.int32
    dma = pltpu.SemaphoreType.DMA
    shapes = (((2, per_dev), f32), ((1, per_dev), f32), (gen_cache.shape, bf16), ((1, per_dev), i32))
    results = pl.pallas_call(
        functools.partial(kernel, (n_dom, n_tp, per_dev, gen, prompt_len, group)),
        out_shape=tuple(pltpu.VMEM(*shape) for shape in shapes),
        in_specs=[any_space] * 10,
        out_specs=(vmem,) * 4,
        scratch_shapes=[
            pltpu.SMEM(ancestors.shape, i32),
            pltpu.SMEM(lengths.shape, i32),
            pltpu.SMEM(tokens.shape, i32),
            pltpu.SMEM(prior_weights.shape, f32),
            pltpu.VMEM(queries.shape, bf16),
            pltpu.VMEM(new_kv.shape, bf16),
            pltpu.VMEM(gen_cache.shape, bf16),
            pltpu.VMEM((prompt_len, HEAD_DIM), bf16),
            pltpu.VMEM((prompt_len, HEAD_DIM), bf16),
            pltpu.VMEM((group, HEAD_DIM), f32),
            pltpu.VMEM((bias_part, 128), f32),
            pltpu.VMEM((n_rows, prompt_len), f32),
            pltpu.VMEM((4, 2, gen, width), bf16),
            pltpu.VMEM((2, 2, gen, width), bf16),
            pltpu.VMEM((4, 2, gen, width), bf16),
            pltpu.VMEM((2 * per_dev, 128), f32),
            pltpu.VMEM((n_plane, 1, 128), f32),
            pltpu.VMEM((n_z, 1, 128), f32),
            dma((5,)),
            dma((5,)),
            dma((PARTS,)),
            dma((6,)),
            dma((6,)),
            dma,
            dma,
            dma,
            dma,
            pltpu.SemaphoreType.REGULAR,
            pltpu.SemaphoreType.REGULAR,
        ],
        compiler_params=pltpu.CompilerParams(collective_id=0, has_side_effects=True),
        name="smc_step",
    )(
        ancestors,
        lengths,
        tokens,
        prior_weights,
        queries,
        new_kv,
        gen_cache,
        prompt_kv,
        twist_vector.reshape(group, HEAD_DIM),
        bias_table,
    )
    held = [pltpu.with_memory_space_constraint(x, pltpu.VMEM) for x in results]
    twist, normalized, resampled, new_lengths = pl.pallas_call(
        finish,
        out_shape=tuple(jax.ShapeDtypeStruct(*shape) for shape in shapes),
        in_specs=[any_space] * 4,
        out_specs=(any_space,) * 4,
        scratch_shapes=[dma((4,))],
        compiler_params=pltpu.CompilerParams(vmem_limit_bytes=4 << 20),
        name="finish",
    )(*held)
    return twist, normalized.reshape(per_dev), resampled, new_lengths.reshape(per_dev)


def solution(mesh):
    in_specs = (
        P(None, "dom", "tp"),
        P(None, "dom", "tp"),
        P("dom", None, "tp"),
        P(None, "tp"),
        P(),
        P(),
        P(None, "dom"),
        P("tp"),
        P(),
        P("dom"),
    )
    out_specs = (P(None, "dom"), P("dom"), P("dom", None, "tp"), P("dom"))
    return jax.shard_map(
        functools.partial(local, mesh.shape["dom"], mesh.shape["tp"]),
        mesh=mesh,
        in_specs=in_specs,
        out_specs=out_specs,
        check_vma=False,
    )
```
